32 devices in a mesh: fsdp: 8 (over y, x, core), seq: 4 (over z).
Axes of the slice: x: 2, y: 2, z: 4, core: 2. Of those that a mesh axis runs over, the one named last changes fastest.
Arguments:
- tokens: bfloat16 [24, 584, 1024], P('fsdp', 'seq'), may hold values from -6 to 6
- counts: int32 [24], P('fsdp'), may hold values from 0 to 577, as said below
- norm1_gain: bfloat16 [1024], P('fsdp'), may hold values from 0.099609375 to 1.8984375
- norm1_shift: bfloat16 [1024], P('fsdp'), may hold values from -3 to 3
- qkv_weight: bfloat16 [1024, 3072], P('fsdp'), may hold values from -0.1875 to 0.1875
- query_bias: bfloat16 [1024], P('fsdp'), may hold values from -3 to 3
- value_bias: bfloat16 [1024], P('fsdp'), may hold values from -3 to 3
- out_weight: bfloat16 [1024, 1024], P('fsdp'), may hold values from -0.875 to 0.875
- out_bias: bfloat16 [1024], P('fsdp'), may hold values from -3 to 3
- norm2_gain: bfloat16 [1024], P('fsdp'), may hold values from 0.099609375 to 1.8984375
- norm2_shift: bfloat16 [1024], P('fsdp'), may hold values from -3 to 3
- fc1_weight: bfloat16 [1024, 4096], P('fsdp'), may hold values from -0.1875 to 0.1875
- fc1_bias: bfloat16 [4096], P('fsdp'), may hold values from -3 to 3
- fc2_weight: bfloat16 [4096, 1024], P('fsdp'), may hold values from -0.09375 to 0.09375
- fc2_bias: bfloat16 [1024], P('fsdp'), may hold values from -3 to 3
- cotangent: bfloat16 [24, 584, 1024], P('fsdp', 'seq'), may hold values from -6 to 6
Outputs:
- output: bfloat16 [24, 584, 1024], P('fsdp', 'seq')
- input_grad: float32 [24, 584, 1024], P('fsdp', 'seq')
- norm1_gain_grad: float32 [1024], P('fsdp')
- norm1_shift_grad: float32 [1024], P('fsdp')
- qkv_weight_grad: float32 [1024, 3072], P('fsdp')
- query_bias_grad: float32 [1024], P('fsdp')
- value_bias_grad: float32 [1024], P('fsdp')
- out_weight_grad: float32 [1024, 1024], P('fsdp')
- out_bias_grad: float32 [1024], P('fsdp')
- norm2_gain_grad: float32 [1024], P('fsdp')
- norm2_shift_grad: float32 [1024], P('fsdp')
- fc1_weight_grad: float32 [1024, 4096], P('fsdp')
- fc1_bias_grad: float32 [4096], P('fsdp')
- fc2_weight_grad: float32 [4096, 1024], P('fsdp')
- fc2_bias_grad: float32 [1024], P('fsdp')
The draws below stay inside these ranges and needn't reach their ends.
Inputs may be any that keep to these rules, and one draw needn't show every extreme that they name: `counts`: each image's count is 577 or 0; image 0 has 577 and the last image has 0.
All inputs are finite; a program needn't handle non-finite values.
Results may differ from the reference program's by a relative error of at most 0.012.
Values may be sent and summed in bfloat16 or wider, within the bound.
No kernel may reach another device: no remote copies, remote signals or barrier semaphores. Data moves between devices by JAX's collectives and lax.ppermute only.
A program may use at most 192 MiB of HBM per device.

```python
import jax
import jax.numpy as jnp
from jax import lax

D = 1024
HEADS = 16
HEAD_DIM = 64
FF = 4096
SEQ_LEN = 584
VALID = 577
IMG_DEV = 3
IMAGES = 24


def draw_counts(key, part):
    chosen = jax.random.randint(key, (IMAGES,), 0, 8)
    kept_flag = (chosen < 7).astype(jnp.int32)
    position = jnp.arange(IMAGES, dtype=jnp.int32)
    kept_flag = jnp.where(position == 0, 1, jnp.where(position == IMAGES - 1, 0, kept_flag))
    return (kept_flag * VALID).astype(jnp.int32)


def spiked(result, stream_key, source, target, parts, factor):
    def block_of(dim):
        return (jnp.arange(result.shape[dim]) // (result.shape[dim] // parts)).reshape((-1,) + (1,) * (result.ndim - 1 - dim))

    one_side = jax.random.permutation(stream_key, parts)[block_of(target)]
    other_side = (block_of(target) + parts // 2) % parts
    return jnp.where((block_of(source) == one_side) | (block_of(source) == other_side), factor * result, result)


def levels(stream_key, extent, pieces, least, high):
    factor_of, own = 1.0, jax.random.fold_in(stream_key, 6)
    for dim, parts in pieces:
        steps = jnp.exp(jax.random.uniform(jax.random.fold_in(own, dim), (parts,), jnp.float32, least / len(pieces), high / len(pieces)))
        factor_of = factor_of * jnp.repeat(steps, extent[dim] // parts).reshape([-1 if axis == dim else 1 for axis in range(len(extent))])
    return factor_of


def centred(own_key, dims, scale, reach, split=(), kind=jnp.bfloat16):
    result = scale * jax.random.normal(own_key, dims, jnp.float32)
    if split:
        result = result * levels(own_key, dims, split, -0.22, 0.18)
    return jnp.clip(result, -reach, reach).astype(kind)


def bell_draw_with(own_key, extent, spread, limit, split, heavy, kind=jnp.bfloat16):
    result = spread * jax.random.normal(own_key, extent, jnp.float32)
    if split:
        result = result * levels(own_key, extent, split, -0.22, 0.18)
    return jnp.clip(spiked(result, jax.random.fold_in(own_key, 3), *heavy), -limit, limit).astype(kind)


def setup_inputs(seed: int = 0) -> dict:
    splits = jax.random.split(jax.random.key(seed), 17)
    tokens = centred(splits[0], (IMAGES, SEQ_LEN, D), 1.0, 6.0, ((0, 8), (1, 4)))
    counts = draw_counts(jax.random.fold_in(splits[16], 71), 0)
    norm1_gain = jnp.clip(1.0 + 0.18 * jax.random.normal(splits[2], (D,), jnp.float32), 0.099609375, 1.8984375).astype(jnp.bfloat16)
    norm1_shift = centred(splits[3], (D,), 0.5, 3.0, ((0, 8),))
    qkv_weight = centred(splits[4], (D, 3 * D), D ** -0.5, 0.1875, ((0, 8),))
    query_bias = centred(splits[5], (D,), 0.5, 3.0, ((0, 8),))
    value_bias = centred(splits[6], (D,), 0.5, 3.0, ((0, 8),))
    out_weight = centred(splits[7], (D, D), 48 ** -0.5, 0.875, ((0, 8),))
    out_bias = centred(splits[8], (D,), 0.5, 3.0, ((0, 8),))
    norm2_gain = jnp.clip(1.0 + 0.18 * jax.random.normal(splits[9], (D,), jnp.float32), 0.099609375, 1.8984375).astype(jnp.bfloat16)
    norm2_shift = centred(splits[10], (D,), 0.5, 3.0, ((0, 8),))
    fc1_weight = centred(splits[11], (D, FF), D ** -0.5, 0.1875, ((0, 8),))
    fc1_bias = centred(splits[12], (FF,), 0.5, 3.0, ((0, 8),))
    fc2_weight = centred(splits[13], (FF, D), FF ** -0.5, 0.09375, ((0, 8),))
    fc2_bias = centred(splits[14], (D,), 0.5, 3.0, ((0, 8),))
    cotangent = bell_draw_with(splits[15], (IMAGES, SEQ_LEN, D), 1.0, 6.0, ((0, 8), (1, 4)), (0, 2, 8, 2.0))
    return dict(tokens=tokens, counts=counts, norm1_gain=norm1_gain, norm1_shift=norm1_shift, qkv_weight=qkv_weight, query_bias=query_bias, value_bias=value_bias, out_weight=out_weight, out_bias=out_bias, norm2_gain=norm2_gain, norm2_shift=norm2_shift, fc1_weight=fc1_weight, fc1_bias=fc1_bias, fc2_weight=fc2_weight, fc2_bias=fc2_bias, cotangent=cotangent)


EPS = 1e-05
MASKED = -1e+30

@jax.custom_vjp
def low(v):
    return lax.optimization_barrier(v.astype(jnp.bfloat16)).astype(jnp.float32)

@jax.custom_vjp
def low_back(v):
    return v

def low_keep(v):
    return (low(v), None)

def low_pass(kept, grad):
    return (grad,)

def back_keep(v):
    return (v, None)

def back_low(kept, grad):
    return (low(grad),)
low.defvjp(low_keep, low_pass)
low_back.defvjp(back_keep, back_low)

def norm_apply(values, gain_vec, shift_vec):
    average = lax.optimization_barrier(jnp.mean(values, axis=-1, keepdims=True))
    centered = values - average
    inverse = lax.rsqrt(lax.optimization_barrier(jnp.mean(centered * centered, axis=-1, keepdims=True)) + EPS)
    return centered * inverse * gain_vec + shift_vec

def quick_gelu(values):
    return values * jax.nn.sigmoid(1.702 * values)

def dot_exact(left, right):
    return jnp.dot(left, right, precision=lax.Precision.HIGHEST, preferred_element_type=jnp.float32)

def group_forward(params, group_tokens, group_counts):
    norm1_gain, norm1_shift, qkv_weight, query_bias, value_bias, out_weight, out_bias, norm2_gain, norm2_shift, fc1_weight, fc1_bias, fc2_weight, fc2_bias = params
    images = group_tokens.shape[0]
    rows_in = group_tokens.reshape(images * SEQ_LEN, D)
    normed_one = low(norm_apply(rows_in, norm1_gain, norm1_shift))
    projected = dot_exact(normed_one, qkv_weight)
    queries = low_back(low(projected[:, :D] + query_bias)).reshape(images, SEQ_LEN, HEADS, HEAD_DIM)
    key_rows = low_back(low(projected[:, D:2 * D])).reshape(images, SEQ_LEN, HEADS, HEAD_DIM)
    value_rows = low_back(low(projected[:, 2 * D:] + value_bias)).reshape(images, SEQ_LEN, HEADS, HEAD_DIM)
    scores = jnp.einsum('gshd,gthd->ghst', queries, key_rows, precision=lax.Precision.HIGHEST) * HEAD_DIM ** (-0.5)
    allowed = lax.broadcasted_iota(jnp.int32, (1, 1, 1, SEQ_LEN), 3) < group_counts[:, None, None, None]
    scores = low_back(jnp.where(allowed, scores, MASKED))
    highest = lax.optimization_barrier(jnp.max(scores, axis=-1, keepdims=True))
    exponent = jnp.exp(scores - highest)
    attention = exponent / lax.optimization_barrier(jnp.sum(exponent, axis=-1, keepdims=True))
    context = jnp.einsum('ghst,gthd->gshd', low(attention), value_rows, precision=lax.Precision.HIGHEST)
    context = low_back(low(context)).reshape(images * SEQ_LEN, D)
    branch = low_back(dot_exact(context, out_weight) + out_bias)
    flags = (group_counts > 0).astype(jnp.float32)
    flag_rows = jnp.broadcast_to(flags[:, None], (images, SEQ_LEN)).reshape(images * SEQ_LEN, 1)
    mixed = rows_in + branch * flag_rows
    normed_two = low(norm_apply(mixed, norm2_gain, norm2_shift))
    hidden = low_back(dot_exact(normed_two, fc1_weight) + fc1_bias)
    active = low(quick_gelu(hidden))
    output_rows = mixed + dot_exact(active, fc2_weight) + fc2_bias
    return output_rows.reshape(images, SEQ_LEN, D)

def reference(tokens, counts, norm1_gain, norm1_shift, qkv_weight, query_bias, value_bias, out_weight, out_bias, norm2_gain, norm2_shift, fc1_weight, fc1_bias, fc2_weight, fc2_bias, cotangent):
    params = (norm1_gain.astype(jnp.float32), norm1_shift.astype(jnp.float32), qkv_weight.astype(jnp.float32), query_bias.astype(jnp.float32), value_bias.astype(jnp.float32), out_weight.astype(jnp.float32), out_bias.astype(jnp.float32), norm2_gain.astype(jnp.float32), norm2_shift.astype(jnp.float32), fc1_weight.astype(jnp.float32), fc1_bias.astype(jnp.float32), fc2_weight.astype(jnp.float32), fc2_bias.astype(jnp.float32))
    groups = IMAGES // IMG_DEV
    group_counts = counts.astype(jnp.int32).reshape(groups, IMG_DEV)
    stepper = jax.checkpoint(group_forward)

    def whole(params_in, inputs):

        def apply_group(members):
            return stepper(params_in, members[0], members[1])
        results = lax.map(apply_group, (inputs.reshape(groups, IMG_DEV, SEQ_LEN, D), group_counts))
        return results.reshape(IMAGES, SEQ_LEN, D)
    output, back_fn = jax.vjp(whole, params, tokens.astype(jnp.float32))
    param_grads, input_grad = back_fn(cotangent.astype(jnp.float32))
    return (output.astype(jnp.bfloat16), input_grad, param_grads[0], param_grads[1], param_grads[2], param_grads[3], param_grads[4], param_grads[5], param_grads[6], param_grads[7], param_grads[8], param_grads[9], param_grads[10], param_grads[11], param_grads[12])
```

```python
import functools

import jax
import jax.numpy as jnp
from jax import lax
from jax.experimental import pallas as pl
from jax.experimental.pallas import tpu as pltpu
from jax.sharding import PartitionSpec as P

HEAD_DIM = 64
EPS = 1e-05
MASKED = -1e30
SCALE = HEAD_DIM ** (-0.5)
F32 = jnp.float32
BF16 = jnp.bfloat16
PIECES = 8
LIMIT = 62 * 1024 * 1024


def call(body, grid, in_specs, out_specs, out_shape, scratch, flops, moved, name):
    return pl.pallas_call(
        body,
        grid_spec=pltpu.PrefetchScalarGridSpec(
            num_scalar_prefetch=1,
            grid=grid,
            in_specs=in_specs,
            out_specs=out_specs,
            scratch_shapes=scratch,
        ),
        out_shape=out_shape,
        compiler_params=pltpu.CompilerParams(
            dimension_semantics=("arbitrary",) * len(grid), vmem_limit_bytes=LIMIT
        ),
        cost_estimate=pl.CostEstimate(flops=flops, bytes_accessed=moved, transcendentals=0),
        name=name,
    )


def whole(shape):
    return pl.BlockSpec(shape, lambda *_: (0,) * len(shape))


def dot_nn(left, right):
    return lax.dot_general(left, right, (((1,), (0,)), ((), ())), preferred_element_type=F32)


def dot_nt(left, right):
    return lax.dot_general(left, right, (((1,), (1,)), ((), ())), preferred_element_type=F32)


def dot_tn(left, right):
    return lax.dot_general(left, right, (((0,), (0,)), ((), ())), preferred_element_type=F32)


def lanes(ref, block, width):
    return ref[:, pl.ds(pl.multiple_of(block * width, 128), width)]


def put_lanes(ref, block, width, value):
    ref[:, pl.ds(pl.multiple_of(block * width, 128), width)] = value


def stats(values):
    average = jnp.mean(values, axis=-1, keepdims=True)
    centered = values - average
    inverse = lax.rsqrt(jnp.mean(centered * centered, axis=-1, keepdims=True) + EPS)
    return centered * inverse, inverse


def stacked(refs, rows=None):
    return jnp.concatenate([r[...] if rows is None else r[:rows, :] for r in refs], axis=0)


def project_body(scal, *refs, paired, rows, unit, n_seq, slot):
    xs = refs[:2] if paired else refs[:1]
    gain, shift, bias = refs[len(xs) : len(xs) + 3]
    weights = refs[len(xs) + 3 : len(xs) + 11]
    out, normed, rel = refs[len(xs) + 11 :]

    @pl.when(pl.program_id(0) == 0)
    def _():
        below = scal[1] + slot < n_seq
        for start in range(0, rows, unit):
            span = pl.ds(start, unit)
            values = xs[0][span, :].astype(F32)
            if paired:
                values = jnp.where(below, values, xs[1][span, :].astype(F32))
            normal, _ = stats(values)
            normed[span, :] = (normal * gain[...] + shift[...]).astype(BF16)
        for r in range(PIECES):
            width = rel.shape[1] // PIECES
            rel[:, r * width : (r + 1) * width] = lanes(normed, scal[0] ^ r, width)

    value = dot_nn(rel[...], stacked(weights, rel.shape[1] // PIECES))
    out[...] = (value + bias[0]).astype(BF16)


def project(scal, xs, gain, shift, bias, pieces, n_seq, slot, unit):
    rows, features = xs[0].shape
    group = features // n_seq
    depth = pieces[0].shape[0]
    return call(
        functools.partial(
            project_body, paired=len(xs) == 2, rows=rows, unit=unit, n_seq=n_seq, slot=slot
        ),
        (3,),
        [whole((rows, features))] * len(xs)
        + [whole((1, features))] * 2
        + [pl.BlockSpec((1, 1, group), lambda j, s: (j, 0, 0))]
        + [pl.BlockSpec((depth, group), lambda j, s: (0, n_seq * j + s[1]))] * PIECES,
        [pl.BlockSpec((rows, group), lambda j, s: (0, j)), whole((rows, features))],
        [
            jax.ShapeDtypeStruct((rows, 3 * group), BF16),
            jax.ShapeDtypeStruct((rows, features), BF16),
        ],
        [pltpu.VMEM((rows, features), BF16)],
        2 * rows * features * 3 * group,
        4 * rows * features + 6 * features * group,
        f"project{slot}",
    )(scal, *xs, gain, shift, bias, *pieces)


def half_masks(unit):
    lane = lax.broadcasted_iota(jnp.int32, (unit, 2 * HEAD_DIM), 1)
    return lane < HEAD_DIM


def split_heads(value, low):
    zero = jnp.zeros_like(value)
    return jnp.concatenate([jnp.where(low, value, zero), jnp.where(low, zero, value)], axis=0)


def join_heads(value, low, unit):
    return jnp.where(low, value[:unit], value[unit:])


def attend_body(scal, *refs, n_seq, unit):
    queries, keys, values = refs[:n_seq], refs[n_seq : 2 * n_seq], refs[2 * n_seq : 3 * n_seq]
    mask, outs, lse = refs[3 * n_seq], refs[3 * n_seq + 1 : 4 * n_seq + 1], refs[-1]
    low = half_masks(unit)
    key = stacked(keys)
    value = stacked(values)
    for s in range(n_seq):
        scores = dot_nt(split_heads(queries[s][...], low), key) * SCALE + mask[0]
        top = jnp.max(scores, axis=-1, keepdims=True)
        weight = jnp.exp(scores - top)
        total = jnp.sum(weight, axis=-1, keepdims=True)
        probs = (weight * (1.0 / total)).astype(BF16)
        outs[s][...] = join_heads(dot_nn(probs, value), low, unit).astype(BF16)
        log_total = top + jnp.log(total)
        lse[0, 0, s * unit : (s + 1) * unit, :] = jnp.where(
            low, log_total[:unit], log_total[unit:]
        )


def qkv_specs(n_seq, unit, pairs):
    specs = []
    for j in range(3):
        specs += [
            pl.BlockSpec((unit, 2 * HEAD_DIM), lambda b, p, s, j=j: (b, pairs * j + p))
        ] * n_seq
    return specs


def attend(scal, projected, mask, unit, images):
    n_seq = len(projected)
    rows, wide = projected[0].shape
    group = wide // 3
    pairs = group // (2 * HEAD_DIM)
    tokens = n_seq * unit
    return call(
        functools.partial(attend_body, n_seq=n_seq, unit=unit),
        (images, pairs),
        qkv_specs(n_seq, unit, pairs) + [pl.BlockSpec((1, 1, tokens), lambda b, p, s: (b, 0, 0))],
        [pl.BlockSpec((unit, 2 * HEAD_DIM), lambda b, p, s: (b, p))] * n_seq
        + [pl.BlockSpec((1, 1, tokens, 2 * HEAD_DIM), lambda b, p, s: (b, p, 0, 0))],
        [jax.ShapeDtypeStruct((rows, group), BF16)] * n_seq
        + [jax.ShapeDtypeStruct((images, pairs, tokens, 2 * HEAD_DIM), F32)],
        [],
        images * pairs * 2 * tokens * tokens * 2 * HEAD_DIM * 4,
        n_seq * rows * wide * 4,
        "attend",
    )(scal, *projected, *projected, *projected, mask)


def attend_back_body(scal, *refs, n_seq, unit, pairs):
    queries, keys, values = refs[:n_seq], refs[n_seq : 2 * n_seq], refs[2 * n_seq : 3 * n_seq]
    grads = refs[3 * n_seq : 4 * n_seq]
    mask, lse = refs[4 * n_seq : 4 * n_seq + 2]
    outs = refs[4 * n_seq + 2 : 5 * n_seq + 2]
    key_acc, value_acc = refs[-2:]
    pair = pl.program_id(1)
    low = half_masks(unit)
    key = stacked(keys)
    value = stacked(values)
    for s in range(n_seq):
        query = split_heads(queries[s][...], low)
        grad = split_heads(grads[s][...], low)
        scores = dot_nt(query, key) * SCALE + mask[0]
        saved = lse[0, 0, s * unit : (s + 1) * unit, :]
        column = jnp.concatenate([saved[:, :1], saved[:, HEAD_DIM : HEAD_DIM + 1]], axis=0)
        probs = jnp.exp(scores - column)
        grad_probs = dot_nt(grad, value)
        value_part = dot_tn(probs.astype(BF16), grad)
        center = jnp.sum(grad_probs * probs, axis=-1, keepdims=True)
        grad_scores = (probs * (grad_probs - center)).astype(BF16)
        query_grad = join_heads(dot_nn(grad_scores, key), low, unit) * SCALE
        key_part = dot_tn(grad_scores, query)
        put_lanes(outs[s], pair, 2 * HEAD_DIM, query_grad.astype(BF16))
        if s == 0:
            key_acc[...] = key_part
            value_acc[...] = value_part
        else:
            key_acc[...] += key_part
            value_acc[...] += value_part
    for s in range(n_seq):
        span = pl.ds(s * unit, unit)
        put_lanes(outs[s], pairs + pair, 2 * HEAD_DIM, (key_acc[span, :] * SCALE).astype(BF16))
        put_lanes(outs[s], 2 * pairs + pair, 2 * HEAD_DIM, value_acc[span, :].astype(BF16))


def attend_back(scal, projected, grads, mask, lse, unit, images):
    n_seq = len(projected)
    rows, wide = projected[0].shape
    group = wide // 3
    pairs = group // (2 * HEAD_DIM)
    tokens = n_seq * unit
    return call(
        functools.partial(attend_back_body, n_seq=n_seq, unit=unit, pairs=pairs),
        (images, pairs),
        qkv_specs(n_seq, unit, pairs)
        + [pl.BlockSpec((unit, 2 * HEAD_DIM), lambda b, p, s: (b, p))] * n_seq
        + [
            pl.BlockSpec((1, 1, tokens), lambda b, p, s: (b, 0, 0)),
            pl.BlockSpec((1, 1, tokens, 2 * HEAD_DIM), lambda b, p, s: (b, p, 0, 0)),
        ],
        [pl.BlockSpec((unit, wide), lambda b, p, s: (b, 0))] * n_seq,
        [jax.ShapeDtypeStruct((rows, wide), BF16)] * n_seq,
        [pltpu.VMEM((tokens, 2 * HEAD_DIM), F32)] * 2,
        images * pairs * 2 * tokens * tokens * 2 * HEAD_DIM * 10,
        n_seq * rows * wide * 4,
        "attend_back",
    )(scal, *projected, *projected, *projected, *grads, mask, lse)


def mix_body(scal, *refs, n_seq):
    contexts = refs[:n_seq]
    x, bias, gain, shift = refs[n_seq : n_seq + 4]
    weights = refs[n_seq + 4 : n_seq + 12]
    context, mixed, normed, rel = refs[n_seq + 12 :]
    group = contexts[0].shape[1]
    for t in range(n_seq):
        put_lanes(context, lax.rem(scal[1] + n_seq - t, n_seq), group, contexts[t][...])
    width = rel.shape[1] // PIECES
    for r in range(PIECES):
        rel[:, r * width : (r + 1) * width] = lanes(context, scal[0] ^ r, width)
    branch = dot_nn(rel[...], stacked(weights)) + bias[...]
    flag = (scal[2 + pl.program_id(0)] > 0).astype(F32)
    value = x[...].astype(F32) + branch * flag
    mixed[...] = value
    normal, _ = stats(value)
    normed[...] = (normal * gain[...] + shift[...]).astype(BF16)


def mix(scal, contexts, x, bias, gain, shift, pieces, unit):
    n_seq = len(contexts)
    rows, features = x.shape
    group = features // n_seq
    row_block = pl.BlockSpec((unit, features), lambda b, s: (b, 0))
    return call(
        functools.partial(mix_body, n_seq=n_seq),
        (rows // unit,),
        [pl.BlockSpec((unit, group), lambda b, s: (b, 0))] * n_seq
        + [row_block]
        + [whole((1, features))] * 3
        + [whole(pieces[0].shape)] * PIECES,
        [row_block] * 3,
        [
            jax.ShapeDtypeStruct((rows, features), BF16),
            jax.ShapeDtypeStruct((rows, features), F32),
            jax.ShapeDtypeStruct((rows, features), BF16),
        ],
        [pltpu.VMEM((unit, features), BF16)],
        2 * rows * features * features,
        12 * rows * features + 2 * features * features,
        "mix",
    )(scal, *contexts, x, bias, gain, shift, *pieces)


def widen_body(scal, *refs):
    x, bias = refs[:2]
    weights = refs[2:10]
    active, slope, rel = refs[10:]

    @pl.when(pl.program_id(0) == 0)
    def _():
        width = rel.shape[1] // PIECES
        for r in range(PIECES):
            rel[:, r * width : (r + 1) * width] = lanes(x, scal[0] ^ r, width)

    hidden = dot_nn(rel[...], stacked(weights)) + bias[...]
    gate = jax.nn.sigmoid(1.702 * hidden)
    product = hidden * gate
    active[...] = product.astype(BF16)
    slope[...] = (gate + 1.702 * product * (1.0 - gate)).astype(BF16)


def widen(scal, x, bias, pieces, tile=512):
    rows, features = x.shape
    depth, hidden = pieces[0].shape
    column = pl.BlockSpec((rows, tile), lambda n, s: (0, n))
    return call(
        widen_body,
        (hidden // tile,),
        [whole((rows, features)), pl.BlockSpec((1, tile), lambda n, s: (0, n))]
        + [pl.BlockSpec((depth, tile), lambda n, s: (0, n))] * PIECES,
        [column] * 2,
        [jax.ShapeDtypeStruct((rows, hidden), BF16)] * 2,
        [pltpu.VMEM((rows, features), BF16)],
        2 * rows * features * hidden,
        2 * features * hidden + 4 * rows * hidden,
        "widen",
    )(scal, x, bias, *pieces)


def narrow_body(scal, *refs, unit, keep):
    x, mixed, bias = refs[:3]
    weights = refs[3:11]
    out = refs[11]
    width = weights[0].shape[0]
    total = mixed[...] + bias[...]
    for r in range(PIECES):
        total += dot_nn(lanes(x, scal[0] ^ r, width), weights[r][...])
    for b in range(out.shape[0]):
        out[b] = total[b * unit : b * unit + keep].astype(BF16)


def narrow(scal, x, mixed, bias, pieces, unit, keep, tile=256):
    rows, hidden = x.shape
    depth, features = pieces[0].shape
    images = rows // unit
    return call(
        functools.partial(narrow_body, unit=unit, keep=keep),
        (features // tile,),
        [
            whole((rows, hidden)),
            pl.BlockSpec((rows, tile), lambda n, s: (0, n)),
            pl.BlockSpec((1, tile), lambda n, s: (0, n)),
        ]
        + [pl.BlockSpec((depth, tile), lambda n, s: (0, n))] * PIECES,
        pl.BlockSpec((images, keep, tile), lambda n, s: (0, 0, n)),
        jax.ShapeDtypeStruct((images, keep, features), BF16),
        [],
        2 * rows * features * hidden,
        2 * features * hidden + 2 * rows * hidden + 6 * rows * features,
        "narrow",
    )(scal, x, mixed, bias, *pieces)


def outer_rows_body(scal, left, right, *refs):
    value = dot_tn(left[...], right[...])
    if len(refs) == 2:
        value += refs[0][0].astype(F32)
    refs[-1][0] = value.astype(BF16)


def outer_rows(scal, left, right, offset, added=None):
    rows, hidden = left.shape
    width = hidden // PIECES
    features = right.shape[1]
    block = pl.BlockSpec((1, width, features), lambda m, s: (m, 0, 0))
    half = PIECES // 2
    return call(
        outer_rows_body,
        (half,),
        [
            pl.BlockSpec((rows, width), lambda m, s: (0, s[0] ^ (2 * m + offset))),
            whole((rows, features)),
        ]
        + ([block] if offset == 0 else []),
        block,
        jax.ShapeDtypeStruct((half, width, features), BF16),
        [],
        rows * hidden * features,
        hidden * features * (1 if offset else 2),
        f"outer_rows{offset}",
    )(scal, left, right, *(() if added is None else (added,)))


def outer_body(scal, *refs, count, offset, width):
    lefts, rights = refs[:count], refs[count : 2 * count]
    out, rel = refs[-2:]
    half = PIECES // 2

    @pl.when(pl.program_id(0) == 0)
    def _():
        rows = lefts[0].shape[0]
        for i in range(count):
            for m in range(half):
                rel[i * rows : (i + 1) * rows, m * width : (m + 1) * width] = lanes(
                    lefts[i], scal[0] ^ (2 * m + offset), width
                )

    right = stacked(rights)
    value = dot_tn(rel[...], right)
    for m in range(half):
        part = value[m * width : (m + 1) * width]
        if offset == 0:
            part = part + refs[2 * count][m].astype(F32)
        out[m] = part.astype(BF16)


def outer(scal, lefts, rights, offset, tile, added=None, name=""):
    count = len(lefts)
    rows, features = lefts[0].shape
    wide = rights[0].shape[1]
    width = features // PIECES
    half = PIECES // 2
    block = pl.BlockSpec((half, width, tile), lambda n, s: (0, 0, n))
    return call(
        functools.partial(outer_body, count=count, offset=offset, width=width),
        (wide // tile,),
        [whole((rows, features))] * count
        + [pl.BlockSpec((rows, tile), lambda n, s: (0, n))] * count
        + ([block] if offset == 0 else []),
        block,
        jax.ShapeDtypeStruct((half, width, wide), BF16),
        [pltpu.VMEM((count * rows, half * width), BF16)],
        count * rows * features * wide,
        features * wide * (1 if offset else 2) + count * 2 * rows * (features + wide),
        f"outer_{name}{offset}",
    )(scal, *lefts, *rights, *(() if added is None else (added,)))


def narrow_back_body(scal, *refs):
    grad, slope = refs[:2]
    weights = refs[2:10]
    out = refs[10]
    step = pl.program_id(0)
    part = weights[0].shape[0]
    per = pl.num_programs(0)
    value = dot_nt(grad[...], stacked(weights))
    for r in range(PIECES):
        block = (scal[0] ^ r) * per + step
        put_lanes(
            out,
            block,
            part,
            (value[:, r * part : (r + 1) * part] * lanes(slope, block, part).astype(F32)).astype(
                BF16
            ),
        )


def narrow_back(scal, grad, slope, pieces, steps=4):
    rows, features = grad.shape
    depth = pieces[0].shape[0]
    hidden = slope.shape[1]
    return call(
        narrow_back_body,
        (steps,),
        [whole((rows, features)), whole((rows, hidden))]
        + [pl.BlockSpec((depth // steps, features), lambda n, s: (n, 0))] * PIECES,
        whole((rows, hidden)),
        jax.ShapeDtypeStruct((rows, hidden), BF16),
        [],
        2 * rows * features * hidden,
        2 * features * hidden + 4 * rows * hidden,
        "narrow_back",
    )(scal, grad, slope, *pieces)


def norm_back(grad, normal, inverse, gain):
    scaled = grad * gain
    return inverse * (
        scaled
        - jnp.mean(scaled, axis=-1, keepdims=True)
        - normal * jnp.mean(scaled * normal, axis=-1, keepdims=True)
    )


def rows_sum(value):
    return jnp.sum(value, axis=0, keepdims=True)


def widen_back_body(scal, *refs, unit):
    grad, mixed, dy, gain = refs[:4]
    weights = refs[4:12]
    dmixed, dbranch, sums, bias_sum, acc, nat = refs[12:]
    step = pl.program_id(0)
    value = grad[...]
    bias_sum[...] = rows_sum(value.astype(F32))
    part = dot_nt(value, stacked(weights))

    @pl.when(step == 0)
    def _():
        acc[...] = part

    @pl.when(step > 0)
    def _():
        acc[...] += part

    @pl.when(step == pl.num_programs(0) - 1)
    def _():
        width = acc.shape[1] // PIECES
        totals = [0.0] * 4
        for b in range(acc.shape[0] // unit):
            span = pl.ds(b * unit, unit)
            for r in range(PIECES):
                put_lanes(
                    nat, scal[0] ^ r, width, acc[span, r * width : (r + 1) * width]
                )
            normal, inverse = stats(mixed[span, :])
            grad_out = dy[span, :].astype(F32)
            back = nat[...]
            total = grad_out + norm_back(back, normal, inverse, gain[...])
            dmixed[span, :] = total
            flag = (scal[2 + b] > 0).astype(F32)
            low = (total * flag).astype(BF16)
            dbranch[span, :] = low
            parts = (back * normal, back, low.astype(F32), grad_out)
            totals = [t + rows_sum(p) for t, p in zip(totals, parts)]
        sums[...] = jnp.concatenate(totals + [jnp.zeros((4, acc.shape[1]), F32)], axis=0)


def widen_back(scal, grad, mixed, dy, gain, pieces, unit, tile=1024):
    rows, hidden = grad.shape
    depth = pieces[0].shape[0]
    features = mixed.shape[1]
    full = whole((rows, features))
    return call(
        functools.partial(widen_back_body, unit=unit),
        (hidden // tile,),
        [pl.BlockSpec((rows, tile), lambda n, s: (0, n)), full, full, whole((1, features))]
        + [pl.BlockSpec((depth, tile), lambda n, s: (0, n))] * PIECES,
        [
            full,
            full,
            whole((8, features)),
            pl.BlockSpec((1, tile), lambda n, s: (0, n)),
        ],
        [
            jax.ShapeDtypeStruct((rows, features), F32),
            jax.ShapeDtypeStruct((rows, features), BF16),
            jax.ShapeDtypeStruct((8, features), F32),
            jax.ShapeDtypeStruct((1, hidden), F32),
        ],
        [pltpu.VMEM((rows, features), F32), pltpu.VMEM((unit, features), F32)],
        2 * rows * features * hidden,
        2 * features * hidden + 2 * rows * hidden + 12 * rows * features,
        "widen_back",
    )(scal, grad, mixed, dy, gain, *pieces)


def mix_back_body(scal, *refs, n_seq):
    grad = refs[0]
    weights = refs[1:9]
    outs, rel = refs[9 : 9 + n_seq], refs[-1]
    rel[...] = dot_nt(grad[...], stacked(weights)).astype(BF16)
    width = rel.shape[1] // PIECES
    per = PIECES // n_seq
    for t in range(n_seq):
        owner = lax.rem(scal[1] + t, n_seq)
        for k in range(per):
            outs[t][:, k * width : (k + 1) * width] = lanes(
                rel, scal[0] ^ (owner * per + k), width
            )


def mix_back(scal, grad, pieces, n_seq):
    rows, features = grad.shape
    group = features // n_seq
    return call(
        functools.partial(mix_back_body, n_seq=n_seq),
        (1,),
        [whole((rows, features))] + [whole(pieces[0].shape)] * PIECES,
        [whole((rows, group))] * n_seq,
        [jax.ShapeDtypeStruct((rows, group), BF16)] * n_seq,
        [pltpu.VMEM((rows, features), BF16)],
        2 * rows * features * features,
        4 * rows * features + 2 * features * features,
        "mix_back",
    )(scal, grad, *pieces)


def project_back_body(scal, *refs, n_seq, unit, keep):
    grads = refs[:n_seq]
    x, dmixed, gain = refs[n_seq : n_seq + 3]
    weights = refs[n_seq + 3 : n_seq + 11]
    out, sums, acc, nat, wide = refs[n_seq + 11 :]
    step = pl.program_id(0)
    width = acc.shape[1] // PIECES
    for t in range(n_seq):
        put_lanes(
            wide, lax.rem(scal[1] + n_seq - t, n_seq), grads[t].shape[1], grads[t][...]
        )
    part = dot_nt(wide[...], stacked(weights, width))

    @pl.when(step == 0)
    def _():
        acc[...] = part

    @pl.when(step > 0)
    def _():
        acc[...] += part

    @pl.when(step == pl.num_programs(0) - 1)
    def _():
        totals = [0.0] * 2
        for b in range(acc.shape[0] // unit):
            span = pl.ds(b * unit, unit)
            for r in range(PIECES):
                put_lanes(
                    nat, scal[0] ^ r, width, acc[span, r * width : (r + 1) * width]
                )
            normal, inverse = stats(x[span, :].astype(F32))
            back = nat[...]
            total = dmixed[span, :] + norm_back(back, normal, inverse, gain[...])
            out[b] = total[:keep]
            totals = [t + rows_sum(p) for t, p in zip(totals, (back * normal, back))]
        sums[...] = jnp.concatenate(totals + [jnp.zeros((6, acc.shape[1]), F32)], axis=0)


def project_back(scal, grads, x, dmixed, gain, pieces, unit, keep):
    n_seq = len(grads)
    rows, features = x.shape
    group = features // n_seq
    depth = pieces[0].shape[0]
    images = rows // unit
    full = whole((rows, features))
    return call(
        functools.partial(project_back_body, n_seq=n_seq, unit=unit, keep=keep),
        (3,),
        [pl.BlockSpec((rows, group), lambda j, s: (0, j))] * n_seq
        + [full, full, whole((1, features))]
        + [pl.BlockSpec((depth, features), lambda j, s: (0, j))] * PIECES,
        [whole((images, keep, features)), whole((8, features))],
        [
            jax.ShapeDtypeStruct((images, keep, features), F32),
            jax.ShapeDtypeStruct((8, features), F32),
        ],
        [
            pltpu.VMEM((rows, features), F32),
            pltpu.VMEM((unit, features), F32),
            pltpu.VMEM((rows, features), BF16),
        ],
        6 * rows * features * features,
        6 * features * features + 16 * rows * features,
        "project_back",
    )(scal, *grads, x, dmixed, gain, *pieces)


def flip(value, bit):
    return lax.ppermute(value, "fsdp", [(i, i ^ bit) for i in range(PIECES)])


def flip_mixed(value):
    return lax.ppermute(
        value, "fsdp", [(i, i ^ (4 if i & 1 else 2)) for i in range(PIECES)]
    )


def gather_pieces(shard, odd):
    along_x = flip(shard, 2)
    along_y = flip(shard, 4)
    far = flip_mixed(jnp.where(odd, along_x, along_y))
    pieces = []
    for piece in (shard, along_x, along_y, far):
        pieces += [piece, flip(piece, 1)]
    return pieces


def gather_whole(shard):
    full = lax.all_gather(shard, "fsdp", axis=0, tiled=True)
    size = full.shape[0] // PIECES
    return [full[r * size : (r + 1) * size] for r in range(PIECES)]


def add32(*values):
    total = values[0].astype(F32)
    for value in values[1:]:
        total = total + value.astype(F32)
    return total


def scatter_pieces(theirs_fn, mine_fn, odd):
    theirs = theirs_fn()
    summed = mine_fn(flip(theirs, 1))
    passed = flip_mixed(summed[3])
    none = jnp.zeros_like(passed)
    to_x = add32(summed[1], jnp.where(odd, passed, none)).astype(BF16)
    to_y = add32(summed[2], jnp.where(odd, none, passed)).astype(BF16)
    return add32(summed[0], flip(to_x, 2), flip(to_y, 4))


def scatter_whole(theirs_fn, mine_fn):
    theirs = theirs_fn()
    mine = mine_fn(jnp.zeros_like(theirs))
    full = jnp.stack([mine, theirs], axis=1)
    full = full.reshape(PIECES * full.shape[2], full.shape[3])
    return lax.psum_scatter(full.astype(F32), "fsdp", scatter_dimension=0, tiled=True)


def swap_seq(value, bit, n_seq):
    return lax.ppermute(value, "seq", [(i, i ^ bit) for i in range(n_seq)])


def shift_seq(value, amount, n_seq):
    return lax.ppermute(value, "seq", [(i, (i + amount) % n_seq) for i in range(n_seq)])


def sum_seq(value, place, n_seq):
    bits = [1 << k for k in range(n_seq.bit_length() - 1)]
    for bit in bits:
        half = value.shape[0] // 2
        upper = (place & bit) != 0
        first, second = value[:half], value[half:]
        sent = jnp.where(upper, first, second).astype(BF16)
        value = jnp.where(upper, second, first).astype(F32) + swap_seq(sent, bit, n_seq)
    value = value.astype(BF16)
    for bit in reversed(bits):
        upper = (place & bit) != 0
        other = swap_seq(value, bit, n_seq)
        value = jnp.concatenate(
            [jnp.where(upper, other, value), jnp.where(upper, value, other)], axis=0
        )
    return value.astype(F32)


def butterfly(value, n_fsdp, n_seq):
    for bit in (1 << k for k in range(n_fsdp.bit_length() - 1)):
        value = value + lax.ppermute(value, "fsdp", [(i, i ^ bit) for i in range(n_fsdp)])
    for bit in (1 << k for k in range(n_seq.bit_length() - 1)):
        value = value + swap_seq(value, bit, n_seq)
    return value


def line_gather(x, n_seq):
    ups, downs = [], []
    up = down = x
    for t in range(1, n_seq):
        up = lax.ppermute(up, "seq", [(i, i + 1) for i in range(t - 1, n_seq - 1)])
        down = lax.ppermute(down, "seq", [(i + 1, i) for i in range(0, n_seq - t)])
        ups.append(up)
        downs.append(down)
    return [(x,)] + [(downs[t - 1], ups[n_seq - t - 1]) for t in range(1, n_seq)]


def on_device(
    n_fsdp,
    n_seq,
    tokens,
    counts,
    norm1_gain,
    norm1_shift,
    qkv_weight,
    query_bias,
    value_bias,
    out_weight,
    out_bias,
    norm2_gain,
    norm2_shift,
    fc1_weight,
    fc1_bias,
    fc2_weight,
    fc2_bias,
    cotangent,
):
    images, local_len, features = tokens.shape
    hidden = fc1_weight.shape[1]
    unit = -(-local_len // 16) * 16
    group = features // n_seq
    shard = lax.axis_index("fsdp")
    place = lax.axis_index("seq")
    cross = n_fsdp == PIECES
    odd = (shard & 1) == 1
    me = shard if cross else jnp.zeros_like(shard)
    scal = jnp.concatenate([jnp.stack([me, place]).astype(jnp.int32), counts])
    gather = functools.partial(gather_pieces, odd=odd) if cross else gather_whole
    scatter = functools.partial(scatter_pieces, odd=odd) if cross else scatter_whole

    padding = ((0, 0), (0, unit - local_len), (0, 0))
    x = jnp.pad(tokens, padding).reshape(images * unit, features)
    dy = jnp.pad(cotangent, padding).reshape(images * unit, features)

    vectors = (
        norm1_gain,
        norm1_shift,
        query_bias,
        value_bias,
        out_bias,
        norm2_gain,
        norm2_shift,
        fc2_bias,
        fc1_bias,
    )
    if cross:
        packed = jnp.concatenate(vectors)
        extra = jnp.pad(packed[None], ((0, 15), (0, qkv_weight.shape[1] - packed.shape[0])))
        qkv_pieces = gather(jnp.concatenate([qkv_weight, extra], axis=0))
        depth = features // PIECES
        held = jnp.stack([p[depth, : packed.shape[0]] for p in qkv_pieces]).astype(F32)
        order = jnp.arange(PIECES)
        match = (order[:, None] ^ me) == order[None, :]
        held = jnp.sum(jnp.where(match[:, :, None], held[None], 0.0), axis=1)
        full, at = [], 0
        for v in vectors:
            full.append(held[:, at : at + v.shape[0]].reshape(1, -1))
            at += v.shape[0]
    else:
        qkv_pieces = gather(qkv_weight)
        full = [
            lax.all_gather(v, "fsdp", axis=0, tiled=True).astype(F32).reshape(1, -1)
            for v in vectors
        ]
    gain1, shift1, bias_q, bias_v, bias_o, gain2, shift2, bias_2, bias_1 = full
    slots = line_gather(x, n_seq)
    out_pieces = gather(out_weight)
    fc1_pieces = gather(fc1_weight)
    fc2_pieces = gather(fc2_weight)

    own = lambda v: lax.dynamic_slice_in_dim(v, place * group, group, axis=1)
    bias = jnp.stack([own(bias_q), jnp.zeros((1, group), F32), own(bias_v)])

    spot = jnp.arange(n_seq * unit)
    owner = (spot // unit + place) % n_seq
    inside = spot % unit
    position = owner * local_len + inside
    mask = jnp.where(position[None] < counts[:, None], 0.0, MASKED)
    mask = jnp.where(inside[None] < local_len, mask, 2 * MASKED).astype(F32)[:, None]

    projected, normed = [], []
    for s in range(n_seq):
        out, h = project(scal, slots[s], gain1, shift1, bias, qkv_pieces, n_seq, s, unit)
        projected.append(out)
        normed.append(h)
    *contexts, lse = attend(scal, projected, mask, unit, images)
    contexts = [contexts[0]] + [shift_seq(contexts[t], t, n_seq) for t in range(1, n_seq)]
    context, mixed, normed_two = mix(
        scal, contexts, x, bias_o, gain2, shift2, out_pieces, unit
    )
    active, slope = widen(scal, normed_two, bias_1, fc1_pieces)
    output = narrow(scal, active, mixed, bias_2, fc2_pieces, unit, local_len)

    fc2_sum = scatter(
        lambda: outer_rows(scal, active, dy, 1), lambda a: outer_rows(scal, active, dy, 0, a)
    )
    grad_hidden = narrow_back(scal, dy, slope, fc2_pieces)
    fc1_sum = scatter(
        lambda: outer(scal, [normed_two], [grad_hidden], 1, 512, None, "wide"),
        lambda a: outer(scal, [normed_two], [grad_hidden], 0, 512, a, "wide"),
    )
    dmixed, dbranch, sums2, fc1_bias_sum = widen_back(
        scal, grad_hidden, mixed, dy, gain2, fc1_pieces, unit
    )
    grads = mix_back(scal, dbranch, out_pieces, n_seq)
    arrived = [grads[0]] + [
        shift_seq(grads[t], t, n_seq) for t in range(1, n_seq)
    ]
    arrived = [arrived[(n_seq - s) % n_seq] for s in range(n_seq)]
    out_sum = scatter(
        lambda: outer(scal, [context], [dbranch], 1, 512, None, "mix"),
        lambda a: outer(scal, [context], [dbranch], 0, 512, a, "mix"),
    )
    back = attend_back(scal, projected, arrived, mask, lse, unit, images)
    returned = [back[0]] + [shift_seq(back[t], t, n_seq) for t in range(1, n_seq)]
    qkv_sum = scatter(
        lambda: outer(scal, normed, back, 1, group, None, "qkv"),
        lambda a: outer(scal, normed, back, 0, group, a, "qkv"),
    )
    input_grad, sums1 = project_back(
        scal, returned, x, dmixed, gain1, qkv_pieces, unit, local_len
    )

    fc2_weight_grad = sum_seq(fc2_sum, place, n_seq)
    fc1_weight_grad = sum_seq(fc1_sum, place, n_seq)
    out_weight_grad = sum_seq(out_sum, place, n_seq)
    low = qkv_sum.astype(BF16)
    parts = [low] + [shift_seq(low, t, n_seq) for t in range(1, n_seq)]
    parts = [p.reshape(-1, 3, 1, group) for p in parts]
    where_from = (place - jnp.arange(n_seq)) % n_seq
    qkv_weight_grad = sum(
        jnp.where(
            (where_from[t] == jnp.arange(n_seq))[None, None, :, None], parts[t].astype(F32), 0.0
        )
        for t in range(n_seq)
    ).reshape(-1, 3 * features)

    heads_sum = sum(jnp.sum(b.astype(F32), axis=0) for b in back).reshape(3, group)
    spread = lambda v: lax.dynamic_update_slice_in_dim(
        jnp.zeros((features,), F32), v, place * group, axis=0
    )
    small = jnp.concatenate(
        [
            sums1[0],
            sums1[1],
            spread(heads_sum[0]),
            spread(heads_sum[2]),
            sums2[2],
            sums2[0],
            sums2[1],
            sums2[3],
            fc1_bias_sum[0],
        ]
    )
    small = butterfly(small.reshape(-1, 128), n_fsdp, n_seq).reshape(-1)
    shares, at = [], 0
    for v in vectors:
        size = v.shape[0]
        span = size * n_fsdp
        shares.append(lax.dynamic_slice_in_dim(small[at : at + span], shard * size, size))
        at += span
    g1, s1, qb, vb, ob, g2, s2, b2, b1 = shares
    return (
        output,
        input_grad,
        g1,
        s1,
        qkv_weight_grad,
        qb,
        vb,
        out_weight_grad,
        ob,
        g2,
        s2,
        fc1_weight_grad,
        b1,
        fc2_weight_grad,
        b2,
    )


def solution(mesh):
    rows, vector, matrix = P("fsdp", "seq", None), P("fsdp"), P("fsdp", None)
    return jax.shard_map(
        functools.partial(on_device, mesh.shape["fsdp"], mesh.shape["seq"]),
        mesh=mesh,
        in_specs=(
            rows,
            vector,
            vector,
            vector,
            matrix,
            vector,
            vector,
            matrix,
            vector,
            vector,
            vector,
            matrix,
            vector,
            matrix,
            vector,
            rows,
        ),
        out_specs=(
            rows,
            rows,
            vector,
            vector,
            matrix,
            vector,
            vector,
            matrix,
            vector,
            vector,
            vector,
            matrix,
            vector,
            matrix,
            vector,
        ),
        check_vma=False,
    )
```

```python
import functools

import jax
import jax.numpy as jnp
from jax import lax
from jax.experimental import pallas as pl
from jax.experimental.pallas import tpu as pltpu
from jax.sharding import PartitionSpec as P

HEAD_DIM = 64
EPS = 1e-05
MASKED = -1e30
SCALE = HEAD_DIM ** (-0.5)
F32 = jnp.float32
BF16 = jnp.bfloat16
PIECES = 8
HINT = 64
COVER = 1 << 27
LONG = ("attend_back",)
LIMIT = 62 * 1024 * 1024


def call(body, grid, in_specs, out_specs, out_shape, scratch, flops, moved, name):
    return pl.pallas_call(
        body,
        grid_spec=pltpu.PrefetchScalarGridSpec(
            num_scalar_prefetch=1,
            grid=grid,
            in_specs=in_specs,
            out_specs=out_specs,
            scratch_shapes=scratch,
        ),
        out_shape=out_shape,
        compiler_params=pltpu.CompilerParams(
            dimension_semantics=("arbitrary",) * len(grid), vmem_limit_bytes=LIMIT
        ),
        cost_estimate=pl.CostEstimate(
            flops=0,
            bytes_accessed=COVER if name in LONG else moved // HINT,
            transcendentals=0,
        ),
        name=name,
    )


def whole(shape):
    return pl.BlockSpec(shape, lambda *_: (0,) * len(shape))


def dot_nn(left, right):
    return lax.dot_general(left, right, (((1,), (0,)), ((), ())), preferred_element_type=F32)


def dot_nt(left, right):
    return lax.dot_general(left, right, (((1,), (1,)), ((), ())), preferred_element_type=F32)


def dot_tn(left, right):
    return lax.dot_general(left, right, (((0,), (0,)), ((), ())), preferred_element_type=F32)


def lanes(ref, block, width):
    return ref[:, pl.ds(pl.multiple_of(block * width, 128), width)]


def put_lanes(ref, block, width, value):
    ref[:, pl.ds(pl.multiple_of(block * width, 128), width)] = value


def stats(values):
    average = jnp.mean(values, axis=-1, keepdims=True)
    centered = values - average
    inverse = lax.rsqrt(jnp.mean(centered * centered, axis=-1, keepdims=True) + EPS)
    return centered * inverse, inverse


def stacked(refs, rows=None):
    return jnp.concatenate([r[...] if rows is None else r[:rows, :] for r in refs], axis=0)


def project_body(scal, *refs, rows, unit):
    x, gain, shift, bias_q, bias_v = refs[:5]
    weights = refs[5:13]
    out, normed, rel = refs[13:]
    step = pl.program_id(0)

    @pl.when(pl.program_id(0) == 0)
    def _():
        for start in range(0, rows, unit):
            span = pl.ds(start, unit)
            normal, _ = stats(x[span, :].astype(F32))
            normed[span, :] = (normal * gain[...] + shift[...]).astype(BF16)
        for r in range(PIECES):
            width = rel.shape[1] // PIECES
            rel[:, r * width : (r + 1) * width] = lanes(normed, scal[0] ^ r, width)

    value = dot_nn(rel[...], stacked(weights, rel.shape[1] // PIECES))
    bias = jnp.where(step == 0, bias_q[...], jnp.where(step == 2, bias_v[...], 0.0))
    out[...] = (value + bias).astype(BF16)


def project(scal, x, gain, shift, bias_q, bias_v, pieces, n_seq, slot, unit):
    rows, features = x.shape
    group = features // n_seq
    depth = pieces[0].shape[0]
    return call(
        functools.partial(project_body, rows=rows, unit=unit),
        (3,),
        [whole((rows, features))]
        + [whole((1, features))] * 2
        + [pl.BlockSpec((1, group), lambda j, s: (0, s[1]))] * 2
        + [pl.BlockSpec((depth, group), lambda j, s: (0, n_seq * j + s[1]))] * PIECES,
        [pl.BlockSpec((rows, group), lambda j, s: (0, j)), whole((rows, features))],
        [
            jax.ShapeDtypeStruct((rows, 3 * group), BF16),
            jax.ShapeDtypeStruct((rows, features), BF16),
        ],
        [pltpu.VMEM((rows, features), BF16)],
        2 * rows * features * 3 * group,
        4 * rows * features + 6 * features * group,
        f"project{slot}",
    )(scal, x, gain, shift, bias_q, bias_v, *pieces)


def unpack_body(scal, *refs):
    pieces, outs = refs[:PIECES], refs[PIECES:]
    for r, piece in enumerate(pieces):
        row = 0
        for out in outs:
            count = out.shape[1] // (PIECES * piece.shape[1])
            for k in range(count):
                put_lanes(
                    out,
                    (scal[0] ^ r) * count + k,
                    piece.shape[1],
                    piece[row : row + 1, :].astype(F32),
                )
                row += 1


def unpack(scal, pieces, start, sizes):
    outs = [jax.ShapeDtypeStruct((1, size), F32) for size in sizes]
    return call(
        unpack_body,
        (1,),
        [pl.BlockSpec((16, 128), lambda n, s: (start // 16, 0))] * PIECES,
        [whole(o.shape) for o in outs],
        outs,
        [],
        0,
        0,
        "unpack",
    )(scal, *pieces)


def half_masks(unit):
    lane = lax.broadcasted_iota(jnp.int32, (unit, 2 * HEAD_DIM), 1)
    return lane < HEAD_DIM


def split_heads(value, low):
    zero = jnp.zeros_like(value)
    return jnp.concatenate([jnp.where(low, value, zero), jnp.where(low, zero, value)], axis=0)


def join_heads(value, low, unit):
    return jnp.where(low, value[:unit], value[unit:])


def attend_body(scal, *refs, n_seq, unit):
    queries, keys, values = refs[:n_seq], refs[n_seq : 2 * n_seq], refs[2 * n_seq : 3 * n_seq]
    mask, out, lse = refs[3 * n_seq :]
    low = half_masks(unit)
    key = stacked(keys)
    value = stacked(values)
    for s in range(n_seq):
        scores = dot_nt(split_heads(queries[s][...], low), key) * SCALE + mask[0]
        top = jnp.max(scores, axis=-1, keepdims=True)
        weight = jnp.exp(scores - top)
        total = jnp.sum(weight, axis=-1, keepdims=True)
        probs = (weight * (1.0 / total)).astype(BF16)
        out[scal[1] ^ s] = join_heads(dot_nn(probs, value), low, unit).astype(BF16)
        log_total = top + jnp.log(total)
        lse[0, 0, s * unit : (s + 1) * unit, :] = jnp.where(
            low, log_total[:unit], log_total[unit:]
        )


def qkv_specs(n_seq, unit, pairs):
    specs = []
    for j in range(3):
        specs += [
            pl.BlockSpec((unit, 2 * HEAD_DIM), lambda b, p, s, j=j: (b, pairs * j + p))
        ] * n_seq
    return specs


def attend(scal, projected, mask, unit, images):
    n_seq = len(projected)
    rows, wide = projected[0].shape
    group = wide // 3
    pairs = group // (2 * HEAD_DIM)
    tokens = n_seq * unit
    return call(
        functools.partial(attend_body, n_seq=n_seq, unit=unit),
        (images, pairs),
        qkv_specs(n_seq, unit, pairs) + [pl.BlockSpec((1, 1, tokens), lambda b, p, s: (b, 0, 0))],
        [
            pl.BlockSpec((n_seq, unit, 2 * HEAD_DIM), lambda b, p, s: (0, b, p)),
            pl.BlockSpec((1, 1, tokens, 2 * HEAD_DIM), lambda b, p, s: (b, p, 0, 0)),
        ],
        [
            jax.ShapeDtypeStruct((n_seq, rows, group), BF16),
            jax.ShapeDtypeStruct((images, pairs, tokens, 2 * HEAD_DIM), F32),
        ],
        [],
        images * pairs * 2 * tokens * tokens * 2 * HEAD_DIM * 4,
        n_seq * rows * wide * 4,
        "attend",
    )(scal, *projected, *projected, *projected, mask)


def put_slot(ref, slot, block, value):
    width = value.shape[1]
    ref[slot, :, pl.ds(pl.multiple_of(block * width, 128), width)] = value


def attend_back_body(scal, *refs, n_seq, unit, pairs):
    queries, keys, values = refs[:n_seq], refs[n_seq : 2 * n_seq], refs[2 * n_seq : 3 * n_seq]
    grads, mask, lse, out, key_acc, value_acc = refs[3 * n_seq :]
    pair = pl.program_id(1)
    low = half_masks(unit)
    key = stacked(keys)
    value = stacked(values)
    for s in range(n_seq):
        query = split_heads(queries[s][...], low)
        slot = scal[1] ^ s
        grad = split_heads(grads[slot], low)
        scores = dot_nt(query, key) * SCALE + mask[0]
        saved = lse[0, 0, s * unit : (s + 1) * unit, :]
        column = jnp.concatenate([saved[:, :1], saved[:, HEAD_DIM : HEAD_DIM + 1]], axis=0)
        probs = jnp.exp(scores - column)
        grad_probs = dot_nt(grad, value)
        value_part = dot_tn(probs.astype(BF16), grad)
        center = jnp.sum(grad_probs * probs, axis=-1, keepdims=True)
        grad_scores = (probs * (grad_probs - center)).astype(BF16)
        query_grad = join_heads(dot_nn(grad_scores, key), low, unit) * SCALE
        key_part = dot_tn(grad_scores, query)
        put_slot(out, slot, pair, query_grad.astype(BF16))
        if s == 0:
            key_acc[...] = key_part
            value_acc[...] = value_part
        else:
            key_acc[...] += key_part
            value_acc[...] += value_part
    for s in range(n_seq):
        span = pl.ds(s * unit, unit)
        slot = scal[1] ^ s
        put_slot(out, slot, pairs + pair, (key_acc[span, :] * SCALE).astype(BF16))
        put_slot(out, slot, 2 * pairs + pair, value_acc[span, :].astype(BF16))


def attend_back(scal, projected, grads, mask, lse, unit, images):
    n_seq = len(projected)
    rows, wide = projected[0].shape
    group = wide // 3
    pairs = group // (2 * HEAD_DIM)
    tokens = n_seq * unit
    return call(
        functools.partial(attend_back_body, n_seq=n_seq, unit=unit, pairs=pairs),
        (images, pairs),
        qkv_specs(n_seq, unit, pairs)
        + [
            pl.BlockSpec((n_seq, unit, 2 * HEAD_DIM), lambda b, p, s: (0, b, p)),
            pl.BlockSpec((1, 1, tokens), lambda b, p, s: (b, 0, 0)),
            pl.BlockSpec((1, 1, tokens, 2 * HEAD_DIM), lambda b, p, s: (b, p, 0, 0)),
        ],
        pl.BlockSpec((n_seq, unit, wide), lambda b, p, s: (0, b, 0)),
        jax.ShapeDtypeStruct((n_seq, rows, wide), BF16),
        [pltpu.VMEM((tokens, 2 * HEAD_DIM), F32)] * 2,
        images * pairs * 2 * tokens * tokens * 2 * HEAD_DIM * 10,
        n_seq * rows * wide * 4,
        "attend_back",
    )(scal, *projected, *projected, *projected, grads, mask, lse)


def mix_body(scal, *refs, n_seq):
    contexts, x, bias, gain, shift = refs[:5]
    weights = refs[5:13]
    context, mixed, normed, rel = refs[13:]
    group = contexts.shape[2]
    for t in range(n_seq):
        context[:, t * group : (t + 1) * group] = contexts[t]
    width = rel.shape[1] // PIECES
    for r in range(PIECES):
        rel[:, r * width : (r + 1) * width] = lanes(context, scal[0] ^ r, width)
    branch = dot_nn(rel[...], stacked(weights)) + bias[...]
    flag = (scal[2 + pl.program_id(0)] > 0).astype(F32)
    value = x[...].astype(F32) + branch * flag
    mixed[...] = value
    normal, _ = stats(value)
    normed[...] = (normal * gain[...] + shift[...]).astype(BF16)


def mix(scal, contexts, x, bias, gain, shift, pieces, unit):
    n_seq = contexts.shape[0]
    rows, features = x.shape
    group = features // n_seq
    row_block = pl.BlockSpec((unit, features), lambda b, s: (b, 0))
    return call(
        functools.partial(mix_body, n_seq=n_seq),
        (rows // unit,),
        [pl.BlockSpec((n_seq, unit, group), lambda b, s: (0, b, 0)), row_block]
        + [whole((1, features))] * 3
        + [whole(pieces[0].shape)] * PIECES,
        [row_block] * 3,
        [
            jax.ShapeDtypeStruct((rows, features), BF16),
            jax.ShapeDtypeStruct((rows, features), F32),
            jax.ShapeDtypeStruct((rows, features), BF16),
        ],
        [pltpu.VMEM((unit, features), BF16)],
        2 * rows * features * features,
        12 * rows * features + 2 * features * features,
        "mix",
    )(scal, contexts, x, bias, gain, shift, *pieces)


def widen_body(scal, x, bias, grad, weight, active, grad_hidden):
    hidden = dot_nn(x[...], weight[...]) + bias[...]
    gate = jax.nn.sigmoid(1.702 * hidden)
    product = hidden * gate
    active[...] = product.astype(BF16)
    slope = gate + 1.702 * product * (1.0 - gate)
    grad_hidden[...] = (grad[...].astype(F32) * slope).astype(BF16)


def widen(scal, x, bias, grad, weight, tile=512):
    rows, features = x.shape
    hidden = weight.shape[1]
    column = pl.BlockSpec((rows, tile), lambda n, s: (0, n))
    return call(
        widen_body,
        (hidden // tile,),
        [
            whole((rows, features)),
            pl.BlockSpec((1, tile), lambda n, s: (0, n)),
            column,
            pl.BlockSpec((features, tile), lambda n, s: (0, n)),
        ],
        [column] * 2,
        [jax.ShapeDtypeStruct((rows, hidden), BF16)] * 2,
        [],
        2 * rows * features * hidden,
        2 * features * hidden + 6 * rows * hidden,
        "widen",
    )(scal, x, bias, grad, weight)


def narrow_body(scal, x, mixed, bias, weight, out, *, unit, keep):
    total = dot_nn(x[...], weight[...]) + mixed[...] + bias[...]
    for b in range(out.shape[0]):
        out[b] = total[b * unit : b * unit + keep].astype(BF16)


def narrow(scal, x, mixed, bias, weight, unit, keep, tile=256):
    rows, hidden = x.shape
    features = weight.shape[1]
    images = rows // unit
    column = lambda depth: pl.BlockSpec((depth, tile), lambda n, s: (0, n))
    return call(
        functools.partial(narrow_body, unit=unit, keep=keep),
        (features // tile,),
        [whole((rows, hidden)), column(rows), column(1), column(hidden)],
        pl.BlockSpec((images, keep, tile), lambda n, s: (0, 0, n)),
        jax.ShapeDtypeStruct((images, keep, features), BF16),
        [],
        2 * rows * features * hidden,
        2 * features * hidden + 2 * rows * hidden + 6 * rows * features,
        "narrow",
    )(scal, x, mixed, bias, weight)


def outer_rows_body(scal, left, right, *refs):
    value = dot_tn(left[...], right[...])
    if len(refs) == 1:
        refs[0][0] = value.astype(BF16)
        return
    value = (value + refs[0][0].astype(F32)).astype(BF16)
    for m, out in enumerate(refs[1:]):

        @pl.when(pl.program_id(0) == m)
        def _(out=out):
            out[...] = value


def outer_rows(scal, left, right, offset, added=None):
    rows, hidden = left.shape
    width = hidden // PIECES
    features = right.shape[1]
    block = pl.BlockSpec((1, width, features), lambda m, s: (m, 0, 0))
    half = PIECES // 2
    own = added is not None
    return call(
        outer_rows_body,
        (half,),
        [
            pl.BlockSpec((rows, width), lambda m, s: (0, s[0] ^ (2 * m + offset))),
            whole((rows, features)),
        ]
        + ([block] if own else []),
        [whole((width, features))] * half if own else block,
        [jax.ShapeDtypeStruct((width, features), BF16)] * half
        if own
        else jax.ShapeDtypeStruct((half, width, features), BF16),
        [],
        rows * hidden * features,
        hidden * features * (2 if own else 1),
        f"outer_rows{offset}",
    )(scal, left, right, *((added,) if own else ()))


def outer_body(scal, *refs, count, offset, width, summed):
    lefts, rights = refs[:count], refs[count : 2 * count]
    rel = refs[-1]
    half = PIECES // 2

    @pl.when(pl.program_id(0) == 0)
    def _():
        rows = lefts[0].shape[0]
        for i in range(count):
            for m in range(half):
                rel[i * rows : (i + 1) * rows, m * width : (m + 1) * width] = lanes(
                    lefts[i], scal[0] ^ (2 * m + offset), width
                )

    if len(rights[0].shape) == 3:
        right = jnp.concatenate([r[0] for r in rights], axis=0)
    else:
        right = stacked(rights)
    value = dot_tn(rel[...], right)
    for m in range(half):
        part = value[m * width : (m + 1) * width]
        if offset == 0:
            outs = refs[2 * count + 1 : -1]
            outs[m][...] = (part + refs[2 * count][m].astype(F32)).astype(BF16)
        else:
            refs[2 * count][m] = part.astype(BF16)
    if summed:
        refs[2 * count + 1][...] = rows_sum(right.astype(F32))


def outer(scal, lefts, rights, offset, tile, added=None, name="", summed=False):
    count = len(lefts)
    rows, features = lefts[0].shape
    wide = rights[0].shape[-1]
    if len(rights[0].shape) == 3:
        right_specs = [
            pl.BlockSpec((1, rows, tile), lambda n, s, i=i: (s[1] ^ i, 0, n))
            for i in range(count)
        ]
    else:
        right_specs = [pl.BlockSpec((rows, tile), lambda n, s: (0, n))] * count
    width = features // PIECES
    half = PIECES // 2
    block = pl.BlockSpec((half, width, tile), lambda n, s: (0, 0, n))
    own = added is not None
    return call(
        functools.partial(
            outer_body, count=count, offset=offset, width=width, summed=summed
        ),
        (wide // tile,),
        [whole((rows, features))] * count
        + right_specs
        + ([block] if own else []),
        [pl.BlockSpec((width, tile), lambda n, s: (0, n))] * half
        if own
        else [block] + [pl.BlockSpec((1, tile), lambda n, s: (0, n))] * summed,
        [jax.ShapeDtypeStruct((width, wide), BF16)] * half
        if own
        else [jax.ShapeDtypeStruct((half, width, wide), BF16)]
        + [jax.ShapeDtypeStruct((1, wide), F32)] * summed,
        [pltpu.VMEM((count * rows, half * width), BF16)],
        count * rows * features * wide,
        features * wide * (2 if own else 1) + count * 2 * rows * (features + wide),
        f"outer_{name}{offset}",
    )(scal, *lefts, *rights, *((added,) if own else ()))


def outer_two_body(scal, *refs, offset, width, first):
    lefts, rights = refs[:2], refs[2:4]
    rels = refs[-2:]
    half = PIECES // 2
    step = pl.program_id(0)

    @pl.when(step == 0)
    def _():
        for left, rel in zip(lefts, rels):
            for m in range(half):
                rel[:, m * width : (m + 1) * width] = lanes(
                    left, scal[0] ^ (2 * m + offset), width
                )

    def store(value):
        for m in range(half):
            part = value[m * width : (m + 1) * width]
            if offset == 0:
                refs[5 + m][...] = (part + refs[4][m].astype(F32)).astype(BF16)
            else:
                refs[4][m] = part.astype(BF16)

    @pl.when(step < first)
    def _():
        store(dot_tn(rels[0][...], rights[0][...]))

    @pl.when(step >= first)
    def _():
        store(dot_tn(rels[1][...], rights[1][...]))


def outer_two(scal, lefts, rights, offset, added=None, tile=512):
    rows, features = lefts[0].shape
    first = rights[0].shape[1] // tile
    count = first + rights[1].shape[1] // tile
    wide = count * tile
    width = features // PIECES
    half = PIECES // 2
    block = pl.BlockSpec((half, width, tile), lambda n, s: (0, 0, n))
    own = added is not None
    return call(
        functools.partial(outer_two_body, offset=offset, width=width, first=first),
        (count,),
        [whole((rows, features))] * 2
        + [
            pl.BlockSpec((rows, tile), lambda n, s: (0, jnp.minimum(n, first - 1))),
            pl.BlockSpec((rows, tile), lambda n, s: (0, jnp.maximum(n - first, 0))),
        ]
        + ([block] if own else []),
        [pl.BlockSpec((width, tile), lambda n, s: (0, n))] * half if own else block,
        [jax.ShapeDtypeStruct((width, wide), BF16)] * half
        if own
        else jax.ShapeDtypeStruct((half, width, wide), BF16),
        [pltpu.VMEM((rows, half * width), BF16)] * 2,
        rows * features * wide,
        features * wide * (2 if own else 1),
        f"outer_two{offset}",
    )(scal, *lefts, *rights, *((added,) if own else ()))


def narrow_back_body(scal, grad, weight, out):
    out[...] = dot_nt(grad[...], weight[...]).astype(BF16)


def narrow_back(scal, grad, weight, tile=512):
    rows, features = grad.shape
    hidden = weight.shape[0]
    return call(
        narrow_back_body,
        (hidden // tile,),
        [whole((rows, features)), pl.BlockSpec((tile, features), lambda n, s: (n, 0))],
        pl.BlockSpec((rows, tile), lambda n, s: (0, n)),
        jax.ShapeDtypeStruct((rows, hidden), BF16),
        [],
        2 * rows * features * hidden,
        2 * features * hidden + 2 * rows * hidden,
        "narrow_back",
    )(scal, grad, weight)


def norm_back(grad, normal, inverse, gain):
    scaled = grad * gain
    return inverse * (
        scaled
        - jnp.mean(scaled, axis=-1, keepdims=True)
        - normal * jnp.mean(scaled * normal, axis=-1, keepdims=True)
    )


def rows_sum(value):
    return jnp.sum(value, axis=0, keepdims=True)


def widen_back_body(scal, *refs, unit):
    grad, mixed, dy, gain, weight = refs[:5]
    dmixed, dbranch, sums, bias_sum, acc = refs[5:]
    step = pl.program_id(0)
    value = grad[...]
    bias_sum[...] = rows_sum(value.astype(F32))
    part = dot_nt(value, weight[...])

    @pl.when(step == 0)
    def _():
        acc[...] = part

    @pl.when(step > 0)
    def _():
        acc[...] += part

    @pl.when(step == pl.num_programs(0) - 1)
    def _():
        totals = [0.0] * 4
        for b in range(acc.shape[0] // unit):
            span = pl.ds(b * unit, unit)
            normal, inverse = stats(mixed[span, :])
            grad_out = dy[span, :].astype(F32)
            back = acc[span, :]
            total = grad_out + norm_back(back, normal, inverse, gain[...])
            dmixed[span, :] = total
            flag = (scal[2 + b] > 0).astype(F32)
            low = (total * flag).astype(BF16)
            dbranch[span, :] = low
            parts = (back * normal, back, low.astype(F32), grad_out)
            totals = [t + rows_sum(p) for t, p in zip(totals, parts)]
        sums[...] = jnp.concatenate(totals + [jnp.zeros((4, acc.shape[1]), F32)], axis=0)


def widen_back(scal, grad, mixed, dy, gain, weight, unit, tile=1024):
    rows, hidden = grad.shape
    features = mixed.shape[1]
    full = whole((rows, features))
    return call(
        functools.partial(widen_back_body, unit=unit),
        (hidden // tile,),
        [
            pl.BlockSpec((rows, tile), lambda n, s: (0, n)),
            full,
            full,
            whole((1, features)),
            pl.BlockSpec((features, tile), lambda n, s: (0, n)),
        ],
        [
            full,
            full,
            whole((8, features)),
            pl.BlockSpec((1, tile), lambda n, s: (0, n)),
        ],
        [
            jax.ShapeDtypeStruct((rows, features), F32),
            jax.ShapeDtypeStruct((rows, features), BF16),
            jax.ShapeDtypeStruct((8, features), F32),
            jax.ShapeDtypeStruct((1, hidden), F32),
        ],
        [pltpu.VMEM((rows, features), F32)],
        2 * rows * features * hidden,
        2 * features * hidden + 2 * rows * hidden + 12 * rows * features,
        "widen_back",
    )(scal, grad, mixed, dy, gain, weight)


def mix_back_body(scal, *refs, n_seq):
    grad = refs[0]
    weights = refs[1:9]
    out, rel = refs[9:]
    rel[...] = dot_nt(grad[...], stacked(weights)).astype(BF16)
    width = rel.shape[1] // PIECES
    per = PIECES // n_seq
    for t in range(n_seq):
        for k in range(per):
            out[t, :, k * width : (k + 1) * width] = lanes(
                rel, scal[0] ^ (t * per + k), width
            )


def mix_back(scal, grad, pieces, n_seq):
    rows, features = grad.shape
    group = features // n_seq
    return call(
        functools.partial(mix_back_body, n_seq=n_seq),
        (1,),
        [whole((rows, features))] + [whole(pieces[0].shape)] * PIECES,
        whole((n_seq, rows, group)),
        jax.ShapeDtypeStruct((n_seq, rows, group), BF16),
        [pltpu.VMEM((rows, features), BF16)],
        2 * rows * features * features,
        4 * rows * features + 2 * features * features,
        "mix_back",
    )(scal, grad, *pieces)


def project_back_body(scal, *refs, n_seq, unit, keep):
    grads, x, dmixed, gain = refs[:4]
    weights = refs[4:12]
    out, sums, acc, nat, wide = refs[12:]
    step = pl.program_id(0)
    width = acc.shape[1] // PIECES
    for t in range(n_seq):
        group = grads.shape[2]
        wide[:, t * group : (t + 1) * group] = grads[t]
    part = dot_nt(wide[...], stacked(weights, width))

    @pl.when(step == 0)
    def _():
        acc[...] = part

    @pl.when(step > 0)
    def _():
        acc[...] += part

    @pl.when(step == pl.num_programs(0) - 1)
    def _():
        totals = [0.0] * 2
        for b in range(acc.shape[0] // unit):
            span = pl.ds(b * unit, unit)
            for r in range(PIECES):
                put_lanes(
                    nat, scal[0] ^ r, width, acc[span, r * width : (r + 1) * width]
                )
            normal, inverse = stats(x[span, :].astype(F32))
            back = nat[...]
            total = dmixed[span, :] + norm_back(back, normal, inverse, gain[...])
            out[b] = total[:keep]
            totals = [t + rows_sum(p) for t, p in zip(totals, (back * normal, back))]
        sums[...] = jnp.concatenate(totals + [jnp.zeros((6, acc.shape[1]), F32)], axis=0)


def project_back(scal, grads, x, dmixed, gain, pieces, unit, keep):
    n_seq = grads.shape[0]
    rows, features = x.shape
    group = features // n_seq
    depth = pieces[0].shape[0]
    images = rows // unit
    full = whole((rows, features))
    return call(
        functools.partial(project_back_body, n_seq=n_seq, unit=unit, keep=keep),
        (3,),
        [
            pl.BlockSpec((n_seq, rows, group), lambda j, s: (0, 0, j)),
            full,
            full,
            whole((1, features)),
        ]
        + [pl.BlockSpec((depth, features), lambda j, s: (0, j))] * PIECES,
        [whole((images, keep, features)), whole((8, features))],
        [
            jax.ShapeDtypeStruct((images, keep, features), F32),
            jax.ShapeDtypeStruct((8, features), F32),
        ],
        [
            pltpu.VMEM((rows, features), F32),
            pltpu.VMEM((unit, features), F32),
            pltpu.VMEM((rows, features), BF16),
        ],
        6 * rows * features * features,
        6 * features * features + 16 * rows * features,
        "project_back",
    )(scal, grads, x, dmixed, gain, *pieces)


def flip(value, bit):
    return lax.ppermute(value, "fsdp", [(i, i ^ bit) for i in range(PIECES)])


def flip_mixed(value):
    return lax.ppermute(
        value, "fsdp", [(i, i ^ (4 if i & 1 else 2)) for i in range(PIECES)]
    )


def after(value, *others):
    return lax.optimization_barrier((value, others))[0]


def spread_near(shard):
    return flip(shard, 2), flip(shard, 4), flip(shard, 1)


def spread_far(near, odd, gate=()):
    return flip_mixed(after(jnp.where(odd, near[0], near[1]), gate))


def spread_rest(shard, near, far, near_gate=(), far_gate=()):
    return [
        shard,
        near[2],
        near[0],
        flip(after(near[0], near_gate), 1),
        near[1],
        flip(after(near[1], near_gate), 1),
        far,
        flip(after(far, far_gate), 1),
    ]


def gather_whole(shard):
    full = lax.all_gather(shard, "fsdp", axis=0, tiled=True)
    size = full.shape[0] // PIECES
    return [full[r * size : (r + 1) * size] for r in range(PIECES)]


def sides_body(scal, right, down, passed, to_x, to_y):
    odd = (scal[0] & 1) == 1
    extra = passed[...].astype(F32)
    none = jnp.zeros_like(extra)
    to_x[...] = (right[...].astype(F32) + jnp.where(odd, extra, none)).astype(BF16)
    to_y[...] = (down[...].astype(F32) + jnp.where(odd, none, extra)).astype(BF16)


def small_call(scal, body, operands, outs, name, steps=1):
    spec = lambda v: pl.BlockSpec((v.shape[0] // steps, v.shape[1]), lambda n, s: (n, 0))
    return call(
        body,
        (steps,),
        [spec(v) for v in operands],
        [spec(o) for o in outs],
        outs,
        [],
        0,
        sum(v.size for v in operands),
        name,
    )(scal, *operands)


def row_steps(value):
    return 4 if value.shape[0] % 64 == 0 else 1


def sides(scal, summed, passed):
    like = jax.ShapeDtypeStruct(passed.shape, BF16)
    return small_call(
        scal,
        sides_body,
        (summed[1], summed[2], passed),
        [like] * 2,
        "sides",
        row_steps(passed),
    )


def move_sides(pair):
    return flip(pair[0], 2), flip(pair[1], 4)


def total_body(scal, *refs):
    total = refs[0][...].astype(F32)
    for value in refs[1:-1]:
        total += value[...].astype(F32)
    refs[-1][...] = total.astype(BF16)


def total(scal, parts):
    outs = [jax.ShapeDtypeStruct(parts[0].shape, BF16)]
    return small_call(scal, total_body, parts, outs, "total", row_steps(parts[0]))[0]


def copies_body(scal, *refs):
    out, small = refs[-1], refs[-2][...]
    rows = refs[0].shape[0]
    total = refs[0][...].astype(F32)
    for value in refs[1:-2]:
        total += value[...].astype(F32)
    high = small.astype(BF16)
    rest = (small - high.astype(F32)).astype(BF16)
    lane = small.shape[1]
    for t in range(out.shape[0]):
        out[t, :rows, :] = total.astype(BF16)
        out[t, rows:, :] = jnp.zeros((small.shape[0], total.shape[1]), BF16)
        out[t, rows:, :lane] = high
        out[t, rows:, lane : 2 * lane] = rest


def copies(scal, parts, small, n_seq):
    rows, wide = parts[0].shape
    shape = (n_seq, rows + small.shape[0], wide)
    return call(
        copies_body,
        (1,),
        [whole(p.shape) for p in parts] + [whole(small.shape)],
        whole(shape),
        jax.ShapeDtypeStruct(shape, BF16),
        [],
        0,
        0,
        "copies",
    )(scal, *parts, small)


def choose_body(scal, own, other, *outs, n_seq):
    inner = (scal[1] > 0) & (scal[1] < n_seq - 1)
    value = jnp.where(inner, own[...].astype(F32), other[...].astype(F32))
    at = 0
    for out in outs:
        out[...] = value[:, at : at + out.shape[1]]
        at += out.shape[1]


def choose(scal, own, other, n_seq, widths):
    outs = [jax.ShapeDtypeStruct((own.shape[0], w), F32) for w in widths]
    body = functools.partial(choose_body, n_seq=n_seq)
    return small_call(scal, body, (own, other), outs, "choose", row_steps(own))


def inward(value, n_seq):
    last = n_seq - 1
    return lax.ppermute(value, "seq", [(0, 1), (last, last - 1)])


def across(value):
    return lax.ppermute(value, "seq", [(1, 2), (2, 1)])


def outward(value, n_seq):
    last = n_seq - 1
    return lax.ppermute(value, "seq", [(1, 0), (last - 1, last)])


def join_body(scal, parts, out, small, *, blocks):
    count = parts.shape[0]
    width = parts.shape[2] // blocks
    rows, lane = out.shape[0], small.shape[1]
    total = 0.0
    for t in range(count):
        for j in range(blocks):
            at = (j * count + t) * width
            out[:, at : at + width] = parts[t, :rows, j * width : (j + 1) * width].astype(F32)
        for j in range(2):
            total += parts[t, rows:, j * lane : (j + 1) * lane].astype(F32)
    small[...] = total


def join_columns(scal, parts, rows, lane, blocks):
    count, tall, width = parts.shape
    shapes = (rows, width * count), (tall - rows, lane)
    return call(
        functools.partial(join_body, blocks=blocks),
        (1,),
        [whole(parts.shape)],
        [whole(v) for v in shapes],
        [jax.ShapeDtypeStruct(v, F32) for v in shapes],
        [],
        0,
        0,
        "join",
    )(scal, parts)


def scatter_whole(theirs, mine):
    full = jnp.stack([jnp.stack(mine), theirs], axis=1)
    full = full.reshape(PIECES * full.shape[2], full.shape[3])
    return lax.psum_scatter(full.astype(F32), "fsdp", scatter_dimension=0, tiled=True)


def swap_seq(value, bits, n_seq):
    if bits == 0:
        return value
    return lax.ppermute(value, "seq", [(i, i ^ bits) for i in range(n_seq)])


def hop(pair, t, n_seq):
    up = lax.ppermute(pair[0], "seq", [(i, i + 1) for i in range(t - 1, n_seq - 1)])
    down = lax.ppermute(pair[1], "seq", [(i + 1, i) for i in range(0, n_seq - t)])
    return up, down


def pick(hops, s, place, n_seq):
    value = None
    for p in range(n_seq):
        distance = (p ^ s) - p
        case = hops[abs(distance) - 1][1 if distance > 0 else 0]
        value = case if value is None else jnp.where(place == p, case, value)
    return value


def exchange(value):
    return lax.all_to_all(value, "seq", 0, 0, tiled=True)


def on_device(
    n_fsdp,
    n_seq,
    tokens,
    counts,
    norm1_gain,
    norm1_shift,
    qkv_weight,
    query_bias,
    value_bias,
    out_weight,
    out_bias,
    norm2_gain,
    norm2_shift,
    fc1_weight,
    fc1_bias,
    fc2_weight,
    fc2_bias,
    cotangent,
):
    images, local_len, features = tokens.shape
    unit = -(-local_len // 16) * 16
    group = features // n_seq
    shard = lax.axis_index("fsdp")
    place = lax.axis_index("seq")
    cross = n_fsdp == PIECES
    odd = (shard & 1) == 1
    me = shard if cross else jnp.zeros_like(shard)
    scal = jnp.concatenate([jnp.stack([me, place]).astype(jnp.int32), counts])
    send = lambda arrays: [swap_seq(a, t, n_seq) for t, a in enumerate(arrays)]

    def flat(v):
        v = jnp.pad(v, ((0, 0), (0, unit - local_len), (0, 0)))
        return v.reshape(images * unit, features)

    vectors = (
        norm1_gain,
        norm1_shift,
        query_bias,
        value_bias,
        out_bias,
        norm2_gain,
        norm2_shift,
        fc2_bias,
        fc1_bias,
    )

    gather = lambda v: lax.all_gather(v, "fsdp", axis=0, tiled=True)
    hops = [hop((tokens, tokens), 1, n_seq)]
    for t in range(2, n_seq):
        hops.append(hop(hops[-1], t, n_seq))
    lane = vectors[0].shape[0]
    packed = jnp.concatenate([v.reshape(-1, lane) for v in vectors], axis=0)
    if cross:
        count = packed.shape[0]
        extra = jnp.pad(packed, ((0, -count % 16), (0, qkv_weight.shape[1] - lane)))
        qkv_shard = jnp.concatenate([qkv_weight, extra], axis=0)
        near_q = (flip(qkv_shard, 2), flip(qkv_shard, 4))
        far_q = spread_far(near_q, odd, hops[0])
        near_q = (*near_q, flip(after(qkv_shard, near_q), 1))
        qkv_pieces = spread_rest(qkv_shard, near_q, far_q, far_q)
        fc2_full = gather(after(fc2_weight, far_q))
        full = unpack(
            scal, qkv_pieces, qkv_weight.shape[0], [v.shape[0] * PIECES for v in vectors]
        )
    else:
        qkv_pieces = gather_whole(qkv_weight)
        out_pieces = gather_whole(out_weight)
        fc2_full = gather(fc2_weight)
        held = lax.all_gather(packed, "fsdp", axis=0).astype(F32)
        full, at = [], 0
        for v in vectors:
            size = v.shape[0] // lane
            full.append(held[:, at : at + size].reshape(1, -1))
            at += size
    fc1_full = gather(fc1_weight)
    gain1, shift1, bias_q, bias_v, bias_o, gain2, shift2, bias_2, bias_1 = full

    spot = jnp.arange(n_seq * unit)
    inside = spot % unit
    position = ((spot // unit) ^ place) * local_len + inside
    mask = jnp.where(position[None] < counts[:, None], 0.0, MASKED)
    mask = jnp.where(inside[None] < local_len, mask, 2 * MASKED).astype(F32)[:, None]

    x = flat(tokens)
    dy = flat(cotangent)
    projected, normed = [], []
    for s in range(n_seq):
        entry = flat(pick(after(hops, projected[: s - 1]), s, place, n_seq)) if s else x
        entry = after(entry, projected[-1:], hops[1])
        if cross and s == 1:
            near_o = spread_near(after(out_weight, projected[0]))
        if cross and s == n_seq - 1:
            far_o = spread_far(near_o, odd, projected[1])
            entry = after(entry, far_o)
        out, h = project(
            scal, entry, gain1, shift1, bias_q, bias_v, qkv_pieces, n_seq, s, unit
        )
        projected.append(out)
        normed.append(h)
    if cross:
        out_pieces = spread_rest(out_weight, near_o, far_o, projected[1], projected[2])
    contexts, lse = attend(
        scal, after(projected, out_pieces[1::2]), mask, unit, images
    )
    contexts = exchange(contexts)
    grad_active = narrow_back(scal, after(dy, lse), fc2_full)
    context, mixed, normed_two = mix(
        scal,
        contexts,
        after(x, grad_active),
        bias_o,
        gain2,
        shift2,
        out_pieces,
        unit,
    )
    active, grad_hidden = widen(scal, normed_two, bias_1, grad_active, fc1_full)

    swap = (lambda v: flip(v, 1)) if cross else jnp.zeros_like
    theirs_2 = outer_rows(scal, active, dy, 1)
    other_2 = swap(theirs_2)
    dmixed, dbranch, sums2, fc1_bias_sum = widen_back(
        scal, after(grad_hidden, theirs_2), mixed, dy, gain2, fc1_full, unit
    )
    pair_left = (normed_two, context)
    pair_right = (grad_hidden, dbranch)
    theirs_1 = outer_two(scal, after(pair_left, dmixed, other_2), pair_right, 1)
    other_1 = swap(theirs_1)
    grads = mix_back(scal, after(dbranch, theirs_1), out_pieces, n_seq)
    arrived = exchange(grads)
    mine_2 = outer_rows(scal, after(active, grads), dy, 0, other_2)
    passed_2 = flip_mixed(mine_2[3]) if cross else mine_2[3]
    mine_1 = outer_two(scal, after(pair_left, mine_2), pair_right, 0, other_1)
    passed_1 = flip_mixed(mine_1[3]) if cross else mine_1[3]
    back = attend_back(
        scal, projected, after(arrived, mine_1, passed_2), mask, lse, unit, images
    )
    returned = exchange(back)
    rights = [back] * n_seq
    if cross:
        pair_2 = sides(scal, mine_2, after(passed_2, back))
        fc2_terms = (mine_2[0], *move_sides(pair_2))
    else:
        pair_2 = ()
        fc2_terms = (scatter_whole(theirs_2, mine_2),)
    theirs_q, heads_sum = outer(
        scal, normed, after(rights, pair_2), 1, group, None, "qkv", True
    )
    other_q = swap(theirs_q)
    output = narrow(
        scal,
        after(active, theirs_q),
        mixed,
        bias_2,
        fc2_full,
        unit,
        local_len,
    )
    fc2_own = total(scal, after(fc2_terms, output))
    fc2_in = inward(fc2_own, n_seq)
    if cross:
        pair_1 = sides(scal, mine_1, after(passed_1, fc2_own))
        fc1_terms = (mine_1[0], *move_sides(pair_1))
    else:
        pair_1 = ()
        fc1_terms = (scatter_whole(theirs_1, mine_1),)
    mine_q = outer(
        scal, after(normed, fc2_own, pair_1), rights, 0, group, other_q, "qkv"
    )
    passed_q = flip_mixed(mine_q[3]) if cross else mine_q[3]
    fc2_pair = total(scal, (*fc2_terms, after(fc2_in, mine_q)))
    fc2_across = across(fc2_pair)
    fc1_own = total(scal, after(fc1_terms, fc2_pair))
    fc1_in = inward(fc1_own, n_seq)
    input_grad, sums1 = project_back(
        scal,
        returned,
        x,
        after(dmixed, fc1_own),
        gain1,
        qkv_pieces,
        unit,
        local_len,
    )

    if cross:
        pair_q = sides(scal, mine_q, after(passed_q, input_grad))
        qkv_terms = (mine_q[0], *move_sides(pair_q))
    else:
        pair_q = ()
        qkv_terms = (scatter_whole(theirs_q, mine_q),)
    heads_sum = heads_sum.reshape(3, group)
    spread = lambda v: lax.dynamic_update_slice_in_dim(
        jnp.zeros((features,), F32), v, place * group, axis=0
    )
    sums = (
        sums1[0],
        sums1[1],
        spread(heads_sum[0]),
        spread(heads_sum[2]),
        sums2[2],
        sums2[0],
        sums2[1],
        sums2[3],
        fc1_bias_sum[0],
    )
    small = jnp.concatenate([v.reshape(n_fsdp, -1, lane) for v in sums], axis=1)
    small = lax.all_to_all(small, "fsdp", 0, 0, tiled=True)
    small = jnp.sum(small, axis=0)
    small = jnp.pad(small, ((0, -small.shape[0] % 16), (0, 0)))
    fc2_done = total(scal, (fc2_pair, after(fc2_across, small, pair_q)))
    fc2_out = outward(fc2_done, n_seq)
    fc1_pair = total(scal, (*fc1_terms, after(fc1_in, fc2_done)))
    fc1_across = across(fc1_pair)
    low = copies(scal, after(qkv_terms, fc1_pair), small, n_seq)
    qkv_shares = exchange(low)
    (fc2_weight_grad,) = choose(
        scal, fc2_done, after(fc2_out, low), n_seq, (features,)
    )
    fc1_done = total(scal, (fc1_pair, after(fc1_across, fc2_weight_grad)))
    fc1_out = outward(fc1_done, n_seq)
    qkv_weight_grad, small = join_columns(
        scal, after(qkv_shares, fc1_done), qkv_weight.shape[0], lane, 3
    )
    fc1_weight_grad, out_weight_grad = choose(
        scal,
        fc1_done,
        after(fc1_out, qkv_weight_grad),
        n_seq,
        (fc1_weight.shape[1], features),
    )
    shares, at = [], 0
    for v in vectors:
        size = v.shape[0] // lane
        shares.append(small[at : at + size].reshape(-1))
        at += size
    g1, s1, qb, vb, ob, g2, s2, b2, b1 = shares
    return (
        output,
        input_grad,
        g1,
        s1,
        qkv_weight_grad,
        qb,
        vb,
        out_weight_grad,
        ob,
        g2,
        s2,
        fc1_weight_grad,
        b1,
        fc2_weight_grad,
        b2,
    )


def solution(mesh):
    rows, vector, matrix = P("fsdp", "seq", None), P("fsdp"), P("fsdp", None)
    return jax.shard_map(
        functools.partial(on_device, mesh.shape["fsdp"], mesh.shape["seq"]),
        mesh=mesh,
        in_specs=(
            rows,
            vector,
            vector,
            vector,
            matrix,
            vector,
            vector,
            matrix,
            vector,
            vector,
            vector,
            matrix,
            vector,
            matrix,
            vector,
            rows,
        ),
        out_specs=(
            rows,
            rows,
            vector,
            vector,
            matrix,
            vector,
            vector,
            matrix,
            vector,
            vector,
            vector,
            matrix,
            vector,
            matrix,
            vector,
        ),
        check_vma=False,
    )
```

```python
import functools

import jax
import jax.numpy as jnp
from jax import lax
from jax.experimental import pallas as pl
from jax.experimental.pallas import tpu as pltpu
from jax.sharding import PartitionSpec as P

HEAD_DIM = 64
EPS = 1e-05
MASKED = -1e30
SCALE = HEAD_DIM ** (-0.5)
F32 = jnp.float32
BF16 = jnp.bfloat16
PIECES = 8
HINT = 64
COVER = 1 << 27
LONG = ("attend_back",)
LIMIT = 62 * 1024 * 1024


def call(body, grid, in_specs, out_specs, out_shape, scratch, flops, moved, name):
    return pl.pallas_call(
        body,
        grid_spec=pltpu.PrefetchScalarGridSpec(
            num_scalar_prefetch=1,
            grid=grid,
            in_specs=in_specs,
            out_specs=out_specs,
            scratch_shapes=scratch,
        ),
        out_shape=out_shape,
        compiler_params=pltpu.CompilerParams(
            dimension_semantics=("arbitrary",) * len(grid), vmem_limit_bytes=LIMIT
        ),
        cost_estimate=pl.CostEstimate(
            flops=0,
            bytes_accessed=COVER if name in LONG else moved // HINT,
            transcendentals=0,
        ),
        name=name,
    )


def whole(shape):
    return pl.BlockSpec(shape, lambda *_: (0,) * len(shape))


def dot_nn(left, right):
    return lax.dot_general(left, right, (((1,), (0,)), ((), ())), preferred_element_type=F32)


def dot_nt(left, right):
    return lax.dot_general(left, right, (((1,), (1,)), ((), ())), preferred_element_type=F32)


def dot_tn(left, right):
    return lax.dot_general(left, right, (((0,), (0,)), ((), ())), preferred_element_type=F32)


def lanes(ref, block, width):
    return ref[:, pl.ds(pl.multiple_of(block * width, 128), width)]


def put_lanes(ref, block, width, value):
    ref[:, pl.ds(pl.multiple_of(block * width, 128), width)] = value


def stats(values):
    average = jnp.mean(values, axis=-1, keepdims=True)
    centered = values - average
    inverse = lax.rsqrt(jnp.mean(centered * centered, axis=-1, keepdims=True) + EPS)
    return centered * inverse, inverse


def stacked(refs, rows=None):
    return jnp.concatenate([r[...] if rows is None else r[:rows, :] for r in refs], axis=0)


def project_body(scal, *refs, rows, unit):
    x, gain, shift, bias_q, bias_v = refs[:5]
    weights = refs[5:13]
    out, normed, rel = refs[13:]
    step = pl.program_id(0)

    @pl.when(pl.program_id(0) == 0)
    def _():
        for start in range(0, rows, unit):
            span = pl.ds(start, unit)
            normal, _ = stats(x[span, :].astype(F32))
            normed[span, :] = (normal * gain[...] + shift[...]).astype(BF16)
        for r in range(PIECES):
            width = rel.shape[1] // PIECES
            rel[:, r * width : (r + 1) * width] = lanes(normed, scal[0] ^ r, width)

    value = dot_nn(rel[...], stacked(weights, rel.shape[1] // PIECES))
    bias = jnp.where(step == 0, bias_q[...], jnp.where(step == 2, bias_v[...], 0.0))
    out[...] = (value + bias).astype(BF16)


def project(scal, x, gain, shift, bias_q, bias_v, pieces, n_seq, slot, unit):
    rows, features = x.shape
    group = features // n_seq
    depth = pieces[0].shape[0]
    return call(
        functools.partial(project_body, rows=rows, unit=unit),
        (3,),
        [whole((rows, features))]
        + [whole((1, features))] * 2
        + [pl.BlockSpec((1, group), lambda j, s: (0, s[1]))] * 2
        + [pl.BlockSpec((depth, group), lambda j, s: (0, n_seq * j + s[1]))] * PIECES,
        [pl.BlockSpec((rows, group), lambda j, s: (0, j)), whole((rows, features))],
        [
            jax.ShapeDtypeStruct((rows, 3 * group), BF16),
            jax.ShapeDtypeStruct((rows, features), BF16),
        ],
        [pltpu.VMEM((rows, features), BF16)],
        2 * rows * features * 3 * group,
        4 * rows * features + 6 * features * group,
        "project",
    )(scal, x, gain, shift, bias_q, bias_v, *pieces)


def unpack_body(scal, *refs):
    pieces, outs = refs[:PIECES], refs[PIECES:]
    for r, piece in enumerate(pieces):
        row = 0
        for out in outs:
            count = out.shape[1] // (PIECES * piece.shape[1])
            for k in range(count):
                put_lanes(
                    out,
                    (scal[0] ^ r) * count + k,
                    piece.shape[1],
                    piece[row : row + 1, :].astype(F32),
                )
                row += 1


def unpack(scal, pieces, start, sizes):
    outs = [jax.ShapeDtypeStruct((1, size), F32) for size in sizes]
    return call(
        unpack_body,
        (1,),
        [pl.BlockSpec((16, 128), lambda n, s: (start // 16, 0))] * PIECES,
        [whole(o.shape) for o in outs],
        outs,
        [],
        0,
        0,
        "unpack",
    )(scal, *pieces)


def half_masks(unit):
    lane = lax.broadcasted_iota(jnp.int32, (unit, 2 * HEAD_DIM), 1)
    return lane < HEAD_DIM


def split_heads(value, low):
    zero = jnp.zeros_like(value)
    return jnp.concatenate([jnp.where(low, value, zero), jnp.where(low, zero, value)], axis=0)


def join_heads(value, low, unit):
    return jnp.where(low, value[:unit], value[unit:])


def attend_body(scal, *refs, n_seq, unit):
    queries, keys, values = refs[:n_seq], refs[n_seq : 2 * n_seq], refs[2 * n_seq : 3 * n_seq]
    mask, out, lse = refs[3 * n_seq :]
    low = half_masks(unit)
    key = stacked(keys)
    value = stacked(values)
    for s in range(n_seq):
        scores = dot_nt(split_heads(queries[s][...], low), key) * SCALE + mask[0]
        top = jnp.max(scores, axis=-1, keepdims=True)
        weight = jnp.exp(scores - top)
        total = jnp.sum(weight, axis=-1, keepdims=True)
        probs = (weight * (1.0 / total)).astype(BF16)
        out[scal[1] ^ s] = join_heads(dot_nn(probs, value), low, unit).astype(BF16)
        log_total = top + jnp.log(total)
        lse[0, 0, s * unit : (s + 1) * unit, :] = jnp.where(
            low, log_total[:unit], log_total[unit:]
        )


def qkv_specs(n_seq, unit, pairs):
    specs = []
    for j in range(3):
        specs += [
            pl.BlockSpec((unit, 2 * HEAD_DIM), lambda b, p, s, j=j: (b, pairs * j + p))
        ] * n_seq
    return specs


def attend(scal, projected, mask, unit, images):
    n_seq = len(projected)
    rows, wide = projected[0].shape
    group = wide // 3
    pairs = group // (2 * HEAD_DIM)
    tokens = n_seq * unit
    return call(
        functools.partial(attend_body, n_seq=n_seq, unit=unit),
        (images, pairs),
        qkv_specs(n_seq, unit, pairs) + [pl.BlockSpec((1, 1, tokens), lambda b, p, s: (b, 0, 0))],
        [
            pl.BlockSpec((n_seq, unit, 2 * HEAD_DIM), lambda b, p, s: (0, b, p)),
            pl.BlockSpec((1, 1, tokens, 2 * HEAD_DIM), lambda b, p, s: (b, p, 0, 0)),
        ],
        [
            jax.ShapeDtypeStruct((n_seq, rows, group), BF16),
            jax.ShapeDtypeStruct((images, pairs, tokens, 2 * HEAD_DIM), F32),
        ],
        [],
        images * pairs * 2 * tokens * tokens * 2 * HEAD_DIM * 4,
        n_seq * rows * wide * 4,
        "attend",
    )(scal, *projected, *projected, *projected, mask)


def put_slot(ref, slot, block, value):
    width = value.shape[1]
    ref[slot, :, pl.ds(pl.multiple_of(block * width, 128), width)] = value


def attend_back_body(scal, *refs, n_seq, unit, pairs):
    queries, keys, values = refs[:n_seq], refs[n_seq : 2 * n_seq], refs[2 * n_seq : 3 * n_seq]
    grads, mask, lse, out, key_acc, value_acc = refs[3 * n_seq :]
    pair = pl.program_id(1)
    low = half_masks(unit)
    key = stacked(keys)
    value = stacked(values)
    for s in range(n_seq):
        query = split_heads(queries[s][...], low)
        slot = scal[1] ^ s
        grad = split_heads(grads[slot], low)
        scores = dot_nt(query, key) * SCALE + mask[0]
        saved = lse[0, 0, s * unit : (s + 1) * unit, :]
        column = jnp.concatenate([saved[:, :1], saved[:, HEAD_DIM : HEAD_DIM + 1]], axis=0)
        probs = jnp.exp(scores - column)
        grad_probs = dot_nt(grad, value)
        value_part = dot_tn(probs.astype(BF16), grad)
        center = jnp.sum(grad_probs * probs, axis=-1, keepdims=True)
        grad_scores = (probs * (grad_probs - center)).astype(BF16)
        query_grad = join_heads(dot_nn(grad_scores, key), low, unit) * SCALE
        key_part = dot_tn(grad_scores, query)
        put_slot(out, slot, pair, query_grad.astype(BF16))
        if s == 0:
            key_acc[...] = key_part
            value_acc[...] = value_part
        else:
            key_acc[...] += key_part
            value_acc[...] += value_part
    for s in range(n_seq):
        span = pl.ds(s * unit, unit)
        slot = scal[1] ^ s
        put_slot(out, slot, pairs + pair, (key_acc[span, :] * SCALE).astype(BF16))
        put_slot(out, slot, 2 * pairs + pair, value_acc[span, :].astype(BF16))


def attend_back(scal, projected, grads, mask, lse, unit, images):
    n_seq = len(projected)
    rows, wide = projected[0].shape
    group = wide // 3
    pairs = group // (2 * HEAD_DIM)
    tokens = n_seq * unit
    return call(
        functools.partial(attend_back_body, n_seq=n_seq, unit=unit, pairs=pairs),
        (images, pairs),
        qkv_specs(n_seq, unit, pairs)
        + [
            pl.BlockSpec((n_seq, unit, 2 * HEAD_DIM), lambda b, p, s: (0, b, p)),
            pl.BlockSpec((1, 1, tokens), lambda b, p, s: (b, 0, 0)),
            pl.BlockSpec((1, 1, tokens, 2 * HEAD_DIM), lambda b, p, s: (b, p, 0, 0)),
        ],
        pl.BlockSpec((n_seq, unit, wide), lambda b, p, s: (0, b, 0)),
        jax.ShapeDtypeStruct((n_seq, rows, wide), BF16),
        [pltpu.VMEM((tokens, 2 * HEAD_DIM), F32)] * 2,
        images * pairs * 2 * tokens * tokens * 2 * HEAD_DIM * 10,
        n_seq * rows * wide * 4,
        "attend_back",
    )(scal, *projected, *projected, *projected, grads, mask, lse)


def mix_body(scal, *refs, n_seq):
    contexts, x, bias, gain, shift = refs[:5]
    weights = refs[5:13]
    context, mixed, normed, rel = refs[13:]
    group = contexts.shape[2]
    for t in range(n_seq):
        context[:, t * group : (t + 1) * group] = contexts[t]
    width = rel.shape[1] // PIECES
    for r in range(PIECES):
        rel[:, r * width : (r + 1) * width] = lanes(context, scal[0] ^ r, width)
    branch = dot_nn(rel[...], stacked(weights)) + bias[...]
    flag = (scal[2 + pl.program_id(0)] > 0).astype(F32)
    value = x[...].astype(F32) + branch * flag
    mixed[...] = value
    normal, _ = stats(value)
    normed[...] = (normal * gain[...] + shift[...]).astype(BF16)


def mix(scal, contexts, x, bias, gain, shift, pieces, unit):
    n_seq = contexts.shape[0]
    rows, features = x.shape
    group = features // n_seq
    row_block = pl.BlockSpec((unit, features), lambda b, s: (b, 0))
    return call(
        functools.partial(mix_body, n_seq=n_seq),
        (rows // unit,),
        [pl.BlockSpec((n_seq, unit, group), lambda b, s: (0, b, 0)), row_block]
        + [whole((1, features))] * 3
        + [whole(pieces[0].shape)] * PIECES,
        [row_block] * 3,
        [
            jax.ShapeDtypeStruct((rows, features), BF16),
            jax.ShapeDtypeStruct((rows, features), F32),
            jax.ShapeDtypeStruct((rows, features), BF16),
        ],
        [pltpu.VMEM((unit, features), BF16)],
        2 * rows * features * features,
        12 * rows * features + 2 * features * features,
        "mix",
    )(scal, contexts, x, bias, gain, shift, *pieces)


def widen_body(scal, x, bias, grad, weight, active, grad_hidden):
    hidden = dot_nn(x[...], weight[...]) + bias[...]
    gate = jax.nn.sigmoid(1.702 * hidden)
    product = hidden * gate
    active[...] = product.astype(BF16)
    slope = gate + 1.702 * product * (1.0 - gate)
    grad_hidden[...] = (grad[...].astype(F32) * slope).astype(BF16)


def widen(scal, x, bias, grad, weight, tile=512):
    rows, features = x.shape
    hidden = weight.shape[1]
    column = pl.BlockSpec((rows, tile), lambda n, s: (0, n))
    return call(
        widen_body,
        (hidden // tile,),
        [
            whole((rows, features)),
            pl.BlockSpec((1, tile), lambda n, s: (0, n)),
            column,
            pl.BlockSpec((features, tile), lambda n, s: (0, n)),
        ],
        [column] * 2,
        [jax.ShapeDtypeStruct((rows, hidden), BF16)] * 2,
        [],
        2 * rows * features * hidden,
        2 * features * hidden + 6 * rows * hidden,
        "widen",
    )(scal, x, bias, grad, weight)


def narrow_body(scal, x, mixed, bias, weight, out, *, unit, keep):
    total = dot_nn(x[...], weight[...]) + mixed[...] + bias[...]
    for b in range(out.shape[0]):
        out[b] = total[b * unit : b * unit + keep].astype(BF16)


def narrow(scal, x, mixed, bias, weight, unit, keep, tile=256):
    rows, hidden = x.shape
    features = weight.shape[1]
    images = rows // unit
    column = lambda depth: pl.BlockSpec((depth, tile), lambda n, s: (0, n))
    return call(
        functools.partial(narrow_body, unit=unit, keep=keep),
        (features // tile,),
        [whole((rows, hidden)), column(rows), column(1), column(hidden)],
        pl.BlockSpec((images, keep, tile), lambda n, s: (0, 0, n)),
        jax.ShapeDtypeStruct((images, keep, features), BF16),
        [],
        2 * rows * features * hidden,
        2 * features * hidden + 2 * rows * hidden + 6 * rows * features,
        "narrow",
    )(scal, x, mixed, bias, weight)


def outer_rows_body(scal, left, right, *refs):
    value = dot_tn(left[...], right[...])
    if len(refs) == 1:
        refs[0][0] = value.astype(BF16)
        return
    value = (value + refs[0][0].astype(F32)).astype(BF16)
    for m, out in enumerate(refs[1:]):

        @pl.when(pl.program_id(0) == m)
        def _(out=out):
            out[...] = value


def outer_rows(scal, left, right, offset, added=None):
    rows, hidden = left.shape
    width = hidden // PIECES
    features = right.shape[1]
    block = pl.BlockSpec((1, width, features), lambda m, s: (m, 0, 0))
    half = PIECES // 2
    own = added is not None
    return call(
        outer_rows_body,
        (half,),
        [
            pl.BlockSpec((rows, width), lambda m, s: (0, s[0] ^ (2 * m + offset))),
            whole((rows, features)),
        ]
        + ([block] if own else []),
        [whole((width, features))] * half if own else block,
        [jax.ShapeDtypeStruct((width, features), BF16)] * half
        if own
        else jax.ShapeDtypeStruct((half, width, features), BF16),
        [],
        rows * hidden * features,
        hidden * features * (2 if own else 1),
        f"outer_rows{offset}",
    )(scal, left, right, *((added,) if own else ()))


def outer_body(scal, *refs, count, offset, width, summed):
    lefts, rights = refs[:count], refs[count : 2 * count]
    rel = refs[-1]
    half = PIECES // 2

    @pl.when(pl.program_id(0) == 0)
    def _():
        rows = lefts[0].shape[0]
        for i in range(count):
            for m in range(half):
                rel[i * rows : (i + 1) * rows, m * width : (m + 1) * width] = lanes(
                    lefts[i], scal[0] ^ (2 * m + offset), width
                )

    if len(rights[0].shape) == 3:
        right = jnp.concatenate([r[0] for r in rights], axis=0)
    else:
        right = stacked(rights)
    value = dot_tn(rel[...], right)
    for m in range(half):
        part = value[m * width : (m + 1) * width]
        if offset == 0:
            outs = refs[2 * count + 1 : -1]
            outs[m][...] = (part + refs[2 * count][m].astype(F32)).astype(BF16)
        else:
            refs[2 * count][m] = part.astype(BF16)
    if summed:
        refs[2 * count + 1][...] = rows_sum(right.astype(F32))


def outer(scal, lefts, rights, offset, tile, added=None, name="", summed=False):
    count = len(lefts)
    rows, features = lefts[0].shape
    wide = rights[0].shape[-1]
    if len(rights[0].shape) == 3:
        right_specs = [
            pl.BlockSpec((1, rows, tile), lambda n, s, i=i: (s[1] ^ i, 0, n))
            for i in range(count)
        ]
    else:
        right_specs = [pl.BlockSpec((rows, tile), lambda n, s: (0, n))] * count
    width = features // PIECES
    half = PIECES // 2
    block = pl.BlockSpec((half, width, tile), lambda n, s: (0, 0, n))
    own = added is not None
    return call(
        functools.partial(
            outer_body, count=count, offset=offset, width=width, summed=summed
        ),
        (wide // tile,),
        [whole((rows, features))] * count
        + right_specs
        + ([block] if own else []),
        [pl.BlockSpec((width, tile), lambda n, s: (0, n))] * half
        if own
        else [block] + [pl.BlockSpec((1, tile), lambda n, s: (0, n))] * summed,
        [jax.ShapeDtypeStruct((width, wide), BF16)] * half
        if own
        else [jax.ShapeDtypeStruct((half, width, wide), BF16)]
        + [jax.ShapeDtypeStruct((1, wide), F32)] * summed,
        [pltpu.VMEM((count * rows, half * width), BF16)],
        count * rows * features * wide,
        features * wide * (2 if own else 1) + count * 2 * rows * (features + wide),
        f"outer_{name}{offset}",
    )(scal, *lefts, *rights, *((added,) if own else ()))


def outer_two_body(scal, *refs, offset, width, first):
    lefts, rights = refs[:2], refs[2:4]
    rels = refs[-2:]
    half = PIECES // 2
    step = pl.program_id(0)

    @pl.when(step == 0)
    def _():
        for left, rel in zip(lefts, rels):
            for m in range(half):
                rel[:, m * width : (m + 1) * width] = lanes(
                    left, scal[0] ^ (2 * m + offset), width
                )

    def store(value):
        for m in range(half):
            part = value[m * width : (m + 1) * width]
            if offset == 0:
                refs[5 + m][...] = (part + refs[4][m].astype(F32)).astype(BF16)
            else:
                refs[4][m] = part.astype(BF16)

    @pl.when(step < first)
    def _():
        store(dot_tn(rels[0][...], rights[0][...]))

    @pl.when(step >= first)
    def _():
        store(dot_tn(rels[1][...], rights[1][...]))


def outer_two(scal, lefts, rights, offset, added=None, tile=512):
    rows, features = lefts[0].shape
    first = rights[0].shape[1] // tile
    count = first + rights[1].shape[1] // tile
    wide = count * tile
    width = features // PIECES
    half = PIECES // 2
    block = pl.BlockSpec((half, width, tile), lambda n, s: (0, 0, n))
    own = added is not None
    return call(
        functools.partial(outer_two_body, offset=offset, width=width, first=first),
        (count,),
        [whole((rows, features))] * 2
        + [
            pl.BlockSpec((rows, tile), lambda n, s: (0, jnp.minimum(n, first - 1))),
            pl.BlockSpec((rows, tile), lambda n, s: (0, jnp.maximum(n - first, 0))),
        ]
        + ([block] if own else []),
        [pl.BlockSpec((width, tile), lambda n, s: (0, n))] * half if own else block,
        [jax.ShapeDtypeStruct((width, wide), BF16)] * half
        if own
        else jax.ShapeDtypeStruct((half, width, wide), BF16),
        [pltpu.VMEM((rows, half * width), BF16)] * 2,
        rows * features * wide,
        features * wide * (2 if own else 1),
        f"outer_two{offset}",
    )(scal, *lefts, *rights, *((added,) if own else ()))


def narrow_back_body(scal, grad, weight, out):
    out[...] = dot_nt(grad[...], weight[...]).astype(BF16)


def narrow_back(scal, grad, weight, tile=512):
    rows, features = grad.shape
    hidden = weight.shape[0]
    return call(
        narrow_back_body,
        (hidden // tile,),
        [whole((rows, features)), pl.BlockSpec((tile, features), lambda n, s: (n, 0))],
        pl.BlockSpec((rows, tile), lambda n, s: (0, n)),
        jax.ShapeDtypeStruct((rows, hidden), BF16),
        [],
        2 * rows * features * hidden,
        2 * features * hidden + 2 * rows * hidden,
        "narrow_back",
    )(scal, grad, weight)


def norm_back(grad, normal, inverse, gain):
    scaled = grad * gain
    return inverse * (
        scaled
        - jnp.mean(scaled, axis=-1, keepdims=True)
        - normal * jnp.mean(scaled * normal, axis=-1, keepdims=True)
    )


def rows_sum(value):
    return jnp.sum(value, axis=0, keepdims=True)


def widen_back_body(scal, *refs, unit):
    grad, mixed, dy, gain, weight = refs[:5]
    dmixed, dbranch, sums, bias_sum, acc = refs[5:]
    step = pl.program_id(0)
    value = grad[...]
    bias_sum[...] = rows_sum(value.astype(F32))
    part = dot_nt(value, weight[...])

    @pl.when(step == 0)
    def _():
        acc[...] = part

    @pl.when(step > 0)
    def _():
        acc[...] += part

    @pl.when(step == pl.num_programs(0) - 1)
    def _():
        totals = [0.0] * 4
        for b in range(acc.shape[0] // unit):
            span = pl.ds(b * unit, unit)
            normal, inverse = stats(mixed[span, :])
            grad_out = dy[span, :].astype(F32)
            back = acc[span, :]
            total = grad_out + norm_back(back, normal, inverse, gain[...])
            dmixed[span, :] = total
            flag = (scal[2 + b] > 0).astype(F32)
            low = (total * flag).astype(BF16)
            dbranch[span, :] = low
            parts = (back * normal, back, low.astype(F32), grad_out)
            totals = [t + rows_sum(p) for t, p in zip(totals, parts)]
        sums[...] = jnp.concatenate(totals + [jnp.zeros((4, acc.shape[1]), F32)], axis=0)


def widen_back(scal, grad, mixed, dy, gain, weight, unit, tile=1024):
    rows, hidden = grad.shape
    features = mixed.shape[1]
    full = whole((rows, features))
    return call(
        functools.partial(widen_back_body, unit=unit),
        (hidden // tile,),
        [
            pl.BlockSpec((rows, tile), lambda n, s: (0, n)),
            full,
            full,
            whole((1, features)),
            pl.BlockSpec((features, tile), lambda n, s: (0, n)),
        ],
        [
            full,
            full,
            whole((8, features)),
            pl.BlockSpec((1, tile), lambda n, s: (0, n)),
        ],
        [
            jax.ShapeDtypeStruct((rows, features), F32),
            jax.ShapeDtypeStruct((rows, features), BF16),
            jax.ShapeDtypeStruct((8, features), F32),
            jax.ShapeDtypeStruct((1, hidden), F32),
        ],
        [pltpu.VMEM((rows, features), F32)],
        2 * rows * features * hidden,
        2 * features * hidden + 2 * rows * hidden + 12 * rows * features,
        "widen_back",
    )(scal, grad, mixed, dy, gain, weight)


def mix_back_body(scal, *refs, n_seq):
    grad = refs[0]
    weights = refs[1:9]
    out, rel = refs[9:]
    rel[...] = dot_nt(grad[...], stacked(weights)).astype(BF16)
    width = rel.shape[1] // PIECES
    per = PIECES // n_seq
    for t in range(n_seq):
        for k in range(per):
            out[t, :, k * width : (k + 1) * width] = lanes(
                rel, scal[0] ^ (t * per + k), width
            )


def mix_back(scal, grad, pieces, n_seq):
    rows, features = grad.shape
    group = features // n_seq
    return call(
        functools.partial(mix_back_body, n_seq=n_seq),
        (1,),
        [whole((rows, features))] + [whole(pieces[0].shape)] * PIECES,
        whole((n_seq, rows, group)),
        jax.ShapeDtypeStruct((n_seq, rows, group), BF16),
        [pltpu.VMEM((rows, features), BF16)],
        2 * rows * features * features,
        4 * rows * features + 2 * features * features,
        "mix_back",
    )(scal, grad, *pieces)


def project_back_body(scal, *refs, n_seq, unit, keep):
    grads, x, dmixed, gain = refs[:4]
    weights = refs[4:12]
    out, sums, acc, nat, wide = refs[12:]
    step = pl.program_id(0)
    width = acc.shape[1] // PIECES
    for t in range(n_seq):
        group = grads.shape[2]
        wide[:, t * group : (t + 1) * group] = grads[t]
    part = dot_nt(wide[...], stacked(weights, width))

    @pl.when(step == 0)
    def _():
        acc[...] = part

    @pl.when(step > 0)
    def _():
        acc[...] += part

    @pl.when(step == pl.num_programs(0) - 1)
    def _():
        totals = [0.0] * 2
        for b in range(acc.shape[0] // unit):
            span = pl.ds(b * unit, unit)
            for r in range(PIECES):
                put_lanes(
                    nat, scal[0] ^ r, width, acc[span, r * width : (r + 1) * width]
                )
            normal, inverse = stats(x[span, :].astype(F32))
            back = nat[...]
            total = dmixed[span, :] + norm_back(back, normal, inverse, gain[...])
            out[b] = total[:keep]
            totals = [t + rows_sum(p) for t, p in zip(totals, (back * normal, back))]
        sums[...] = jnp.concatenate(totals + [jnp.zeros((6, acc.shape[1]), F32)], axis=0)


def project_back(scal, grads, x, dmixed, gain, pieces, unit, keep):
    n_seq = grads.shape[0]
    rows, features = x.shape
    group = features // n_seq
    depth = pieces[0].shape[0]
    images = rows // unit
    full = whole((rows, features))
    return call(
        functools.partial(project_back_body, n_seq=n_seq, unit=unit, keep=keep),
        (3,),
        [
            pl.BlockSpec((n_seq, rows, group), lambda j, s: (0, 0, j)),
            full,
            full,
            whole((1, features)),
        ]
        + [pl.BlockSpec((depth, features), lambda j, s: (0, j))] * PIECES,
        [whole((images, keep, features)), whole((8, features))],
        [
            jax.ShapeDtypeStruct((images, keep, features), F32),
            jax.ShapeDtypeStruct((8, features), F32),
        ],
        [
            pltpu.VMEM((rows, features), F32),
            pltpu.VMEM((unit, features), F32),
            pltpu.VMEM((rows, features), BF16),
        ],
        6 * rows * features * features,
        6 * features * features + 16 * rows * features,
        "project_back",
    )(scal, grads, x, dmixed, gain, *pieces)


def flip(value, bit):
    return lax.ppermute(value, "fsdp", [(i, i ^ bit) for i in range(PIECES)])


def flip_mixed(value):
    return lax.ppermute(
        value, "fsdp", [(i, i ^ (4 if i & 1 else 2)) for i in range(PIECES)]
    )


def after(value, *others):
    return lax.optimization_barrier((value, others))[0]


def spread_near(shard):
    return flip(shard, 2), flip(shard, 4), flip(shard, 1)


def spread_far(near, odd, gate=()):
    return flip_mixed(after(jnp.where(odd, near[0], near[1]), gate))


def spread_rest(shard, near, far, near_gate=(), far_gate=()):
    return [
        shard,
        near[2],
        near[0],
        flip(after(near[0], near_gate), 1),
        near[1],
        flip(after(near[1], near_gate), 1),
        far,
        flip(after(far, far_gate), 1),
    ]


def gather_whole(shard):
    full = lax.all_gather(shard, "fsdp", axis=0, tiled=True)
    size = full.shape[0] // PIECES
    return [full[r * size : (r + 1) * size] for r in range(PIECES)]


def sides_body(scal, right, down, passed, to_x, to_y):
    odd = (scal[0] & 1) == 1
    extra = passed[...].astype(F32)
    none = jnp.zeros_like(extra)
    to_x[...] = (right[...].astype(F32) + jnp.where(odd, extra, none)).astype(BF16)
    to_y[...] = (down[...].astype(F32) + jnp.where(odd, none, extra)).astype(BF16)


def small_call(scal, body, operands, outs, name, steps=1):
    spec = lambda v: pl.BlockSpec((v.shape[0] // steps, v.shape[1]), lambda n, s: (n, 0))
    return call(
        body,
        (steps,),
        [spec(v) for v in operands],
        [spec(o) for o in outs],
        outs,
        [],
        0,
        sum(v.size for v in operands),
        name,
    )(scal, *operands)


def row_steps(value):
    return 4 if value.shape[0] % 64 == 0 else 1


def sides(scal, summed, passed):
    like = jax.ShapeDtypeStruct(passed.shape, BF16)
    return small_call(
        scal,
        sides_body,
        (summed[1], summed[2], passed),
        [like] * 2,
        "sides",
        row_steps(passed),
    )


def move_sides(pair):
    return flip(pair[0], 2), flip(pair[1], 4)


def total_body(scal, *refs):
    total = refs[0][...].astype(F32)
    for value in refs[1:-1]:
        total += value[...].astype(F32)
    refs[-1][...] = total.astype(BF16)


def total(scal, parts, half=None):
    rows, wide = parts[0].shape
    rows = rows if half is None else rows // 2
    steps = max(1, min(4, rows // 32)) if rows % 32 == 0 else 1
    block = (rows // steps, wide)
    specs = [
        pl.BlockSpec(
            block, lambda n, s, at=half * steps if p.shape[0] > rows else 0: (n + at, 0)
        )
        for p in parts
    ]
    return call(
        total_body,
        (steps,),
        specs,
        pl.BlockSpec(block, lambda n, s: (n, 0)),
        jax.ShapeDtypeStruct((rows, wide), BF16),
        [],
        0,
        0,
        "total",
    )(scal, *parts)


def copies_body(scal, *refs):
    out, small = refs[-1], refs[-2][...]
    rows = refs[0].shape[0]
    lane = small.shape[1]
    total = refs[0][...].astype(F32)
    for value in refs[1:-2]:
        total += value[...].astype(F32)
    high = small.astype(BF16)
    rest = (small - high.astype(F32)).astype(BF16)
    for t in range(out.shape[0]):
        out[t, :rows, :] = total.astype(BF16)
        out[t, rows:, :] = jnp.zeros((small.shape[0], total.shape[1]), BF16)
        out[t, rows:, :lane] = high
        out[t, rows:, lane : 2 * lane] = rest


def copies(scal, parts, small, n_seq):
    rows, wide = parts[0].shape
    shape = (n_seq, rows + small.shape[0], wide)
    return call(
        copies_body,
        (1,),
        [whole(v.shape) for v in (*parts, small)],
        whole(shape),
        jax.ShapeDtypeStruct(shape, BF16),
        [],
        0,
        0,
        "copies",
    )(scal, *parts, small)


def choose_body(scal, *refs, n_seq, count):
    inner = (scal[1] > 0) & (scal[1] < n_seq - 1)
    for k in range(count):

        @pl.when(pl.program_id(0) == k)
        def _(k=k):
            own, other = refs[k][...].astype(F32), refs[count + k][...].astype(F32)
            value = jnp.where(inner, own, other)
            at = 0
            for out in refs[2 * count :]:
                out[...] = value[:, at : at + out.shape[1]]
                at += out.shape[1]


def choose(scal, owns, others, n_seq, widths):
    count = len(owns)
    rows = owns[0].shape[0]
    return call(
        functools.partial(choose_body, n_seq=n_seq, count=count),
        (count,),
        [whole(v.shape) for v in (*owns, *others)],
        [pl.BlockSpec((rows, w), lambda n, s: (n, 0)) for w in widths],
        [jax.ShapeDtypeStruct((rows * count, w), F32) for w in widths],
        [],
        0,
        0,
        "choose",
    )(scal, *owns, *others)


def inward(value, n_seq):
    last = n_seq - 1
    return lax.ppermute(value, "seq", [(0, 1), (last, last - 1)])


def across(value):
    return lax.ppermute(value, "seq", [(1, 2), (2, 1)])


def outward(value, n_seq):
    last = n_seq - 1
    return lax.ppermute(value, "seq", [(1, 0), (last - 1, last)])


def join_body(scal, parts, out, small):
    count = parts.shape[0]
    width = parts.shape[2] // 3
    rows, lane = out.shape[0], small.shape[1]
    total = 0.0
    for t in range(count):
        for j in range(3):
            at = (j * count + t) * width
            out[:, at : at + width] = parts[t, :rows, j * width : (j + 1) * width].astype(F32)
        for j in range(2):
            total += parts[t, rows:, j * lane : (j + 1) * lane].astype(F32)
    small[...] = total


def join(scal, parts, rows, lane):
    count, tall, wide = parts.shape
    shapes = (rows, wide * count), (tall - rows, lane)
    return call(
        join_body,
        (1,),
        [whole(parts.shape)],
        [whole(v) for v in shapes],
        [jax.ShapeDtypeStruct(v, F32) for v in shapes],
        [],
        0,
        0,
        "join",
    )(scal, parts)


def scatter_whole(theirs, mine):
    full = jnp.stack([jnp.stack(mine), theirs], axis=1)
    full = full.reshape(PIECES * full.shape[2], full.shape[3])
    return lax.psum_scatter(full.astype(F32), "fsdp", scatter_dimension=0, tiled=True)


def swap_seq(value, bits, n_seq):
    if bits == 0:
        return value
    return lax.ppermute(value, "seq", [(i, i ^ bits) for i in range(n_seq)])


def hop(pair, t, n_seq):
    up = lax.ppermute(pair[0], "seq", [(i, i + 1) for i in range(t - 1, n_seq - 1)])
    down = lax.ppermute(pair[1], "seq", [(i + 1, i) for i in range(0, n_seq - t)])
    return up, down


def pick(hops, s, place, n_seq, gate):
    used = sorted({abs((p ^ s) - p) for p in range(n_seq)})
    hops = dict(zip(used, after([hops[d - 1] for d in used], gate)))
    value = None
    for p in range(n_seq):
        distance = (p ^ s) - p
        case = hops[abs(distance)][1 if distance > 0 else 0]
        value = case if value is None else jnp.where(place == p, case, value)
    return value


def exchange(value):
    return lax.all_to_all(value, "seq", 0, 0, tiled=True)


def on_device(
    n_fsdp,
    n_seq,
    tokens,
    counts,
    norm1_gain,
    norm1_shift,
    qkv_weight,
    query_bias,
    value_bias,
    out_weight,
    out_bias,
    norm2_gain,
    norm2_shift,
    fc1_weight,
    fc1_bias,
    fc2_weight,
    fc2_bias,
    cotangent,
):
    images, local_len, features = tokens.shape
    unit = -(-local_len // 8) * 8
    group = features // n_seq
    shard = lax.axis_index("fsdp")
    place = lax.axis_index("seq")
    cross = n_fsdp == PIECES
    odd = (shard & 1) == 1
    me = shard if cross else jnp.zeros_like(shard)
    scal = jnp.concatenate([jnp.stack([me, place]).astype(jnp.int32), counts])
    send = lambda arrays: [swap_seq(a, t, n_seq) for t, a in enumerate(arrays)]

    def flat(v):
        v = jnp.pad(v, ((0, 0), (0, unit - local_len), (0, 0)))
        return v.reshape(images * unit, features)

    vectors = (
        norm1_gain,
        norm1_shift,
        query_bias,
        value_bias,
        out_bias,
        norm2_gain,
        norm2_shift,
        fc2_bias,
        fc1_bias,
    )

    gather = lambda v: lax.all_gather(v, "fsdp", axis=0, tiled=True)
    hops = [hop((tokens, tokens), 1, n_seq)]
    for t in range(2, n_seq):
        hops.append(hop(hops[-1], t, n_seq))
    lane = vectors[0].shape[0]
    packed = jnp.concatenate([v.reshape(-1, lane) for v in vectors], axis=0)
    if cross:
        count = packed.shape[0]
        extra = jnp.pad(packed, ((0, -count % 16), (0, qkv_weight.shape[1] - lane)))
        qkv_shard = jnp.concatenate([qkv_weight, extra], axis=0)
        near_q = (flip(qkv_shard, 2), flip(qkv_shard, 4))
        far_q = spread_far(near_q, odd, hops[0])
        near_q = (*near_q, flip(after(qkv_shard, near_q), 1))
        qkv_pieces = spread_rest(
            qkv_shard, near_q, far_q, hops[1], hops[1]
        )
        fc2_full = gather(after(fc2_weight, near_q[:2], hops[0]))
        full = unpack(
            scal, qkv_pieces, qkv_weight.shape[0], [v.shape[0] * PIECES for v in vectors]
        )
    else:
        qkv_pieces = gather_whole(qkv_weight)
        out_pieces = gather_whole(out_weight)
        fc2_full = gather(fc2_weight)
        held = lax.all_gather(packed, "fsdp", axis=0).astype(F32)
        full, at = [], 0
        for v in vectors:
            size = v.shape[0] // lane
            full.append(held[:, at : at + size].reshape(1, -1))
            at += size
    fc1_full = gather(fc1_weight)
    gain1, shift1, bias_q, bias_v, bias_o, gain2, shift2, bias_2, bias_1 = full

    spot = jnp.arange(n_seq * unit)
    inside = spot % unit
    position = ((spot // unit) ^ place) * local_len + inside
    mask = jnp.where(position[None] < counts[:, None], 0.0, MASKED)
    mask = jnp.where(inside[None] < local_len, mask, 2 * MASKED).astype(F32)[:, None]

    x = flat(tokens)
    dy = flat(cotangent)
    projected, normed = [], []
    for s in range(n_seq):
        entry = flat(pick(hops, s, place, n_seq, projected[: s - 1])) if s else x
        entry = after(entry, projected[-1:], hops[1])
        out, h = project(
            scal, entry, gain1, shift1, bias_q, bias_v, qkv_pieces, n_seq, s, unit
        )
        projected.append(out)
        normed.append(h)
    contexts, lse = attend(scal, projected, mask, unit, images)
    ready = ()
    if cross:
        near_o = spread_near(after(out_weight, projected[2]))
        far_o = spread_far(near_o, odd, lse)
        ready = near_o
    contexts = exchange(after(contexts, ready))
    grad_active = narrow_back(scal, after(dy, lse, ready), fc2_full)
    if cross:
        out_pieces = spread_rest(out_weight, near_o, far_o, lse, grad_active)
    context, mixed, normed_two = mix(
        scal,
        contexts,
        after(x, grad_active),
        bias_o,
        gain2,
        shift2,
        out_pieces,
        unit,
    )
    active, grad_hidden = widen(scal, normed_two, bias_1, grad_active, fc1_full)

    swap = (lambda v: flip(v, 1)) if cross else jnp.zeros_like
    theirs_2 = outer_rows(scal, active, dy, 1)
    other_2 = swap(theirs_2)
    dmixed, dbranch, sums2, fc1_bias_sum = widen_back(
        scal, after(grad_hidden, theirs_2), mixed, dy, gain2, fc1_full, unit
    )
    pair_left = (normed_two, context)
    pair_right = (grad_hidden, dbranch)
    theirs_1 = outer_two(scal, after(pair_left, dmixed, other_2), pair_right, 1)
    other_1 = swap(theirs_1)
    grads = mix_back(scal, after(dbranch, theirs_1), out_pieces, n_seq)
    arrived = exchange(grads)
    mine_2 = outer_rows(scal, after(active, grads), dy, 0, other_2)
    passed_2 = flip_mixed(mine_2[3]) if cross else mine_2[3]
    mine_1 = outer_two(scal, after(pair_left, mine_2), pair_right, 0, other_1)
    passed_1 = flip_mixed(mine_1[3]) if cross else mine_1[3]
    back = attend_back(
        scal, projected, after(arrived, mine_1), mask, lse, unit, images
    )
    if cross:
        pair_2 = sides(scal, mine_2, after(passed_2, back))
        fc2_terms = (mine_2[0], *move_sides(pair_2))
    else:
        pair_2 = ()
        fc2_terms = (scatter_whole(theirs_2, mine_2),)
    returned = exchange(after(back, pair_2, passed_1))
    rights = [back] * n_seq
    theirs_q, heads_sum = outer(
        scal, normed, after(rights, pair_2), 1, group, None, "qkv", True
    )
    other_q = swap(theirs_q)
    if cross:
        pair_1 = sides(scal, mine_1, after(passed_1, theirs_q))
        fc1_terms = (mine_1[0], *move_sides(pair_1))
    else:
        pair_1 = ()
        fc1_terms = (scatter_whole(theirs_1, mine_1),)
    output = narrow(
        scal,
        after(active, pair_1, theirs_q),
        mixed,
        bias_2,
        fc2_full,
        unit,
        local_len,
    )
    fc2_own = total(scal, after(fc2_terms, output, other_q))
    fc2_in = inward(fc2_own, n_seq)
    mine_q = outer(
        scal, after(normed, fc2_own), rights, 0, group, other_q, "qkv"
    )
    passed_q = flip_mixed(mine_q[3]) if cross else mine_q[3]
    halves = range(2)
    fc1_terms = after(fc1_terms, mine_q)
    fc1_own = [total(scal, fc1_terms, k) for k in halves]
    fc1_in = [inward(v, n_seq) for v in fc1_own]
    input_grad, sums1 = project_back(
        scal,
        returned,
        x,
        after(dmixed, fc1_own),
        gain1,
        qkv_pieces,
        unit,
        local_len,
    )

    if cross:
        pair_q = sides(scal, mine_q, after(passed_q, input_grad))
        qkv_terms = (mine_q[0], *move_sides(pair_q))
    else:
        pair_q = ()
        qkv_terms = (scatter_whole(theirs_q, mine_q),)
    fc2_pair = total(
        scal, (*fc2_terms, after(fc2_in, input_grad, fc1_in[0], pair_q))
    )
    fc2_across = across(fc2_pair)
    fc1_pair = [total(scal, (*fc1_terms, after(fc1_in[0], fc2_pair)), 0)]
    fc1_pair += [total(scal, (*fc1_terms, after(fc1_in[1], fc1_pair)), 1)]
    fc1_across = [across(v) for v in fc1_pair]
    heads_sum = heads_sum.reshape(3, group)
    spread = lambda v: lax.dynamic_update_slice_in_dim(
        jnp.zeros((features,), F32), v, place * group, axis=0
    )
    sums = (
        sums1[0],
        sums1[1],
        spread(heads_sum[0]),
        spread(heads_sum[2]),
        sums2[2],
        sums2[0],
        sums2[1],
        sums2[3],
        fc1_bias_sum[0],
    )
    small = jnp.concatenate([v.reshape(n_fsdp, -1, lane) for v in sums], axis=1)
    if cross:
        for bit in (1, 2, 4):
            small = small + flip(small, bit)
        small = lax.dynamic_index_in_dim(small, shard, 0, False)
    else:
        small = jnp.sum(lax.all_to_all(small, "fsdp", 0, 0, tiled=True), axis=0)
    small = jnp.pad(small, ((0, -small.shape[0] % 16), (0, 0)))
    low = copies(scal, after(qkv_terms, fc1_pair), small, n_seq)
    shared = exchange(low)
    fc2_done = total(scal, (fc2_pair, after(fc2_across, low)))
    fc2_out = outward(fc2_done, n_seq)
    fc1_done = [total(scal, (fc1_pair[0], after(fc1_across[0], fc2_done)))]
    (fc2_weight_grad,) = choose(
        scal, (fc2_done,), (after(fc2_out, fc1_done),), n_seq, (features,)
    )
    fc1_done += [total(scal, (fc1_pair[1], after(fc1_across[1], fc2_weight_grad)))]
    fc1_out = [outward(v, n_seq) for v in fc1_done]
    qkv_weight_grad, small = join(
        scal, after(shared, fc1_done), qkv_weight.shape[0], lane
    )
    fc1_weight_grad, out_weight_grad = choose(
        scal,
        fc1_done,
        after(fc1_out, qkv_weight_grad),
        n_seq,
        (fc1_weight.shape[1], features),
    )
    shares, at = [], 0
    for v in vectors:
        size = v.shape[0] // lane
        shares.append(small[at : at + size].reshape(-1))
        at += size
    g1, s1, qb, vb, ob, g2, s2, b2, b1 = shares
    return (
        output,
        input_grad,
        g1,
        s1,
        qkv_weight_grad,
        qb,
        vb,
        out_weight_grad,
        ob,
        g2,
        s2,
        fc1_weight_grad,
        b1,
        fc2_weight_grad,
        b2,
    )


def solution(mesh):
    rows, vector, matrix = P("fsdp", "seq", None), P("fsdp"), P("fsdp", None)
    return jax.shard_map(
        functools.partial(on_device, mesh.shape["fsdp"], mesh.shape["seq"]),
        mesh=mesh,
        in_specs=(
            rows,
            vector,
            vector,
            vector,
            matrix,
            vector,
            vector,
            matrix,
            vector,
            vector,
            vector,
            matrix,
            vector,
            matrix,
            vector,
            rows,
        ),
        out_specs=(
            rows,
            rows,
            vector,
            vector,
            matrix,
            vector,
            vector,
            matrix,
            vector,
            vector,
            vector,
            matrix,
            vector,
            matrix,
            vector,
        ),
        check_vma=False,
    )
```

```python
import functools

import jax
import jax.numpy as jnp
from jax import lax
from jax.experimental import pallas as pl
from jax.experimental.pallas import tpu as pltpu
from jax.sharding import PartitionSpec as P

HEAD_DIM = 64
EPS = 1e-05
MASKED = -1e30
SCALE = HEAD_DIM ** (-0.5)
F32 = jnp.float32
BF16 = jnp.bfloat16
PIECES = 8
HINT = 64
COVER = 1 << 27
LONG = ("attend_back",)
LIMIT = 62 * 1024 * 1024


def call(body, grid, in_specs, out_specs, out_shape, scratch, flops, moved, name):
    return pl.pallas_call(
        body,
        grid_spec=pltpu.PrefetchScalarGridSpec(
            num_scalar_prefetch=1,
            grid=grid,
            in_specs=in_specs,
            out_specs=out_specs,
            scratch_shapes=scratch,
        ),
        out_shape=out_shape,
        compiler_params=pltpu.CompilerParams(
            dimension_semantics=("arbitrary",) * len(grid), vmem_limit_bytes=LIMIT
        ),
        cost_estimate=pl.CostEstimate(
            flops=0,
            bytes_accessed=COVER if name in LONG else moved // HINT,
            transcendentals=0,
        ),
        name=name,
    )


def whole(shape):
    return pl.BlockSpec(shape, lambda *_: (0,) * len(shape))


def dot_nn(left, right):
    return lax.dot_general(left, right, (((1,), (0,)), ((), ())), preferred_element_type=F32)


def dot_nt(left, right):
    return lax.dot_general(left, right, (((1,), (1,)), ((), ())), preferred_element_type=F32)


def dot_tn(left, right):
    return lax.dot_general(left, right, (((0,), (0,)), ((), ())), preferred_element_type=F32)


def lanes(ref, block, width):
    return ref[:, pl.ds(pl.multiple_of(block * width, 128), width)]


def put_lanes(ref, block, width, value):
    ref[:, pl.ds(pl.multiple_of(block * width, 128), width)] = value


def reorder(into, source, count, where):
    width = into.shape[1] // count

    @pl.loop(0, count)
    def _(r):
        put_lanes(into, r, width, lanes(source, where(r), width))


def stats(values):
    average = jnp.mean(values, axis=-1, keepdims=True)
    centered = values - average
    inverse = lax.rsqrt(jnp.mean(centered * centered, axis=-1, keepdims=True) + EPS)
    return centered * inverse, inverse


def stacked(refs, rows=None):
    return jnp.concatenate([r[...] if rows is None else r[:rows, :] for r in refs], axis=0)


def project_body(scal, *refs, rows, unit):
    x, gain, shift, bias_q, bias_v = refs[:5]
    weights = refs[5:13]
    out, normed, rel = refs[13:]
    step = pl.program_id(0)

    @pl.when(pl.program_id(0) == 0)
    def _():
        @pl.loop(0, rows // unit)
        def _(b):
            span = pl.ds(pl.multiple_of(b * unit, 8), unit)
            normal, _ = stats(x[span, :].astype(F32))
            normed[span, :] = (normal * gain[...] + shift[...]).astype(BF16)

        reorder(rel, normed, PIECES, lambda r: scal[0] ^ r)

    value = dot_nn(rel[...], stacked(weights, rel.shape[1] // PIECES))
    bias = jnp.where(step == 0, bias_q[...], jnp.where(step == 2, bias_v[...], 0.0))
    out[...] = (value + bias).astype(BF16)


def project(scal, x, gain, shift, bias_q, bias_v, pieces, n_seq, slot, unit):
    rows, features = x.shape
    group = features // n_seq
    depth = pieces[0].shape[0]
    return call(
        functools.partial(project_body, rows=rows, unit=unit),
        (3,),
        [whole((rows, features))]
        + [whole((1, features))] * 2
        + [pl.BlockSpec((1, group), lambda j, s: (0, s[1]))] * 2
        + [pl.BlockSpec((depth, group), lambda j, s: (0, n_seq * j + s[1]))] * PIECES,
        [pl.BlockSpec((rows, group), lambda j, s: (0, j)), whole((rows, features))],
        [
            jax.ShapeDtypeStruct((rows, 3 * group), BF16),
            jax.ShapeDtypeStruct((rows, features), BF16),
        ],
        [pltpu.VMEM((rows, features), BF16)],
        2 * rows * features * 3 * group,
        4 * rows * features + 6 * features * group,
        "project",
    )(scal, x, gain, shift, bias_q, bias_v, *pieces)


def unpack_body(scal, *refs):
    pieces, outs = refs[:PIECES], refs[PIECES:]
    for r, piece in enumerate(pieces):
        row = 0
        for out in outs:
            count = out.shape[1] // (PIECES * piece.shape[1])
            for k in range(count):
                put_lanes(
                    out,
                    (scal[0] ^ r) * count + k,
                    piece.shape[1],
                    piece[row : row + 1, :].astype(F32),
                )
                row += 1


def unpack(scal, pieces, start, sizes):
    outs = [jax.ShapeDtypeStruct((1, size), F32) for size in sizes]
    return call(
        unpack_body,
        (1,),
        [pl.BlockSpec((16, 128), lambda n, s: (start // 16, 0))] * PIECES,
        [whole(o.shape) for o in outs],
        outs,
        [],
        0,
        0,
        "unpack",
    )(scal, *pieces)


def half_masks(unit):
    lane = lax.broadcasted_iota(jnp.int32, (unit, 2 * HEAD_DIM), 1)
    return lane < HEAD_DIM


def split_heads(value, low):
    zero = jnp.zeros_like(value)
    return jnp.concatenate([jnp.where(low, value, zero), jnp.where(low, zero, value)], axis=0)


def join_heads(value, low, unit):
    return jnp.where(low, value[:unit], value[unit:])


def attend_body(scal, *refs, n_seq, unit):
    queries, keys, values = refs[:n_seq], refs[n_seq : 2 * n_seq], refs[2 * n_seq : 3 * n_seq]
    mask, out, lse = refs[3 * n_seq :]
    low = half_masks(unit)
    key = stacked(keys)
    value = stacked(values)
    for s in range(n_seq):
        scores = dot_nt(split_heads(queries[s][...], low), key) * SCALE + mask[0]
        top = jnp.max(scores, axis=-1, keepdims=True)
        weight = jnp.exp(scores - top)
        total = jnp.sum(weight, axis=-1, keepdims=True)
        probs = (weight * (1.0 / total)).astype(BF16)
        out[scal[1] ^ s] = join_heads(dot_nn(probs, value), low, unit).astype(BF16)
        log_total = top + jnp.log(total)
        lse[0, 0, s * unit : (s + 1) * unit, :] = jnp.where(
            low, log_total[:unit], log_total[unit:]
        )


def qkv_specs(n_seq, unit, pairs):
    specs = []
    for j in range(3):
        specs += [
            pl.BlockSpec((unit, 2 * HEAD_DIM), lambda b, p, s, j=j: (b, pairs * j + p))
        ] * n_seq
    return specs


def attend(scal, projected, mask, unit, images):
    n_seq = len(projected)
    rows, wide = projected[0].shape
    group = wide // 3
    pairs = group // (2 * HEAD_DIM)
    tokens = n_seq * unit
    return call(
        functools.partial(attend_body, n_seq=n_seq, unit=unit),
        (images, pairs),
        qkv_specs(n_seq, unit, pairs) + [pl.BlockSpec((1, 1, tokens), lambda b, p, s: (b, 0, 0))],
        [
            pl.BlockSpec((n_seq, unit, 2 * HEAD_DIM), lambda b, p, s: (0, b, p)),
            pl.BlockSpec((1, 1, tokens, 2 * HEAD_DIM), lambda b, p, s: (b, p, 0, 0)),
        ],
        [
            jax.ShapeDtypeStruct((n_seq, rows, group), BF16),
            jax.ShapeDtypeStruct((images, pairs, tokens, 2 * HEAD_DIM), F32),
        ],
        [],
        images * pairs * 2 * tokens * tokens * 2 * HEAD_DIM * 4,
        n_seq * rows * wide * 4,
        "attend",
    )(scal, *projected, *projected, *projected, mask)


def put_slot(ref, slot, block, value):
    width = value.shape[1]
    ref[slot, :, pl.ds(pl.multiple_of(block * width, 128), width)] = value


def attend_back_body(scal, *refs, n_seq, unit, pairs):
    queries, keys, values = refs[:n_seq], refs[n_seq : 2 * n_seq], refs[2 * n_seq : 3 * n_seq]
    grads, mask, lse, out, key_acc, value_acc, held = refs[3 * n_seq :]
    pair = pl.program_id(1)
    low = half_masks(unit)
    key = stacked(keys)
    value = stacked(values)
    for s in range(n_seq):
        held[s] = queries[s][...]
    key_acc[...] = jnp.zeros_like(key_acc)
    value_acc[...] = jnp.zeros_like(value_acc)

    def one(s):
        query = split_heads(held[s], low)
        slot = scal[1] ^ s
        grad = split_heads(grads[slot], low)
        scores = dot_nt(query, key) * SCALE + mask[0]
        saved = lse[0, 0, pl.ds(pl.multiple_of(s * unit, 8), unit), :]
        column = jnp.concatenate([saved[:, :1], saved[:, HEAD_DIM : HEAD_DIM + 1]], axis=0)
        probs = jnp.exp(scores - column)
        grad_probs = dot_nt(grad, value)
        value_part = dot_tn(probs.astype(BF16), grad)
        center = jnp.sum(grad_probs * probs, axis=-1, keepdims=True)
        grad_scores = (probs * (grad_probs - center)).astype(BF16)
        query_grad = join_heads(dot_nn(grad_scores, key), low, unit) * SCALE
        key_part = dot_tn(grad_scores, query)
        put_slot(out, slot, pair, query_grad.astype(BF16))
        return key_part, value_part

    @pl.loop(0, n_seq, step=2)
    def _(s):
        first, second = one(s), one(s + 1)
        key_acc[...] += first[0] + second[0]
        value_acc[...] += first[1] + second[1]

    for s in range(n_seq):
        span = pl.ds(s * unit, unit)
        slot = scal[1] ^ s
        put_slot(out, slot, pairs + pair, (key_acc[span, :] * SCALE).astype(BF16))
        put_slot(out, slot, 2 * pairs + pair, value_acc[span, :].astype(BF16))


def attend_back(scal, projected, grads, mask, lse, unit, images):
    n_seq = len(projected)
    rows, wide = projected[0].shape
    group = wide // 3
    pairs = group // (2 * HEAD_DIM)
    tokens = n_seq * unit
    return call(
        functools.partial(attend_back_body, n_seq=n_seq, unit=unit, pairs=pairs),
        (images, pairs),
        qkv_specs(n_seq, unit, pairs)
        + [
            pl.BlockSpec((n_seq, unit, 2 * HEAD_DIM), lambda b, p, s: (0, b, p)),
            pl.BlockSpec((1, 1, tokens), lambda b, p, s: (b, 0, 0)),
            pl.BlockSpec((1, 1, tokens, 2 * HEAD_DIM), lambda b, p, s: (b, p, 0, 0)),
        ],
        pl.BlockSpec((n_seq, unit, wide), lambda b, p, s: (0, b, 0)),
        jax.ShapeDtypeStruct((n_seq, rows, wide), BF16),
        [pltpu.VMEM((tokens, 2 * HEAD_DIM), F32)] * 2
        + [pltpu.VMEM((n_seq, unit, 2 * HEAD_DIM), BF16)],
        images * pairs * 2 * tokens * tokens * 2 * HEAD_DIM * 10,
        n_seq * rows * wide * 4,
        "attend_back",
    )(scal, *projected, *projected, *projected, grads, mask, lse)


def mix_body(scal, *refs, n_seq):
    contexts, x, bias, gain, shift = refs[:5]
    weights = refs[5:13]
    context, mixed, normed, rel = refs[13:]
    group = contexts.shape[2]

    @pl.loop(0, n_seq)
    def _(t):
        put_lanes(context, t, group, contexts[t])

    reorder(rel, context, PIECES, lambda r: scal[0] ^ r)
    branch = dot_nn(rel[...], stacked(weights)) + bias[...]
    flag = (scal[2 + pl.program_id(0)] > 0).astype(F32)
    value = x[...].astype(F32) + branch * flag
    mixed[...] = value
    normal, _ = stats(value)
    normed[...] = (normal * gain[...] + shift[...]).astype(BF16)


def mix(scal, contexts, x, bias, gain, shift, pieces, unit):
    n_seq = contexts.shape[0]
    rows, features = x.shape
    group = features // n_seq
    row_block = pl.BlockSpec((unit, features), lambda b, s: (b, 0))
    return call(
        functools.partial(mix_body, n_seq=n_seq),
        (rows // unit,),
        [pl.BlockSpec((n_seq, unit, group), lambda b, s: (0, b, 0)), row_block]
        + [whole((1, features))] * 3
        + [whole(pieces[0].shape)] * PIECES,
        [row_block] * 3,
        [
            jax.ShapeDtypeStruct((rows, features), BF16),
            jax.ShapeDtypeStruct((rows, features), F32),
            jax.ShapeDtypeStruct((rows, features), BF16),
        ],
        [pltpu.VMEM((unit, features), BF16)],
        2 * rows * features * features,
        12 * rows * features + 2 * features * features,
        "mix",
    )(scal, contexts, x, bias, gain, shift, *pieces)


def widen_body(scal, x, bias, grad, weight, active, grad_hidden):
    hidden = dot_nn(x[...], weight[...]) + bias[...]
    gate = jax.nn.sigmoid(1.702 * hidden)
    product = hidden * gate
    active[...] = product.astype(BF16)
    slope = gate + 1.702 * product * (1.0 - gate)
    grad_hidden[...] = (grad[...].astype(F32) * slope).astype(BF16)


def widen(scal, x, bias, grad, weight, tile=512):
    rows, features = x.shape
    hidden = weight.shape[1]
    column = pl.BlockSpec((rows, tile), lambda n, s: (0, n))
    return call(
        widen_body,
        (hidden // tile,),
        [
            whole((rows, features)),
            pl.BlockSpec((1, tile), lambda n, s: (0, n)),
            column,
            pl.BlockSpec((features, tile), lambda n, s: (0, n)),
        ],
        [column] * 2,
        [jax.ShapeDtypeStruct((rows, hidden), BF16)] * 2,
        [],
        2 * rows * features * hidden,
        2 * features * hidden + 6 * rows * hidden,
        "widen",
    )(scal, x, bias, grad, weight)


def narrow_body(scal, x, mixed, bias, weight, out, held, *, unit, keep):
    held[...] = dot_nn(x[...], weight[...]) + mixed[...] + bias[...]

    @pl.loop(0, out.shape[0])
    def _(b):
        span = pl.ds(pl.multiple_of(b * unit, 8), unit)
        out[b] = held[span, :][:keep].astype(BF16)


def narrow(scal, x, mixed, bias, weight, unit, keep, tile=256):
    rows, hidden = x.shape
    features = weight.shape[1]
    images = rows // unit
    column = lambda depth: pl.BlockSpec((depth, tile), lambda n, s: (0, n))
    return call(
        functools.partial(narrow_body, unit=unit, keep=keep),
        (features // tile,),
        [whole((rows, hidden)), column(rows), column(1), column(hidden)],
        pl.BlockSpec((images, keep, tile), lambda n, s: (0, 0, n)),
        jax.ShapeDtypeStruct((images, keep, features), BF16),
        [pltpu.VMEM((rows, tile), F32)],
        2 * rows * features * hidden,
        2 * features * hidden + 2 * rows * hidden + 6 * rows * features,
        "narrow",
    )(scal, x, mixed, bias, weight)


def outer_rows_body(scal, left, right, *refs):
    value = dot_tn(left[...], right[...])
    if len(refs) == 1:
        refs[0][0] = value.astype(BF16)
        return
    held = refs[-1]
    held[...] = (value + refs[0][0].astype(F32)).astype(BF16)
    part = held.shape[0] // 8
    for m, out in enumerate(refs[1:-1]):

        @pl.when(pl.program_id(0) == m)
        def _(out=out):
            @pl.loop(0, 8)
            def _(i):
                span = pl.ds(pl.multiple_of(i * part, 16), part)
                out[span, :] = held[span, :]


def outer_rows(scal, left, right, offset, added=None):
    rows, hidden = left.shape
    width = hidden // PIECES
    features = right.shape[1]
    block = pl.BlockSpec((1, width, features), lambda m, s: (m, 0, 0))
    half = PIECES // 2
    own = added is not None
    return call(
        outer_rows_body,
        (half,),
        [
            pl.BlockSpec((rows, width), lambda m, s: (0, s[0] ^ (2 * m + offset))),
            whole((rows, features)),
        ]
        + ([block] if own else []),
        [whole((width, features))] * half if own else block,
        [jax.ShapeDtypeStruct((width, features), BF16)] * half
        if own
        else jax.ShapeDtypeStruct((half, width, features), BF16),
        [pltpu.VMEM((width, features), BF16)] if own else [],
        rows * hidden * features,
        hidden * features * (2 if own else 1),
        f"outer_rows{offset}",
    )(scal, left, right, *((added,) if own else ()))


def outer_body(scal, *refs, count, offset, width):
    lefts, right = refs[:count], refs[count]
    rel, acc = refs[-2:]
    half = PIECES // 2

    @pl.when(pl.program_id(0) == 0)
    def _():
        for i in range(count):
            reorder(rel.at[i], lefts[i], half, lambda m: scal[0] ^ (2 * m + offset))

    acc[...] = jnp.zeros_like(acc)

    @pl.loop(0, count)
    def _(i):
        acc[...] += dot_tn(rel[i], right[scal[1] ^ i])

    for m in range(half):
        part = acc[m * width : (m + 1) * width, :]
        if offset == 0:
            outs = refs[count + 2 : -2]
            outs[m][...] = (part + refs[count + 1][m].astype(F32)).astype(BF16)
        else:
            refs[count + 1][m] = part.astype(BF16)
    if offset:
        refs[count + 2][...] = sum(rows_sum(right[i].astype(F32)) for i in range(count))


def outer(scal, lefts, right, offset, tile, added=None, name=""):
    count = len(lefts)
    rows, features = lefts[0].shape
    wide = right.shape[2]
    width = features // PIECES
    half = PIECES // 2
    block = pl.BlockSpec((half, width, tile), lambda n, s: (0, 0, n))
    own = added is not None
    return call(
        functools.partial(outer_body, count=count, offset=offset, width=width),
        (wide // tile,),
        [whole((rows, features))] * count
        + [pl.BlockSpec((count, rows, tile), lambda n, s: (0, 0, n))]
        + ([block] if own else []),
        [pl.BlockSpec((width, tile), lambda n, s: (0, n))] * half
        if own
        else [block, pl.BlockSpec((1, tile), lambda n, s: (0, n))],
        [jax.ShapeDtypeStruct((width, wide), BF16)] * half
        if own
        else [
            jax.ShapeDtypeStruct((half, width, wide), BF16),
            jax.ShapeDtypeStruct((1, wide), F32),
        ],
        [
            pltpu.VMEM((count, rows, half * width), BF16),
            pltpu.VMEM((half * width, tile), F32),
        ],
        count * rows * features * wide,
        features * wide * (1 if offset else 2) + count * 2 * rows * (features + wide),
        f"outer_{name}{offset}",
    )(scal, *lefts, right, *(() if added is None else (added,)))


def outer_two_body(scal, *refs, offset, width, first):
    lefts, rights = refs[:2], refs[2:4]
    rels = refs[-2:]
    half = PIECES // 2
    step = pl.program_id(0)

    @pl.when(step == 0)
    def _():
        for left, rel in zip(lefts, rels):
            reorder(rel, left, half, lambda m: scal[0] ^ (2 * m + offset))

    def store(value):
        for m in range(half):
            part = value[m * width : (m + 1) * width]
            if offset == 0:
                refs[5 + m][...] = (part + refs[4][m].astype(F32)).astype(BF16)
            else:
                refs[4][m] = part.astype(BF16)

    @pl.when(step < first)
    def _():
        store(dot_tn(rels[0][...], rights[0][...]))

    @pl.when(step >= first)
    def _():
        store(dot_tn(rels[1][...], rights[1][...]))


def outer_two(scal, lefts, rights, offset, added=None, tile=512):
    rows, features = lefts[0].shape
    first = rights[0].shape[1] // tile
    count = first + rights[1].shape[1] // tile
    wide = count * tile
    width = features // PIECES
    half = PIECES // 2
    block = pl.BlockSpec((half, width, tile), lambda n, s: (0, 0, n))
    own = added is not None
    return call(
        functools.partial(outer_two_body, offset=offset, width=width, first=first),
        (count,),
        [whole((rows, features))] * 2
        + [
            pl.BlockSpec((rows, tile), lambda n, s: (0, jnp.minimum(n, first - 1))),
            pl.BlockSpec((rows, tile), lambda n, s: (0, jnp.maximum(n - first, 0))),
        ]
        + ([block] if own else []),
        [pl.BlockSpec((width, tile), lambda n, s: (0, n))] * half if own else block,
        [jax.ShapeDtypeStruct((width, wide), BF16)] * half
        if own
        else jax.ShapeDtypeStruct((half, width, wide), BF16),
        [pltpu.VMEM((rows, half * width), BF16)] * 2,
        rows * features * wide,
        features * wide * (2 if own else 1),
        f"outer_two{offset}",
    )(scal, *lefts, *rights, *((added,) if own else ()))


def narrow_back_body(scal, grad, weight, out):
    out[...] = dot_nt(grad[...], weight[...]).astype(BF16)


def narrow_back(scal, grad, weight, tile=512):
    rows, features = grad.shape
    hidden = weight.shape[0]
    return call(
        narrow_back_body,
        (hidden // tile,),
        [whole((rows, features)), pl.BlockSpec((tile, features), lambda n, s: (n, 0))],
        pl.BlockSpec((rows, tile), lambda n, s: (0, n)),
        jax.ShapeDtypeStruct((rows, hidden), BF16),
        [],
        2 * rows * features * hidden,
        2 * features * hidden + 2 * rows * hidden,
        "narrow_back",
    )(scal, grad, weight)


def norm_back(grad, normal, inverse, gain):
    scaled = grad * gain
    return inverse * (
        scaled
        - jnp.mean(scaled, axis=-1, keepdims=True)
        - normal * jnp.mean(scaled * normal, axis=-1, keepdims=True)
    )


def clear(ref, unit, condition):
    @pl.when(condition)
    def _():
        @pl.loop(0, ref.shape[0] // unit)
        def _(b):
            span = pl.ds(pl.multiple_of(b * unit, 8), unit)
            ref[span, :] = jnp.zeros((unit, ref.shape[1]), ref.dtype)


def rows_sum(value):
    return jnp.sum(value, axis=0, keepdims=True)


def widen_back_body(scal, *refs, unit):
    grad, mixed, dy, gain, weight = refs[:5]
    dmixed, dbranch, sums, bias_sum, acc = refs[5:]
    step = pl.program_id(0)
    value = grad[...]
    bias_sum[...] = rows_sum(value.astype(F32))
    clear(acc, unit, step == 0)
    part = dot_nt(value, weight[...])

    acc[...] += part

    @pl.when(step == pl.num_programs(0) - 1)
    def _():
        def image(b, totals):
            span = pl.ds(pl.multiple_of(b * unit, 8), unit)
            normal, inverse = stats(mixed[span, :])
            grad_out = dy[span, :].astype(F32)
            back = acc[span, :]
            total = grad_out + norm_back(back, normal, inverse, gain[...])
            dmixed[span, :] = total
            flag = (scal[2 + b] > 0).astype(F32)
            low = (total * flag).astype(BF16)
            dbranch[span, :] = low
            parts = (back * normal, back, low.astype(F32), grad_out)
            return tuple(t + rows_sum(p) for t, p in zip(totals, parts))

        none = jnp.zeros((1, acc.shape[1]), F32)
        totals = lax.fori_loop(0, acc.shape[0] // unit, image, (none,) * 4)
        sums[...] = jnp.concatenate(list(totals) + [none] * 4, axis=0)


def widen_back(scal, grad, mixed, dy, gain, weight, unit, tile=1024):
    rows, hidden = grad.shape
    features = mixed.shape[1]
    full = whole((rows, features))
    return call(
        functools.partial(widen_back_body, unit=unit),
        (hidden // tile,),
        [
            pl.BlockSpec((rows, tile), lambda n, s: (0, n)),
            full,
            full,
            whole((1, features)),
            pl.BlockSpec((features, tile), lambda n, s: (0, n)),
        ],
        [
            full,
            full,
            whole((8, features)),
            pl.BlockSpec((1, tile), lambda n, s: (0, n)),
        ],
        [
            jax.ShapeDtypeStruct((rows, features), F32),
            jax.ShapeDtypeStruct((rows, features), BF16),
            jax.ShapeDtypeStruct((8, features), F32),
            jax.ShapeDtypeStruct((1, hidden), F32),
        ],
        [pltpu.VMEM((rows, features), F32)],
        2 * rows * features * hidden,
        2 * features * hidden + 2 * rows * hidden + 12 * rows * features,
        "widen_back",
    )(scal, grad, mixed, dy, gain, weight)


def mix_back_body(scal, *refs, n_seq):
    grad = refs[0]
    weights = refs[1:9]
    out, rel = refs[9:]
    rel[...] = dot_nt(grad[...], stacked(weights)).astype(BF16)
    width = rel.shape[1] // PIECES
    per = PIECES // n_seq

    @pl.loop(0, n_seq)
    def _(t):
        for k in range(per):
            out[t, :, k * width : (k + 1) * width] = lanes(
                rel, scal[0] ^ (t * per + k), width
            )


def mix_back(scal, grad, pieces, n_seq, unit):
    rows, features = grad.shape
    group = features // n_seq
    return call(
        functools.partial(mix_back_body, n_seq=n_seq),
        (rows // unit,),
        [pl.BlockSpec((unit, features), lambda b, s: (b, 0))] + [whole(pieces[0].shape)] * PIECES,
        pl.BlockSpec((n_seq, unit, group), lambda b, s: (0, b, 0)),
        jax.ShapeDtypeStruct((n_seq, rows, group), BF16),
        [pltpu.VMEM((unit, features), BF16)],
        2 * rows * features * features,
        4 * rows * features + 2 * features * features,
        "mix_back",
    )(scal, grad, *pieces)


def project_back_body(scal, *refs, n_seq, unit, keep):
    grads, x, dmixed, gain = refs[:4]
    weights = refs[4:12]
    out, sums, acc, nat, wide = refs[12:]
    step = pl.program_id(0)
    width = acc.shape[1] // PIECES
    @pl.loop(0, n_seq)
    def _(t):
        put_lanes(wide, t, grads.shape[2], grads[t])

    clear(acc, unit, step == 0)
    part = dot_nt(wide[...], stacked(weights, width))

    acc[...] += part

    @pl.when(step == pl.num_programs(0) - 1)
    def _():
        def image(b, totals):
            span = pl.ds(pl.multiple_of(b * unit, 8), unit)

            @pl.loop(0, PIECES)
            def _(r):
                part = acc[span, pl.ds(pl.multiple_of(r * width, 128), width)]
                put_lanes(nat, scal[0] ^ r, width, part)

            normal, inverse = stats(x[span, :].astype(F32))
            back = nat[...]
            total = dmixed[span, :] + norm_back(back, normal, inverse, gain[...])
            out[b] = total[:keep]
            return tuple(t + rows_sum(p) for t, p in zip(totals, (back * normal, back)))

        none = jnp.zeros((1, acc.shape[1]), F32)
        totals = lax.fori_loop(0, acc.shape[0] // unit, image, (none,) * 2)
        sums[...] = jnp.concatenate(list(totals) + [none] * 6, axis=0)


def project_back(scal, grads, x, dmixed, gain, pieces, unit, keep):
    n_seq = grads.shape[0]
    rows, features = x.shape
    group = features // n_seq
    depth = pieces[0].shape[0]
    images = rows // unit
    full = whole((rows, features))
    return call(
        functools.partial(project_back_body, n_seq=n_seq, unit=unit, keep=keep),
        (3,),
        [
            pl.BlockSpec((n_seq, rows, group), lambda j, s: (0, 0, j)),
            full,
            full,
            whole((1, features)),
        ]
        + [pl.BlockSpec((depth, features), lambda j, s: (0, j))] * PIECES,
        [whole((images, keep, features)), whole((8, features))],
        [
            jax.ShapeDtypeStruct((images, keep, features), F32),
            jax.ShapeDtypeStruct((8, features), F32),
        ],
        [
            pltpu.VMEM((rows, features), F32),
            pltpu.VMEM((unit, features), F32),
            pltpu.VMEM((rows, features), BF16),
        ],
        6 * rows * features * features,
        6 * features * features + 16 * rows * features,
        "project_back",
    )(scal, grads, x, dmixed, gain, *pieces)


def flip(value, bit):
    return lax.ppermute(value, "fsdp", [(i, i ^ bit) for i in range(PIECES)])


def flip_mixed(value):
    return lax.ppermute(
        value, "fsdp", [(i, i ^ (4 if i & 1 else 2)) for i in range(PIECES)]
    )


def after(value, *others):
    return lax.optimization_barrier((value, others))[0]


def spread_near(shard):
    return flip(shard, 2), flip(shard, 4), flip(shard, 1)


def spread_far(near, odd, gate=()):
    return flip_mixed(after(jnp.where(odd, near[0], near[1]), gate))


def spread_rest(shard, near, far, near_gate=(), far_gate=()):
    return [
        shard,
        near[2],
        near[0],
        flip(after(near[0], near_gate), 1),
        near[1],
        flip(after(near[1], near_gate), 1),
        far,
        flip(after(far, far_gate), 1),
    ]


def gather_whole(shard):
    full = lax.all_gather(shard, "fsdp", axis=0, tiled=True)
    size = full.shape[0] // PIECES
    return [full[r * size : (r + 1) * size] for r in range(PIECES)]


def sides_body(scal, right, down, passed, to_x, to_y):
    odd = (scal[0] & 1) == 1
    extra = passed[...].astype(F32)
    none = jnp.zeros_like(extra)
    to_x[...] = (right[...].astype(F32) + jnp.where(odd, extra, none)).astype(BF16)
    to_y[...] = (down[...].astype(F32) + jnp.where(odd, none, extra)).astype(BF16)


def small_call(scal, body, operands, outs, name, steps=1):
    spec = lambda v: pl.BlockSpec((v.shape[0] // steps, v.shape[1]), lambda n, s: (n, 0))
    return call(
        body,
        (steps,),
        [spec(v) for v in operands],
        [spec(o) for o in outs],
        outs,
        [],
        0,
        sum(v.size for v in operands),
        name,
    )(scal, *operands)


def row_steps(value):
    return 4 if value.shape[0] % 64 == 0 else 1


def sides(scal, summed, passed):
    like = jax.ShapeDtypeStruct(passed.shape, BF16)
    return small_call(
        scal,
        sides_body,
        (summed[1], summed[2], passed),
        [like] * 2,
        "sides",
        row_steps(passed),
    )


def move_sides(pair):
    return flip(pair[0], 2), flip(pair[1], 4)


def total_body(scal, *refs):
    total = refs[0][...].astype(F32)
    for value in refs[1:-1]:
        total += value[...].astype(F32)
    refs[-1][...] = total.astype(BF16)


def total(scal, parts, half=None):
    rows, wide = parts[0].shape
    rows = rows if half is None else rows // 2
    steps = max(1, min(4, rows // 32)) if rows % 32 == 0 else 1
    block = (rows // steps, wide)
    specs = [
        pl.BlockSpec(
            block, lambda n, s, at=half * steps if p.shape[0] > rows else 0: (n + at, 0)
        )
        for p in parts
    ]
    return call(
        total_body,
        (steps,),
        specs,
        pl.BlockSpec(block, lambda n, s: (n, 0)),
        jax.ShapeDtypeStruct((rows, wide), BF16),
        [],
        0,
        0,
        "total",
    )(scal, *parts)


def copies_body(scal, *refs):
    out, small = refs[-1], refs[-2][...]
    rows = refs[0].shape[0]
    lane = small.shape[1]
    total = refs[0][...].astype(F32)
    for value in refs[1:-2]:
        total += value[...].astype(F32)
    high = small.astype(BF16)
    rest = (small - high.astype(F32)).astype(BF16)
    for t in range(out.shape[0]):
        out[t, :rows, :] = total.astype(BF16)
        out[t, rows:, :] = jnp.zeros((small.shape[0], total.shape[1]), BF16)
        out[t, rows:, :lane] = high
        out[t, rows:, lane : 2 * lane] = rest


def copies(scal, parts, small, n_seq):
    rows, wide = parts[0].shape
    shape = (n_seq, rows + small.shape[0], wide)
    return call(
        copies_body,
        (1,),
        [whole(v.shape) for v in (*parts, small)],
        whole(shape),
        jax.ShapeDtypeStruct(shape, BF16),
        [],
        0,
        0,
        "copies",
    )(scal, *parts, small)


def choose_body(scal, *refs, n_seq, count):
    inner = (scal[1] > 0) & (scal[1] < n_seq - 1)
    for k in range(count):

        @pl.when(pl.program_id(0) == k)
        def _(k=k):
            own, other = refs[k][...].astype(F32), refs[count + k][...].astype(F32)
            value = jnp.where(inner, own, other)
            at = 0
            for out in refs[2 * count :]:
                out[...] = value[:, at : at + out.shape[1]]
                at += out.shape[1]


def choose(scal, owns, others, n_seq, widths):
    count = len(owns)
    rows = owns[0].shape[0]
    return call(
        functools.partial(choose_body, n_seq=n_seq, count=count),
        (count,),
        [whole(v.shape) for v in (*owns, *others)],
        [pl.BlockSpec((rows, w), lambda n, s: (n, 0)) for w in widths],
        [jax.ShapeDtypeStruct((rows * count, w), F32) for w in widths],
        [],
        0,
        0,
        "choose",
    )(scal, *owns, *others)


def inward(value, n_seq):
    last = n_seq - 1
    return lax.ppermute(value, "seq", [(0, 1), (last, last - 1)])


def across(value):
    return lax.ppermute(value, "seq", [(1, 2), (2, 1)])


def outward(value, n_seq):
    last = n_seq - 1
    return lax.ppermute(value, "seq", [(1, 0), (last - 1, last)])


def join_body(scal, parts, out, small):
    count = parts.shape[0]
    width = parts.shape[2] // 3
    rows, lane = out.shape[0], small.shape[1]
    total = 0.0
    for t in range(count):
        for j in range(3):
            at = (j * count + t) * width
            out[:, at : at + width] = parts[t, :rows, j * width : (j + 1) * width].astype(F32)
        for j in range(2):
            total += parts[t, rows:, j * lane : (j + 1) * lane].astype(F32)
    small[...] = total


def join(scal, parts, rows, lane):
    count, tall, wide = parts.shape
    shapes = (rows, wide * count), (tall - rows, lane)
    return call(
        join_body,
        (1,),
        [whole(parts.shape)],
        [whole(v) for v in shapes],
        [jax.ShapeDtypeStruct(v, F32) for v in shapes],
        [],
        0,
        0,
        "join",
    )(scal, parts)


def scatter_whole(theirs, mine):
    full = jnp.stack([jnp.stack(mine), theirs], axis=1)
    full = full.reshape(PIECES * full.shape[2], full.shape[3])
    return lax.psum_scatter(full.astype(F32), "fsdp", scatter_dimension=0, tiled=True)


def swap_seq(value, bits, n_seq):
    if bits == 0:
        return value
    return lax.ppermute(value, "seq", [(i, i ^ bits) for i in range(n_seq)])


def hop(pair, t, n_seq):
    up = lax.ppermute(pair[0], "seq", [(i, i + 1) for i in range(t - 1, n_seq - 1)])
    down = lax.ppermute(pair[1], "seq", [(i + 1, i) for i in range(0, n_seq - t)])
    return up, down


def pick(hops, s, place, n_seq, gate):
    used = sorted({abs((p ^ s) - p) for p in range(n_seq)})
    hops = dict(zip(used, after([hops[d - 1] for d in used], gate)))
    value = None
    for p in range(n_seq):
        distance = (p ^ s) - p
        case = hops[abs(distance)][1 if distance > 0 else 0]
        value = case if value is None else jnp.where(place == p, case, value)
    return value


def exchange(value):
    return lax.all_to_all(value, "seq", 0, 0, tiled=True)


def on_device(
    n_fsdp,
    n_seq,
    tokens,
    counts,
    norm1_gain,
    norm1_shift,
    qkv_weight,
    query_bias,
    value_bias,
    out_weight,
    out_bias,
    norm2_gain,
    norm2_shift,
    fc1_weight,
    fc1_bias,
    fc2_weight,
    fc2_bias,
    cotangent,
):
    images, local_len, features = tokens.shape
    unit = -(-local_len // 8) * 8
    group = features // n_seq
    shard = lax.axis_index("fsdp")
    place = lax.axis_index("seq")
    cross = n_fsdp == PIECES
    odd = (shard & 1) == 1
    me = shard if cross else jnp.zeros_like(shard)
    scal = jnp.concatenate([jnp.stack([me, place]).astype(jnp.int32), counts])
    send = lambda arrays: [swap_seq(a, t, n_seq) for t, a in enumerate(arrays)]

    def flat(v):
        v = jnp.pad(v, ((0, 0), (0, unit - local_len), (0, 0)))
        return v.reshape(images * unit, features)

    vectors = (
        norm1_gain,
        norm1_shift,
        query_bias,
        value_bias,
        out_bias,
        norm2_gain,
        norm2_shift,
        fc2_bias,
        fc1_bias,
    )

    gather = lambda v: lax.all_gather(v, "fsdp", axis=0, tiled=True)
    hops = [hop((tokens, tokens), 1, n_seq)]
    for t in range(2, n_seq):
        hops.append(hop(hops[-1], t, n_seq))
    lane = vectors[0].shape[0]
    packed = jnp.concatenate([v.reshape(-1, lane) for v in vectors], axis=0)
    if cross:
        count = packed.shape[0]
        extra = jnp.pad(packed, ((0, -count % 16), (0, qkv_weight.shape[1] - lane)))
        qkv_shard = jnp.concatenate([qkv_weight, extra], axis=0)
        near_q = (flip(qkv_shard, 2), flip(qkv_shard, 4))
        far_q = spread_far(near_q, odd, hops[0])
        near_q = (*near_q, flip(after(qkv_shard, near_q), 1))
        qkv_pieces = spread_rest(
            qkv_shard, near_q, far_q, hops[1], hops[1]
        )
        fc2_full = gather(after(fc2_weight, near_q[:2], hops[0]))
        full = unpack(
            scal, qkv_pieces, qkv_weight.shape[0], [v.shape[0] * PIECES for v in vectors]
        )
    else:
        qkv_pieces = gather_whole(qkv_weight)
        out_pieces = gather_whole(out_weight)
        fc2_full = gather(fc2_weight)
        held = lax.all_gather(packed, "fsdp", axis=0).astype(F32)
        full, at = [], 0
        for v in vectors:
            size = v.shape[0] // lane
            full.append(held[:, at : at + size].reshape(1, -1))
            at += size
    fc1_full = gather(fc1_weight)
    gain1, shift1, bias_q, bias_v, bias_o, gain2, shift2, bias_2, bias_1 = full

    spot = jnp.arange(n_seq * unit)
    inside = spot % unit
    position = ((spot // unit) ^ place) * local_len + inside
    mask = jnp.where(position[None] < counts[:, None], 0.0, MASKED)
    mask = jnp.where(inside[None] < local_len, mask, 2 * MASKED).astype(F32)[:, None]

    x = flat(tokens)
    dy = flat(cotangent)
    projected, normed = [], []
    for s in range(n_seq):
        entry = flat(pick(hops, s, place, n_seq, projected[: s - 1])) if s else x
        entry = after(entry, projected[-1:], hops[1])
        out, h = project(
            scal, entry, gain1, shift1, bias_q, bias_v, qkv_pieces, n_seq, s, unit
        )
        projected.append(out)
        normed.append(h)
    contexts, lse = attend(scal, projected, mask, unit, images)
    ready = ()
    if cross:
        near_o = spread_near(after(out_weight, projected[2]))
        far_o = spread_far(near_o, odd, lse)
        ready = near_o
    contexts = exchange(after(contexts, ready))
    grad_active = narrow_back(scal, after(dy, lse, ready), fc2_full)
    if cross:
        out_pieces = spread_rest(out_weight, near_o, far_o, lse, grad_active)
    context, mixed, normed_two = mix(
        scal,
        contexts,
        after(x, grad_active),
        bias_o,
        gain2,
        shift2,
        out_pieces,
        unit,
    )
    active, grad_hidden = widen(scal, normed_two, bias_1, grad_active, fc1_full)

    swap = (lambda v: flip(v, 1)) if cross else jnp.zeros_like
    theirs_2 = outer_rows(scal, active, dy, 1)
    other_2 = swap(theirs_2)
    dmixed, dbranch, sums2, fc1_bias_sum = widen_back(
        scal, after(grad_hidden, theirs_2), mixed, dy, gain2, fc1_full, unit
    )
    pair_left = (normed_two, context)
    pair_right = (grad_hidden, dbranch)
    theirs_1 = outer_two(scal, after(pair_left, dmixed, other_2), pair_right, 1)
    other_1 = swap(theirs_1)
    grads = mix_back(scal, after(dbranch, theirs_1), out_pieces, n_seq, unit)
    arrived = exchange(grads)
    mine_2 = outer_rows(scal, after(active, grads), dy, 0, other_2)
    passed_2 = flip_mixed(mine_2[3]) if cross else mine_2[3]
    mine_1 = outer_two(scal, after(pair_left, mine_2), pair_right, 0, other_1)
    passed_1 = flip_mixed(mine_1[3]) if cross else mine_1[3]
    back = attend_back(
        scal, projected, after(arrived, mine_1), mask, lse, unit, images
    )
    if cross:
        pair_2 = sides(scal, mine_2, after(passed_2, back))
        fc2_terms = (mine_2[0], *move_sides(pair_2))
    else:
        pair_2 = ()
        fc2_terms = (scatter_whole(theirs_2, mine_2),)
    returned = exchange(after(back, pair_2, passed_1))
    theirs_q, heads_sum = outer(
        scal, normed, after(back, pair_2), 1, group, None, "qkv"
    )
    other_q = swap(theirs_q)
    if cross:
        pair_1 = sides(scal, mine_1, after(passed_1, theirs_q))
        fc1_terms = (mine_1[0], *move_sides(pair_1))
    else:
        pair_1 = ()
        fc1_terms = (scatter_whole(theirs_1, mine_1),)
    output = narrow(
        scal,
        after(active, pair_1, theirs_q),
        mixed,
        bias_2,
        fc2_full,
        unit,
        local_len,
    )
    fc2_own = total(scal, after(fc2_terms, output, other_q))
    fc2_in = inward(fc2_own, n_seq)
    mine_q = outer(
        scal, after(normed, fc2_own), back, 0, group, other_q, "qkv"
    )
    passed_q = flip_mixed(mine_q[3]) if cross else mine_q[3]
    halves = range(2)
    fc1_terms = after(fc1_terms, mine_q)
    fc1_own = [total(scal, fc1_terms, k) for k in halves]
    fc1_in = [inward(v, n_seq) for v in fc1_own]
    input_grad, sums1 = project_back(
        scal,
        returned,
        x,
        after(dmixed, fc1_own),
        gain1,
        qkv_pieces,
        unit,
        local_len,
    )

    if cross:
        pair_q = sides(scal, mine_q, after(passed_q, input_grad))
        qkv_terms = (mine_q[0], *move_sides(pair_q))
    else:
        pair_q = ()
        qkv_terms = (scatter_whole(theirs_q, mine_q),)
    fc2_pair = total(
        scal, (*fc2_terms, after(fc2_in, input_grad, fc1_in[0], pair_q))
    )
    fc2_across = across(fc2_pair)
    fc1_pair = [total(scal, (*fc1_terms, after(fc1_in[0], fc2_pair)), 0)]
    fc1_pair += [total(scal, (*fc1_terms, after(fc1_in[1], fc1_pair)), 1)]
    fc1_across = [across(v) for v in fc1_pair]
    heads_sum = heads_sum.reshape(3, group)
    spread = lambda v: lax.dynamic_update_slice_in_dim(
        jnp.zeros((features,), F32), v, place * group, axis=0
    )
    sums = (
        sums1[0],
        sums1[1],
        spread(heads_sum[0]),
        spread(heads_sum[2]),
        sums2[2],
        sums2[0],
        sums2[1],
        sums2[3],
        fc1_bias_sum[0],
    )
    small = jnp.concatenate([v.reshape(n_fsdp, -1, lane) for v in sums], axis=1)
    if cross:
        for bit in (1, 2, 4):
            small = small + flip(small, bit)
        small = lax.dynamic_index_in_dim(small, shard, 0, False)
    else:
        small = jnp.sum(lax.all_to_all(small, "fsdp", 0, 0, tiled=True), axis=0)
    small = jnp.pad(small, ((0, -small.shape[0] % 16), (0, 0)))
    low = copies(scal, after(qkv_terms, fc1_pair), small, n_seq)
    shared = exchange(low)
    fc2_done = total(scal, (fc2_pair, after(fc2_across, low)))
    fc2_out = outward(fc2_done, n_seq)
    fc1_done = [total(scal, (fc1_pair[0], after(fc1_across[0], fc2_done)))]
    (fc2_weight_grad,) = choose(
        scal, (fc2_done,), (after(fc2_out, fc1_done),), n_seq, (features,)
    )
    fc1_done += [total(scal, (fc1_pair[1], after(fc1_across[1], fc2_weight_grad)))]
    fc1_out = [outward(v, n_seq) for v in fc1_done]
    qkv_weight_grad, small = join(
        scal, after(shared, fc1_done), qkv_weight.shape[0], lane
    )
    fc1_weight_grad, out_weight_grad = choose(
        scal,
        fc1_done,
        after(fc1_out, qkv_weight_grad),
        n_seq,
        (fc1_weight.shape[1], features),
    )
    shares, at = [], 0
    for v in vectors:
        size = v.shape[0] // lane
        shares.append(small[at : at + size].reshape(-1))
        at += size
    g1, s1, qb, vb, ob, g2, s2, b2, b1 = shares
    return (
        output,
        input_grad,
        g1,
        s1,
        qkv_weight_grad,
        qb,
        vb,
        out_weight_grad,
        ob,
        g2,
        s2,
        fc1_weight_grad,
        b1,
        fc2_weight_grad,
        b2,
    )


def solution(mesh):
    rows, vector, matrix = P("fsdp", "seq", None), P("fsdp"), P("fsdp", None)
    return jax.shard_map(
        functools.partial(on_device, mesh.shape["fsdp"], mesh.shape["seq"]),
        mesh=mesh,
        in_specs=(
            rows,
            vector,
            vector,
            vector,
            matrix,
            vector,
            vector,
            matrix,
            vector,
            vector,
            vector,
            matrix,
            vector,
            matrix,
            vector,
            rows,
        ),
        out_specs=(
            rows,
            rows,
            vector,
            vector,
            matrix,
            vector,
            vector,
            matrix,
            vector,
            vector,
            vector,
            matrix,
            vector,
            matrix,
            vector,
        ),
        check_vma=False,
    )
```

```python
import functools

import jax
import jax.numpy as jnp
from jax import lax
from jax.experimental import pallas as pl
from jax.experimental.pallas import tpu as pltpu
from jax.sharding import PartitionSpec as P

HEAD_DIM = 64
EPS = 1e-05
MASKED = -1e30
SCALE = HEAD_DIM ** (-0.5)
F32 = jnp.float32
BF16 = jnp.bfloat16
PIECES = 8
HINT = 64
COVER = 1 << 27
LONG = ("attend_back",)
LIMIT = 62 * 1024 * 1024


def call(body, grid, in_specs, out_specs, out_shape, scratch, flops, moved, name):
    return pl.pallas_call(
        body,
        grid_spec=pltpu.PrefetchScalarGridSpec(
            num_scalar_prefetch=1,
            grid=grid,
            in_specs=in_specs,
            out_specs=out_specs,
            scratch_shapes=scratch,
        ),
        out_shape=out_shape,
        compiler_params=pltpu.CompilerParams(
            dimension_semantics=("arbitrary",) * len(grid), vmem_limit_bytes=LIMIT
        ),
        cost_estimate=pl.CostEstimate(
            flops=0,
            bytes_accessed=COVER if name in LONG else moved // HINT,
            transcendentals=0,
        ),
        name=name,
    )


def whole(shape):
    return pl.BlockSpec(shape, lambda *_: (0,) * len(shape))


def dot_nn(left, right):
    return lax.dot_general(left, right, (((1,), (0,)), ((), ())), preferred_element_type=F32)


def dot_nt(left, right):
    return lax.dot_general(left, right, (((1,), (1,)), ((), ())), preferred_element_type=F32)


def dot_tn(left, right):
    return lax.dot_general(left, right, (((0,), (0,)), ((), ())), preferred_element_type=F32)


def lanes(ref, block, width):
    return ref[:, pl.ds(pl.multiple_of(block * width, 128), width)]


def put_lanes(ref, block, width, value):
    ref[:, pl.ds(pl.multiple_of(block * width, 128), width)] = value


def reorder(into, source, count, where):
    width = into.shape[1] // count

    @pl.loop(0, count)
    def _(r):
        put_lanes(into, r, width, lanes(source, where(r), width))


def stats(values):
    average = jnp.mean(values, axis=-1, keepdims=True)
    centered = values - average
    inverse = lax.rsqrt(jnp.mean(centered * centered, axis=-1, keepdims=True) + EPS)
    return centered * inverse, inverse


def stacked(refs, rows=None):
    return jnp.concatenate([r[...] if rows is None else r[:rows, :] for r in refs], axis=0)


def project_body(scal, *refs, rows, unit):
    x, gain, shift, bias_q, bias_v = refs[:5]
    weights = refs[5:13]
    out, normed, rel = refs[13:]
    step = pl.program_id(0)

    @pl.when(pl.program_id(0) == 0)
    def _():
        @pl.loop(0, rows // unit)
        def _(b):
            span = pl.ds(pl.multiple_of(b * unit, 8), unit)
            normal, _ = stats(x[span, :].astype(F32))
            normed[span, :] = (normal * gain[...] + shift[...]).astype(BF16)

        reorder(rel, normed, PIECES, lambda r: scal[0] ^ r)

    value = dot_nn(rel[...], stacked(weights, rel.shape[1] // PIECES))
    bias = jnp.where(step == 0, bias_q[...], jnp.where(step == 2, bias_v[...], 0.0))
    out[...] = (value + bias).astype(BF16)


def project(scal, x, gain, shift, bias_q, bias_v, pieces, n_seq, slot, unit):
    rows, features = x.shape
    group = features // n_seq
    depth = pieces[0].shape[0]
    return call(
        functools.partial(project_body, rows=rows, unit=unit),
        (3,),
        [whole((rows, features))]
        + [whole((1, features))] * 2
        + [pl.BlockSpec((1, group), lambda j, s: (0, s[1]))] * 2
        + [pl.BlockSpec((depth, group), lambda j, s: (0, n_seq * j + s[1]))] * PIECES,
        [pl.BlockSpec((rows, group), lambda j, s: (0, j)), whole((rows, features))],
        [
            jax.ShapeDtypeStruct((rows, 3 * group), BF16),
            jax.ShapeDtypeStruct((rows, features), BF16),
        ],
        [pltpu.VMEM((rows, features), BF16)],
        2 * rows * features * 3 * group,
        4 * rows * features + 6 * features * group,
        "project",
    )(scal, x, gain, shift, bias_q, bias_v, *pieces)


def unpack_body(scal, *refs):
    pieces, outs = refs[:PIECES], refs[PIECES:]
    for r, piece in enumerate(pieces):
        row = 0
        for out in outs:
            count = out.shape[1] // (PIECES * piece.shape[1])
            for k in range(count):
                put_lanes(
                    out,
                    (scal[0] ^ r) * count + k,
                    piece.shape[1],
                    piece[row : row + 1, :].astype(F32),
                )
                row += 1


def unpack(scal, pieces, start, sizes):
    outs = [jax.ShapeDtypeStruct((1, size), F32) for size in sizes]
    return call(
        unpack_body,
        (1,),
        [pl.BlockSpec((16, 128), lambda n, s: (start // 16, 0))] * PIECES,
        [whole(o.shape) for o in outs],
        outs,
        [],
        0,
        0,
        "unpack",
    )(scal, *pieces)


def half_masks(unit):
    lane = lax.broadcasted_iota(jnp.int32, (unit, 2 * HEAD_DIM), 1)
    return lane < HEAD_DIM


def split_heads(value, low):
    zero = jnp.zeros_like(value)
    return jnp.concatenate([jnp.where(low, value, zero), jnp.where(low, zero, value)], axis=0)


def join_heads(value, low, unit):
    return jnp.where(low, value[:unit], value[unit:])


def attend_body(scal, *refs, n_seq, unit):
    queries, keys, values = refs[:n_seq], refs[n_seq : 2 * n_seq], refs[2 * n_seq : 3 * n_seq]
    mask, out, lse = refs[3 * n_seq :]
    low = half_masks(unit)
    key = stacked(keys)
    value = stacked(values)
    for s in range(n_seq):
        scores = dot_nt(split_heads(queries[s][...], low), key) * SCALE + mask[0]
        top = jnp.max(scores, axis=-1, keepdims=True)
        weight = jnp.exp(scores - top)
        total = jnp.sum(weight, axis=-1, keepdims=True)
        probs = (weight * (1.0 / total)).astype(BF16)
        out[scal[1] ^ s] = join_heads(dot_nn(probs, value), low, unit).astype(BF16)
        log_total = top + jnp.log(total)
        lse[0, 0, s * unit : (s + 1) * unit, :] = jnp.where(
            low, log_total[:unit], log_total[unit:]
        )


def qkv_specs(n_seq, unit, pairs):
    specs = []
    for j in range(3):
        specs += [
            pl.BlockSpec((unit, 2 * HEAD_DIM), lambda b, p, s, j=j: (b, pairs * j + p))
        ] * n_seq
    return specs


def attend(scal, projected, mask, unit, images):
    n_seq = len(projected)
    rows, wide = projected[0].shape
    group = wide // 3
    pairs = group // (2 * HEAD_DIM)
    tokens = n_seq * unit
    return call(
        functools.partial(attend_body, n_seq=n_seq, unit=unit),
        (images, pairs),
        qkv_specs(n_seq, unit, pairs) + [pl.BlockSpec((1, 1, tokens), lambda b, p, s: (b, 0, 0))],
        [
            pl.BlockSpec((n_seq, unit, 2 * HEAD_DIM), lambda b, p, s: (0, b, p)),
            pl.BlockSpec((1, 1, tokens, 2 * HEAD_DIM), lambda b, p, s: (b, p, 0, 0)),
        ],
        [
            jax.ShapeDtypeStruct((n_seq, rows, group), BF16),
            jax.ShapeDtypeStruct((images, pairs, tokens, 2 * HEAD_DIM), F32),
        ],
        [],
        images * pairs * 2 * tokens * tokens * 2 * HEAD_DIM * 4,
        n_seq * rows * wide * 4,
        "attend",
    )(scal, *projected, *projected, *projected, mask)


def put_slot(ref, slot, block, value):
    width = value.shape[1]
    ref[slot, :, pl.ds(pl.multiple_of(block * width, 128), width)] = value


def attend_back_body(scal, *refs, n_seq, unit, pairs):
    queries, keys, values = refs[:n_seq], refs[n_seq : 2 * n_seq], refs[2 * n_seq : 3 * n_seq]
    grads, mask, lse, out, key_acc, value_acc, held = refs[3 * n_seq :]
    pair = pl.program_id(1)
    low = half_masks(unit)
    key = stacked(keys)
    value = stacked(values)
    for s in range(n_seq):
        held[s] = queries[s][...]
    key_acc[...] = jnp.zeros_like(key_acc)
    value_acc[...] = jnp.zeros_like(value_acc)

    def one(s):
        query = split_heads(held[s], low)
        slot = scal[1] ^ s
        grad = split_heads(grads[slot], low)
        scores = dot_nt(query, key) * SCALE + mask[0]
        saved = lse[0, 0, pl.ds(pl.multiple_of(s * unit, 8), unit), :]
        column = jnp.concatenate([saved[:, :1], saved[:, HEAD_DIM : HEAD_DIM + 1]], axis=0)
        probs = jnp.exp(scores - column)
        grad_probs = dot_nt(grad, value)
        value_part = dot_tn(probs.astype(BF16), grad)
        center = jnp.sum(grad_probs * probs, axis=-1, keepdims=True)
        grad_scores = (probs * (grad_probs - center)).astype(BF16)
        query_grad = join_heads(dot_nn(grad_scores, key), low, unit) * SCALE
        key_part = dot_tn(grad_scores, query)
        put_slot(out, slot, pair, query_grad.astype(BF16))
        return key_part, value_part

    @pl.loop(0, n_seq, step=2)
    def _(s):
        first, second = one(s), one(s + 1)
        key_acc[...] += first[0] + second[0]
        value_acc[...] += first[1] + second[1]

    for s in range(n_seq):
        span = pl.ds(s * unit, unit)
        slot = scal[1] ^ s
        put_slot(out, slot, pairs + pair, (key_acc[span, :] * SCALE).astype(BF16))
        put_slot(out, slot, 2 * pairs + pair, value_acc[span, :].astype(BF16))


def attend_back(scal, projected, grads, mask, lse, unit, images):
    n_seq = len(projected)
    rows, wide = projected[0].shape
    group = wide // 3
    pairs = group // (2 * HEAD_DIM)
    tokens = n_seq * unit
    return call(
        functools.partial(attend_back_body, n_seq=n_seq, unit=unit, pairs=pairs),
        (images, pairs),
        qkv_specs(n_seq, unit, pairs)
        + [
            pl.BlockSpec((n_seq, unit, 2 * HEAD_DIM), lambda b, p, s: (0, b, p)),
            pl.BlockSpec((1, 1, tokens), lambda b, p, s: (b, 0, 0)),
            pl.BlockSpec((1, 1, tokens, 2 * HEAD_DIM), lambda b, p, s: (b, p, 0, 0)),
        ],
        pl.BlockSpec((n_seq, unit, wide), lambda b, p, s: (0, b, 0)),
        jax.ShapeDtypeStruct((n_seq, rows, wide), BF16),
        [pltpu.VMEM((tokens, 2 * HEAD_DIM), F32)] * 2
        + [pltpu.VMEM((n_seq, unit, 2 * HEAD_DIM), BF16)],
        images * pairs * 2 * tokens * tokens * 2 * HEAD_DIM * 10,
        n_seq * rows * wide * 4,
        "attend_back",
    )(scal, *projected, *projected, *projected, grads, mask, lse)


def mix_body(scal, *refs, n_seq):
    contexts, x, bias, gain, shift = refs[:5]
    weights = refs[5:13]
    context, mixed, normed, rel = refs[13:]
    group = contexts.shape[2]

    @pl.loop(0, n_seq)
    def _(t):
        put_lanes(context, t, group, contexts[t])

    reorder(rel, context, PIECES, lambda r: scal[0] ^ r)
    branch = dot_nn(rel[...], stacked(weights)) + bias[...]
    flag = (scal[2 + pl.program_id(0)] > 0).astype(F32)
    value = x[...].astype(F32) + branch * flag
    mixed[...] = value
    normal, _ = stats(value)
    normed[...] = (normal * gain[...] + shift[...]).astype(BF16)


def mix(scal, contexts, x, bias, gain, shift, pieces, unit):
    n_seq = contexts.shape[0]
    rows, features = x.shape
    group = features // n_seq
    row_block = pl.BlockSpec((unit, features), lambda b, s: (b, 0))
    return call(
        functools.partial(mix_body, n_seq=n_seq),
        (rows // unit,),
        [pl.BlockSpec((n_seq, unit, group), lambda b, s: (0, b, 0)), row_block]
        + [whole((1, features))] * 3
        + [whole(pieces[0].shape)] * PIECES,
        [row_block] * 3,
        [
            jax.ShapeDtypeStruct((rows, features), BF16),
            jax.ShapeDtypeStruct((rows, features), F32),
            jax.ShapeDtypeStruct((rows, features), BF16),
        ],
        [pltpu.VMEM((unit, features), BF16)],
        2 * rows * features * features,
        12 * rows * features + 2 * features * features,
        "mix",
    )(scal, contexts, x, bias, gain, shift, *pieces)


def widen_body(scal, x, bias, grad, weight, active, grad_hidden):
    hidden = dot_nn(x[...], weight[...]) + bias[...]
    gate = jax.nn.sigmoid(1.702 * hidden)
    product = hidden * gate
    active[...] = product.astype(BF16)
    slope = gate + 1.702 * product * (1.0 - gate)
    grad_hidden[...] = (grad[...].astype(F32) * slope).astype(BF16)


def widen(scal, x, bias, grad, weight, tile=512):
    rows, features = x.shape
    hidden = weight.shape[1]
    column = pl.BlockSpec((rows, tile), lambda n, s: (0, n))
    return call(
        widen_body,
        (hidden // tile,),
        [
            whole((rows, features)),
            pl.BlockSpec((1, tile), lambda n, s: (0, n)),
            column,
            pl.BlockSpec((features, tile), lambda n, s: (0, n)),
        ],
        [column] * 2,
        [jax.ShapeDtypeStruct((rows, hidden), BF16)] * 2,
        [],
        2 * rows * features * hidden,
        2 * features * hidden + 6 * rows * hidden,
        "widen",
    )(scal, x, bias, grad, weight)


def narrow_body(scal, x, mixed, bias, weight, out, held, *, unit, keep):
    held[...] = dot_nn(x[...], weight[...]) + mixed[...] + bias[...]

    @pl.loop(0, out.shape[0])
    def _(b):
        span = pl.ds(pl.multiple_of(b * unit, 8), unit)
        out[b] = held[span, :][:keep].astype(BF16)


def narrow(scal, x, mixed, bias, weight, unit, keep, tile=256):
    rows, hidden = x.shape
    features = weight.shape[1]
    images = rows // unit
    column = lambda depth: pl.BlockSpec((depth, tile), lambda n, s: (0, n))
    return call(
        functools.partial(narrow_body, unit=unit, keep=keep),
        (features // tile,),
        [whole((rows, hidden)), column(rows), column(1), column(hidden)],
        pl.BlockSpec((images, keep, tile), lambda n, s: (0, 0, n)),
        jax.ShapeDtypeStruct((images, keep, features), BF16),
        [pltpu.VMEM((rows, tile), F32)],
        2 * rows * features * hidden,
        2 * features * hidden + 2 * rows * hidden + 6 * rows * features,
        "narrow",
    )(scal, x, mixed, bias, weight)


def outer_rows_body(scal, left, right, *refs):
    value = dot_tn(left[...], right[...])
    if len(refs) == 1:
        refs[0][0] = value.astype(BF16)
        return
    held = refs[-1]
    held[...] = (value + refs[0][0].astype(F32)).astype(BF16)
    part = held.shape[0] // 8
    for m, out in enumerate(refs[1:-1]):

        @pl.when(pl.program_id(0) == m)
        def _(out=out):
            @pl.loop(0, 8)
            def _(i):
                span = pl.ds(pl.multiple_of(i * part, 16), part)
                out[span, :] = held[span, :]


def outer_rows(scal, left, right, offset, added=None):
    rows, hidden = left.shape
    width = hidden // PIECES
    features = right.shape[1]
    block = pl.BlockSpec((1, width, features), lambda m, s: (m, 0, 0))
    half = PIECES // 2
    own = added is not None
    return call(
        outer_rows_body,
        (half,),
        [
            pl.BlockSpec((rows, width), lambda m, s: (0, s[0] ^ (2 * m + offset))),
            whole((rows, features)),
        ]
        + ([block] if own else []),
        [whole((width, features))] * half if own else block,
        [jax.ShapeDtypeStruct((width, features), BF16)] * half
        if own
        else jax.ShapeDtypeStruct((half, width, features), BF16),
        [pltpu.VMEM((width, features), BF16)] if own else [],
        rows * hidden * features,
        hidden * features * (2 if own else 1),
        f"outer_rows{offset}",
    )(scal, left, right, *((added,) if own else ()))


def outer_body(scal, *refs, count, offset, width):
    lefts, right = refs[:count], refs[count]
    rel, acc = refs[-2:]
    half = PIECES // 2

    @pl.when(pl.program_id(0) == 0)
    def _():
        for i in range(count):
            reorder(rel.at[i], lefts[i], half, lambda m: scal[0] ^ (2 * m + offset))

    acc[...] = jnp.zeros_like(acc)

    @pl.loop(0, count)
    def _(i):
        acc[...] += dot_tn(rel[i], right[scal[1] ^ i])

    for m in range(half):
        part = acc[m * width : (m + 1) * width, :]
        if offset == 0:
            outs = refs[count + 2 : -2]
            outs[m][...] = (part + refs[count + 1][m].astype(F32)).astype(BF16)
        else:
            refs[count + 1][m] = part.astype(BF16)
    if offset:
        refs[count + 2][...] = sum(rows_sum(right[i].astype(F32)) for i in range(count))


def outer(scal, lefts, right, offset, tile, added=None, name=""):
    count = len(lefts)
    rows, features = lefts[0].shape
    wide = right.shape[2]
    width = features // PIECES
    half = PIECES // 2
    block = pl.BlockSpec((half, width, tile), lambda n, s: (0, 0, n))
    own = added is not None
    return call(
        functools.partial(outer_body, count=count, offset=offset, width=width),
        (wide // tile,),
        [whole((rows, features))] * count
        + [pl.BlockSpec((count, rows, tile), lambda n, s: (0, 0, n))]
        + ([block] if own else []),
        [pl.BlockSpec((width, tile), lambda n, s: (0, n))] * half
        if own
        else [block, pl.BlockSpec((1, tile), lambda n, s: (0, n))],
        [jax.ShapeDtypeStruct((width, wide), BF16)] * half
        if own
        else [
            jax.ShapeDtypeStruct((half, width, wide), BF16),
            jax.ShapeDtypeStruct((1, wide), F32),
        ],
        [
            pltpu.VMEM((count, rows, half * width), BF16),
            pltpu.VMEM((half * width, tile), F32),
        ],
        count * rows * features * wide,
        features * wide * (1 if offset else 2) + count * 2 * rows * (features + wide),
        f"outer_{name}{offset}",
    )(scal, *lefts, right, *(() if added is None else (added,)))


def outer_two_body(scal, *refs, offset, width, first):
    lefts, rights = refs[:2], refs[2:4]
    rels = refs[-2:]
    half = PIECES // 2
    step = pl.program_id(0)

    @pl.when(step == 0)
    def _():
        for left, rel in zip(lefts, rels):
            reorder(rel, left, half, lambda m: scal[0] ^ (2 * m + offset))

    def store(value):
        for m in range(half):
            part = value[m * width : (m + 1) * width]
            if offset == 0:
                refs[5 + m][...] = (part + refs[4][m].astype(F32)).astype(BF16)
            else:
                refs[4][m] = part.astype(BF16)

    @pl.when(step < first)
    def _():
        store(dot_tn(rels[0][...], rights[0][...]))

    @pl.when(step >= first)
    def _():
        store(dot_tn(rels[1][...], rights[1][...]))


def outer_two(scal, lefts, rights, offset, added=None, tile=512):
    rows, features = lefts[0].shape
    first = rights[0].shape[1] // tile
    count = first + rights[1].shape[1] // tile
    wide = count * tile
    width = features // PIECES
    half = PIECES // 2
    block = pl.BlockSpec((half, width, tile), lambda n, s: (0, 0, n))
    own = added is not None
    return call(
        functools.partial(outer_two_body, offset=offset, width=width, first=first),
        (count,),
        [whole((rows, features))] * 2
        + [
            pl.BlockSpec((rows, tile), lambda n, s: (0, jnp.minimum(n, first - 1))),
            pl.BlockSpec((rows, tile), lambda n, s: (0, jnp.maximum(n - first, 0))),
        ]
        + ([block] if own else []),
        [pl.BlockSpec((width, tile), lambda n, s: (0, n))] * half if own else block,
        [jax.ShapeDtypeStruct((width, wide), BF16)] * half
        if own
        else jax.ShapeDtypeStruct((half, width, wide), BF16),
        [pltpu.VMEM((rows, half * width), BF16)] * 2,
        rows * features * wide,
        features * wide * (2 if own else 1),
        f"outer_two{offset}",
    )(scal, *lefts, *rights, *((added,) if own else ()))


def narrow_back_body(scal, grad, weight, out):
    out[...] = dot_nt(grad[...], weight[...]).astype(BF16)


def narrow_back(scal, grad, weight, tile=512):
    rows, features = grad.shape
    hidden = weight.shape[0]
    return call(
        narrow_back_body,
        (hidden // tile,),
        [whole((rows, features)), pl.BlockSpec((tile, features), lambda n, s: (n, 0))],
        pl.BlockSpec((rows, tile), lambda n, s: (0, n)),
        jax.ShapeDtypeStruct((rows, hidden), BF16),
        [],
        2 * rows * features * hidden,
        2 * features * hidden + 2 * rows * hidden,
        "narrow_back",
    )(scal, grad, weight)


def norm_back(grad, normal, inverse, gain):
    scaled = grad * gain
    return inverse * (
        scaled
        - jnp.mean(scaled, axis=-1, keepdims=True)
        - normal * jnp.mean(scaled * normal, axis=-1, keepdims=True)
    )


def clear(ref, unit, condition):
    @pl.when(condition)
    def _():
        @pl.loop(0, ref.shape[0] // unit)
        def _(b):
            span = pl.ds(pl.multiple_of(b * unit, 8), unit)
            ref[span, :] = jnp.zeros((unit, ref.shape[1]), ref.dtype)


def rows_sum(value):
    return jnp.sum(value, axis=0, keepdims=True)


def widen_back_body(scal, *refs, unit):
    grad, mixed, dy, gain, weight = refs[:5]
    dmixed, dbranch, sums, bias_sum, acc = refs[5:]
    step = pl.program_id(0)
    value = grad[...]
    bias_sum[...] = rows_sum(value.astype(F32))
    clear(acc, unit, step == 0)
    part = dot_nt(value, weight[...])

    acc[...] += part

    @pl.when(step == pl.num_programs(0) - 1)
    def _():
        def image(b, totals):
            span = pl.ds(pl.multiple_of(b * unit, 8), unit)
            normal, inverse = stats(mixed[span, :])
            grad_out = dy[span, :].astype(F32)
            back = acc[span, :]
            total = grad_out + norm_back(back, normal, inverse, gain[...])
            dmixed[span, :] = total
            flag = (scal[2 + b] > 0).astype(F32)
            low = (total * flag).astype(BF16)
            dbranch[span, :] = low
            parts = (back * normal, back, low.astype(F32), grad_out)
            return tuple(t + rows_sum(p) for t, p in zip(totals, parts))

        none = jnp.zeros((1, acc.shape[1]), F32)
        totals = lax.fori_loop(0, acc.shape[0] // unit, image, (none,) * 4)
        sums[...] = jnp.concatenate(list(totals) + [none] * 4, axis=0)


def widen_back(scal, grad, mixed, dy, gain, weight, unit, tile=1024):
    rows, hidden = grad.shape
    features = mixed.shape[1]
    full = whole((rows, features))
    return call(
        functools.partial(widen_back_body, unit=unit),
        (hidden // tile,),
        [
            pl.BlockSpec((rows, tile), lambda n, s: (0, n)),
            full,
            full,
            whole((1, features)),
            pl.BlockSpec((features, tile), lambda n, s: (0, n)),
        ],
        [
            full,
            full,
            whole((8, features)),
            pl.BlockSpec((1, tile), lambda n, s: (0, n)),
        ],
        [
            jax.ShapeDtypeStruct((rows, features), F32),
            jax.ShapeDtypeStruct((rows, features), BF16),
            jax.ShapeDtypeStruct((8, features), F32),
            jax.ShapeDtypeStruct((1, hidden), F32),
        ],
        [pltpu.VMEM((rows, features), F32)],
        2 * rows * features * hidden,
        2 * features * hidden + 2 * rows * hidden + 12 * rows * features,
        "widen_back",
    )(scal, grad, mixed, dy, gain, weight)


def mix_back_body(scal, *refs, n_seq):
    grad = refs[0]
    weights = refs[1:9]
    out, rel = refs[9:]
    rel[...] = dot_nt(grad[...], stacked(weights)).astype(BF16)
    width = rel.shape[1] // PIECES
    per = PIECES // n_seq

    @pl.loop(0, n_seq)
    def _(t):
        for k in range(per):
            out[t, :, k * width : (k + 1) * width] = lanes(
                rel, scal[0] ^ (t * per + k), width
            )


def mix_back(scal, grad, pieces, n_seq, unit):
    rows, features = grad.shape
    group = features // n_seq
    return call(
        functools.partial(mix_back_body, n_seq=n_seq),
        (rows // unit,),
        [pl.BlockSpec((unit, features), lambda b, s: (b, 0))] + [whole(pieces[0].shape)] * PIECES,
        pl.BlockSpec((n_seq, unit, group), lambda b, s: (0, b, 0)),
        jax.ShapeDtypeStruct((n_seq, rows, group), BF16),
        [pltpu.VMEM((unit, features), BF16)],
        2 * rows * features * features,
        4 * rows * features + 2 * features * features,
        "mix_back",
    )(scal, grad, *pieces)


def project_back_body(scal, *refs, n_seq, unit, keep):
    grads, x, dmixed, gain = refs[:4]
    weights = refs[4:12]
    out, sums, acc, nat, wide = refs[12:]
    step = pl.program_id(0)
    width = acc.shape[1] // PIECES
    @pl.loop(0, n_seq)
    def _(t):
        put_lanes(wide, t, grads.shape[2], grads[t])

    clear(acc, unit, step == 0)
    part = dot_nt(wide[...], stacked(weights, width))

    acc[...] += part

    @pl.when(step == pl.num_programs(0) - 1)
    def _():
        def image(b, totals):
            span = pl.ds(pl.multiple_of(b * unit, 8), unit)

            @pl.loop(0, PIECES)
            def _(r):
                part = acc[span, pl.ds(pl.multiple_of(r * width, 128), width)]
                put_lanes(nat, scal[0] ^ r, width, part)

            normal, inverse = stats(x[span, :].astype(F32))
            back = nat[...]
            total = dmixed[span, :] + norm_back(back, normal, inverse, gain[...])
            out[b] = total[:keep]
            return tuple(t + rows_sum(p) for t, p in zip(totals, (back * normal, back)))

        none = jnp.zeros((1, acc.shape[1]), F32)
        totals = lax.fori_loop(0, acc.shape[0] // unit, image, (none,) * 2)
        sums[...] = jnp.concatenate(list(totals) + [none] * 6, axis=0)


def project_back(scal, grads, x, dmixed, gain, pieces, unit, keep):
    n_seq = grads.shape[0]
    rows, features = x.shape
    group = features // n_seq
    depth = pieces[0].shape[0]
    images = rows // unit
    full = whole((rows, features))
    return call(
        functools.partial(project_back_body, n_seq=n_seq, unit=unit, keep=keep),
        (3,),
        [
            pl.BlockSpec((n_seq, rows, group), lambda j, s: (0, 0, j)),
            full,
            full,
            whole((1, features)),
        ]
        + [pl.BlockSpec((depth, features), lambda j, s: (0, j))] * PIECES,
        [whole((images, keep, features)), whole((8, features))],
        [
            jax.ShapeDtypeStruct((images, keep, features), F32),
            jax.ShapeDtypeStruct((8, features), F32),
        ],
        [
            pltpu.VMEM((rows, features), F32),
            pltpu.VMEM((unit, features), F32),
            pltpu.VMEM((rows, features), BF16),
        ],
        6 * rows * features * features,
        6 * features * features + 16 * rows * features,
        "project_back",
    )(scal, grads, x, dmixed, gain, *pieces)


def flip(value, bit):
    return lax.ppermute(value, "fsdp", [(i, i ^ bit) for i in range(PIECES)])


def flip_mixed(value):
    return lax.ppermute(
        value, "fsdp", [(i, i ^ (4 if i & 1 else 2)) for i in range(PIECES)]
    )


def after(value, *others):
    return lax.optimization_barrier((value, others))[0]


def spread_near(shard):
    return flip(shard, 2), flip(shard, 4), flip(shard, 1)


def spread_far(near, odd, gate=()):
    return flip_mixed(after(jnp.where(odd, near[0], near[1]), gate))


def spread_rest(shard, near, far, near_gate=(), far_gate=()):
    return [
        shard,
        near[2],
        near[0],
        flip(after(near[0], near_gate), 1),
        near[1],
        flip(after(near[1], near_gate), 1),
        far,
        flip(after(far, far_gate), 1),
    ]


def gather_whole(shard):
    full = lax.all_gather(shard, "fsdp", axis=0, tiled=True)
    size = full.shape[0] // PIECES
    return [full[r * size : (r + 1) * size] for r in range(PIECES)]


def sides_body(scal, right, down, passed, to_x, to_y):
    odd = (scal[0] & 1) == 1
    extra = passed[...].astype(F32)
    none = jnp.zeros_like(extra)
    to_x[...] = (right[...].astype(F32) + jnp.where(odd, extra, none)).astype(BF16)
    to_y[...] = (down[...].astype(F32) + jnp.where(odd, none, extra)).astype(BF16)


def small_call(scal, body, operands, outs, name, steps=1):
    spec = lambda v: pl.BlockSpec((v.shape[0] // steps, v.shape[1]), lambda n, s: (n, 0))
    return call(
        body,
        (steps,),
        [spec(v) for v in operands],
        [spec(o) for o in outs],
        outs,
        [],
        0,
        sum(v.size for v in operands),
        name,
    )(scal, *operands)


def row_steps(value):
    return 2 if value.shape[0] % 64 == 0 else 1


def sides(scal, summed, passed):
    like = jax.ShapeDtypeStruct(passed.shape, BF16)
    return small_call(
        scal,
        sides_body,
        (summed[1], summed[2], passed),
        [like] * 2,
        "sides",
        row_steps(passed),
    )


def move_sides(pair):
    return flip(pair[0], 2), flip(pair[1], 4)


def total_body(scal, *refs):
    total = refs[0][...].astype(F32)
    for value in refs[1:-1]:
        total += value[...].astype(F32)
    refs[-1][...] = total.astype(BF16)


def total(scal, parts, half=None):
    rows, wide = parts[0].shape
    rows = rows if half is None else rows // 2
    steps = max(1, min(2, rows // 32)) if rows % 32 == 0 else 1
    block = (rows // steps, wide)
    specs = [
        pl.BlockSpec(
            block, lambda n, s, at=half * steps if p.shape[0] > rows else 0: (n + at, 0)
        )
        for p in parts
    ]
    return call(
        total_body,
        (steps,),
        specs,
        pl.BlockSpec(block, lambda n, s: (n, 0)),
        jax.ShapeDtypeStruct((rows, wide), BF16),
        [],
        0,
        0,
        "total",
    )(scal, *parts)


def copies_body(scal, *refs):
    out, small = refs[-1], refs[-2][...]
    rows = refs[0].shape[0]
    lane = small.shape[1]
    total = refs[0][...].astype(F32)
    for value in refs[1:-2]:
        total += value[...].astype(F32)
    high = small.astype(BF16)
    rest = (small - high.astype(F32)).astype(BF16)
    for t in range(out.shape[0]):
        out[t, :rows, :] = total.astype(BF16)
        out[t, rows:, :] = jnp.zeros((small.shape[0], total.shape[1]), BF16)
        out[t, rows:, :lane] = high
        out[t, rows:, lane : 2 * lane] = rest


def copies(scal, parts, small, n_seq):
    rows, wide = parts[0].shape
    shape = (n_seq, rows + small.shape[0], wide)
    return call(
        copies_body,
        (1,),
        [whole(v.shape) for v in (*parts, small)],
        whole(shape),
        jax.ShapeDtypeStruct(shape, BF16),
        [],
        0,
        0,
        "copies",
    )(scal, *parts, small)


def choose_body(scal, *refs, n_seq, count):
    inner = (scal[1] > 0) & (scal[1] < n_seq - 1)
    for k in range(count):

        @pl.when(pl.program_id(0) == k)
        def _(k=k):
            own, other = refs[k][...].astype(F32), refs[count + k][...].astype(F32)
            value = jnp.where(inner, own, other)
            at = 0
            for out in refs[2 * count :]:
                out[...] = value[:, at : at + out.shape[1]]
                at += out.shape[1]


def choose(scal, owns, others, n_seq, widths):
    count = len(owns)
    rows = owns[0].shape[0]
    return call(
        functools.partial(choose_body, n_seq=n_seq, count=count),
        (count,),
        [whole(v.shape) for v in (*owns, *others)],
        [pl.BlockSpec((rows, w), lambda n, s: (n, 0)) for w in widths],
        [jax.ShapeDtypeStruct((rows * count, w), F32) for w in widths],
        [],
        0,
        0,
        "choose",
    )(scal, *owns, *others)


def inward(value, n_seq):
    last = n_seq - 1
    return lax.ppermute(value, "seq", [(0, 1), (last, last - 1)])


def across(value):
    return lax.ppermute(value, "seq", [(1, 2), (2, 1)])


def outward(value, n_seq):
    last = n_seq - 1
    return lax.ppermute(value, "seq", [(1, 0), (last - 1, last)])


def join_body(scal, parts, out, small):
    count = parts.shape[0]
    width = parts.shape[2] // 3
    rows, lane = out.shape[0], small.shape[1]
    total = 0.0
    for t in range(count):
        for j in range(3):
            at = (j * count + t) * width
            out[:, at : at + width] = parts[t, :rows, j * width : (j + 1) * width].astype(F32)
        for j in range(2):
            total += parts[t, rows:, j * lane : (j + 1) * lane].astype(F32)
    small[...] = total


def join(scal, parts, rows, lane):
    count, tall, wide = parts.shape
    shapes = (rows, wide * count), (tall - rows, lane)
    return call(
        join_body,
        (1,),
        [whole(parts.shape)],
        [whole(v) for v in shapes],
        [jax.ShapeDtypeStruct(v, F32) for v in shapes],
        [],
        0,
        0,
        "join",
    )(scal, parts)


def scatter_whole(theirs, mine):
    full = jnp.stack([jnp.stack(mine), theirs], axis=1)
    full = full.reshape(PIECES * full.shape[2], full.shape[3])
    return lax.psum_scatter(full.astype(F32), "fsdp", scatter_dimension=0, tiled=True)


def swap_seq(value, bits, n_seq):
    if bits == 0:
        return value
    return lax.ppermute(value, "seq", [(i, i ^ bits) for i in range(n_seq)])


def hop(pair, t, n_seq):
    up = lax.ppermute(pair[0], "seq", [(i, i + 1) for i in range(t - 1, n_seq - 1)])
    down = lax.ppermute(pair[1], "seq", [(i + 1, i) for i in range(0, n_seq - t)])
    return up, down


def pick(hops, s, place, n_seq, gate):
    used = sorted({abs((p ^ s) - p) for p in range(n_seq)})
    hops = dict(zip(used, after([hops[d - 1] for d in used], gate)))
    value = None
    for p in range(n_seq):
        distance = (p ^ s) - p
        case = hops[abs(distance)][1 if distance > 0 else 0]
        value = case if value is None else jnp.where(place == p, case, value)
    return value


def exchange(value):
    return lax.all_to_all(value, "seq", 0, 0, tiled=True)


def on_device(
    n_fsdp,
    n_seq,
    tokens,
    counts,
    norm1_gain,
    norm1_shift,
    qkv_weight,
    query_bias,
    value_bias,
    out_weight,
    out_bias,
    norm2_gain,
    norm2_shift,
    fc1_weight,
    fc1_bias,
    fc2_weight,
    fc2_bias,
    cotangent,
):
    images, local_len, features = tokens.shape
    unit = -(-local_len // 8) * 8
    group = features // n_seq
    shard = lax.axis_index("fsdp")
    place = lax.axis_index("seq")
    cross = n_fsdp == PIECES
    odd = (shard & 1) == 1
    me = shard if cross else jnp.zeros_like(shard)
    scal = jnp.concatenate([jnp.stack([me, place]).astype(jnp.int32), counts])
    send = lambda arrays: [swap_seq(a, t, n_seq) for t, a in enumerate(arrays)]

    def flat(v):
        v = jnp.pad(v, ((0, 0), (0, unit - local_len), (0, 0)))
        return v.reshape(images * unit, features)

    vectors = (
        norm1_gain,
        norm1_shift,
        query_bias,
        value_bias,
        out_bias,
        norm2_gain,
        norm2_shift,
        fc2_bias,
        fc1_bias,
    )

    gather = lambda v: lax.all_gather(v, "fsdp", axis=0, tiled=True)
    hops = [hop((tokens, tokens), 1, n_seq)]
    for t in range(2, n_seq):
        hops.append(hop(hops[-1], t, n_seq))
    lane = vectors[0].shape[0]
    packed = jnp.concatenate([v.reshape(-1, lane) for v in vectors], axis=0)
    if cross:
        count = packed.shape[0]
        extra = jnp.pad(packed, ((0, -count % 16), (0, qkv_weight.shape[1] - lane)))
        qkv_shard = jnp.concatenate([qkv_weight, extra], axis=0)
        near_q = (flip(qkv_shard, 2), flip(qkv_shard, 4))
        far_q = spread_far(near_q, odd, hops[0])
        near_q = (*near_q, flip(after(qkv_shard, near_q), 1))
        qkv_pieces = spread_rest(
            qkv_shard, near_q, far_q, hops[1], hops[1]
        )
        fc2_full = gather(after(fc2_weight, near_q[:2], hops[0]))
        full = unpack(
            scal, qkv_pieces, qkv_weight.shape[0], [v.shape[0] * PIECES for v in vectors]
        )
    else:
        qkv_pieces = gather_whole(qkv_weight)
        out_pieces = gather_whole(out_weight)
        fc2_full = gather(fc2_weight)
        held = lax.all_gather(packed, "fsdp", axis=0).astype(F32)
        full, at = [], 0
        for v in vectors:
            size = v.shape[0] // lane
            full.append(held[:, at : at + size].reshape(1, -1))
            at += size
    fc1_full = gather(fc1_weight)
    gain1, shift1, bias_q, bias_v, bias_o, gain2, shift2, bias_2, bias_1 = full

    spot = jnp.arange(n_seq * unit)
    inside = spot % unit
    position = ((spot // unit) ^ place) * local_len + inside
    mask = jnp.where(position[None] < counts[:, None], 0.0, MASKED)
    mask = jnp.where(inside[None] < local_len, mask, 2 * MASKED).astype(F32)[:, None]

    x = flat(tokens)
    dy = flat(cotangent)
    projected, normed = [], []
    for s in range(n_seq):
        entry = flat(pick(hops, s, place, n_seq, projected[: s - 1])) if s else x
        entry = after(entry, projected[-1:], hops[1])
        out, h = project(
            scal, entry, gain1, shift1, bias_q, bias_v, qkv_pieces, n_seq, s, unit
        )
        projected.append(out)
        normed.append(h)
    contexts, lse = attend(scal, projected, mask, unit, images)
    ready = ()
    if cross:
        near_o = spread_near(after(out_weight, projected[2]))
        far_o = spread_far(near_o, odd, lse)
        ready = near_o
    contexts = exchange(after(contexts, ready))
    grad_active = narrow_back(scal, after(dy, lse, ready), fc2_full)
    if cross:
        out_pieces = spread_rest(out_weight, near_o, far_o, lse, grad_active)
    context, mixed, normed_two = mix(
        scal,
        contexts,
        after(x, grad_active),
        bias_o,
        gain2,
        shift2,
        out_pieces,
        unit,
    )
    active, grad_hidden = widen(scal, normed_two, bias_1, grad_active, fc1_full)

    swap = (lambda v: flip(v, 1)) if cross else jnp.zeros_like
    theirs_2 = outer_rows(scal, active, dy, 1)
    other_2 = swap(theirs_2)
    dmixed, dbranch, sums2, fc1_bias_sum = widen_back(
        scal, after(grad_hidden, theirs_2), mixed, dy, gain2, fc1_full, unit
    )
    pair_left = (normed_two, context)
    pair_right = (grad_hidden, dbranch)
    theirs_1 = outer_two(scal, after(pair_left, dmixed, other_2), pair_right, 1)
    other_1 = swap(theirs_1)
    grads = mix_back(scal, after(dbranch, theirs_1), out_pieces, n_seq, unit)
    arrived = exchange(grads)
    mine_2 = outer_rows(scal, after(active, grads), dy, 0, other_2)
    passed_2 = flip_mixed(mine_2[3]) if cross else mine_2[3]
    mine_1 = outer_two(scal, after(pair_left, mine_2), pair_right, 0, other_1)
    passed_1 = flip_mixed(mine_1[3]) if cross else mine_1[3]
    back = attend_back(
        scal, projected, after(arrived, mine_1), mask, lse, unit, images
    )
    if cross:
        pair_2 = sides(scal, mine_2, after(passed_2, back))
        fc2_terms = (mine_2[0], *move_sides(pair_2))
    else:
        pair_2 = ()
        fc2_terms = (scatter_whole(theirs_2, mine_2),)
    returned = exchange(after(back, pair_2, passed_1))
    theirs_q, heads_sum = outer(
        scal, normed, after(back, pair_2), 1, group, None, "qkv"
    )
    other_q = swap(theirs_q)
    if cross:
        pair_1 = sides(scal, mine_1, after(passed_1, theirs_q))
        fc1_terms = (mine_1[0], *move_sides(pair_1))
    else:
        pair_1 = ()
        fc1_terms = (scatter_whole(theirs_1, mine_1),)
    output = narrow(
        scal,
        after(active, pair_1, theirs_q),
        mixed,
        bias_2,
        fc2_full,
        unit,
        local_len,
    )
    fc2_own = total(scal, after(fc2_terms, output, other_q))
    fc2_in = inward(fc2_own, n_seq)
    mine_q = outer(
        scal, after(normed, fc2_own), back, 0, group, other_q, "qkv"
    )
    passed_q = flip_mixed(mine_q[3]) if cross else mine_q[3]
    halves = range(2)
    fc1_terms = after(fc1_terms, mine_q)
    fc1_own = [total(scal, fc1_terms, k) for k in halves]
    fc1_in = [inward(v, n_seq) for v in fc1_own]
    input_grad, sums1 = project_back(
        scal,
        returned,
        x,
        after(dmixed, fc1_own),
        gain1,
        qkv_pieces,
        unit,
        local_len,
    )

    if cross:
        pair_q = sides(scal, mine_q, after(passed_q, input_grad))
        qkv_terms = (mine_q[0], *move_sides(pair_q))
    else:
        pair_q = ()
        qkv_terms = (scatter_whole(theirs_q, mine_q),)
    fc2_pair = total(
        scal, (*fc2_terms, after(fc2_in, input_grad, fc1_in[0], pair_q))
    )
    fc2_across = across(fc2_pair)
    fc1_pair = [total(scal, (*fc1_terms, after(fc1_in[0], fc2_pair)), 0)]
    fc1_pair += [total(scal, (*fc1_terms, after(fc1_in[1], fc1_pair)), 1)]
    fc1_across = [across(v) for v in fc1_pair]
    heads_sum = heads_sum.reshape(3, group)
    spread = lambda v: lax.dynamic_update_slice_in_dim(
        jnp.zeros((features,), F32), v, place * group, axis=0
    )
    sums = (
        sums1[0],
        sums1[1],
        spread(heads_sum[0]),
        spread(heads_sum[2]),
        sums2[2],
        sums2[0],
        sums2[1],
        sums2[3],
        fc1_bias_sum[0],
    )
    small = jnp.concatenate([v.reshape(n_fsdp, -1, lane) for v in sums], axis=1)
    if cross:
        for bit in (1, 2, 4):
            small = small + flip(small, bit)
        small = lax.dynamic_index_in_dim(small, shard, 0, False)
    else:
        small = jnp.sum(lax.all_to_all(small, "fsdp", 0, 0, tiled=True), axis=0)
    small = jnp.pad(small, ((0, -small.shape[0] % 16), (0, 0)))
    low = copies(scal, after(qkv_terms, fc1_pair), small, n_seq)
    shared = exchange(low)
    fc2_done = total(scal, (fc2_pair, after(fc2_across, low)))
    fc2_out = outward(fc2_done, n_seq)
    fc1_done = [total(scal, (fc1_pair[0], after(fc1_across[0], fc2_done)))]
    (fc2_weight_grad,) = choose(
        scal, (fc2_done,), (after(fc2_out, fc1_done),), n_seq, (features,)
    )
    fc1_done += [total(scal, (fc1_pair[1], after(fc1_across[1], fc2_weight_grad)))]
    fc1_out = [outward(v, n_seq) for v in fc1_done]
    qkv_weight_grad, small = join(
        scal, after(shared, fc1_done), qkv_weight.shape[0], lane
    )
    fc1_weight_grad, out_weight_grad = choose(
        scal,
        fc1_done,
        after(fc1_out, qkv_weight_grad),
        n_seq,
        (fc1_weight.shape[1], features),
    )
    shares, at = [], 0
    for v in vectors:
        size = v.shape[0] // lane
        shares.append(small[at : at + size].reshape(-1))
        at += size
    g1, s1, qb, vb, ob, g2, s2, b2, b1 = shares
    return (
        output,
        input_grad,
        g1,
        s1,
        qkv_weight_grad,
        qb,
        vb,
        out_weight_grad,
        ob,
        g2,
        s2,
        fc1_weight_grad,
        b1,
        fc2_weight_grad,
        b2,
    )


def solution(mesh):
    rows, vector, matrix = P("fsdp", "seq", None), P("fsdp"), P("fsdp", None)
    return jax.shard_map(
        functools.partial(on_device, mesh.shape["fsdp"], mesh.shape["seq"]),
        mesh=mesh,
        in_specs=(
            rows,
            vector,
            vector,
            vector,
            matrix,
            vector,
            vector,
            matrix,
            vector,
            vector,
            vector,
            matrix,
            vector,
            matrix,
            vector,
            rows,
        ),
        out_specs=(
            rows,
            rows,
            vector,
            vector,
            matrix,
            vector,
            vector,
            matrix,
            vector,
            vector,
            vector,
            matrix,
            vector,
            matrix,
            vector,
        ),
        check_vma=False,
    )
```
